32 devices in a mesh: groups: 2 (over y), row: 4 (over z), col: 4 (over x, core).
Axes of the slice: x: 2, y: 2, z: 4, core: 2. Of those that a mesh axis runs over, the one named last changes fastest.
Arguments:
- alignment: bfloat16 [256, 128, 256], P(('groups', 'row'), 'col'), parts along dimension 0, may hold values from -6 to 6
- sequence_mask: int32 [256], P('groups'), parts along dimension 0, may hold values 0 or 1
- residue_mask: int32 [256], P('groups'), parts along dimension 0, may hold values 0 or 1
- layer_norm_gain: float32 [256], replicated, may hold values from 0.5 to 1.5
- norm_shift: float32 [256], replicated, may hold values from -3 to 3
- proj_weight: bfloat16 [256, 64], replicated, may hold values from -0.375 to 0.375
- proj_bias: float32 [64], replicated, may hold values from -3 to 3
- out_weight: bfloat16 [1024, 128], replicated, may hold values from -2 to 2
- out_bias: float32 [128], replicated, may hold values from -4 to 4
- cotangent: bfloat16 [256, 128, 128], P(('groups', 'row'), 'col'), parts along dimension 0, may hold values from -2 to 2
Outputs:
- pair_output_update: bfloat16 [256, 128, 128], P(('groups', 'row'), 'col'), parts along dimension 0
- alignment_gradient: bfloat16 [256, 128, 256], P(('groups', 'row'), 'col'), parts along dimension 0
- norm_gain_gradient: float32 [512], P('groups'), parts along dimension 0
- norm_shift_gradient: float32 [512], P('groups'), parts along dimension 0
- projection_weight_gradient: float32 [512, 64], P('groups'), parts along dimension 0
- projection_bias_gradient: float32 [128], P('groups'), parts along dimension 0
- output_weight_gradient: float32 [2048, 128], P('groups'), parts along dimension 0
The draws below stay inside these ranges and needn't reach their ends.
There are 2 independent parts, one for each index of `groups`. The reference program is written for one: setup_inputs(seed, part) draws one part's arguments, and reference() takes and returns one part's arrays. A program takes and returns all parts, laid end to end along the dimension named above; an argument that names none is the same for every part. Nothing has to cross between parts.
All inputs are finite; a program needn't handle non-finite values.
Results may differ from the reference program's by a relative error of at most 0.0074.
Values may be sent and summed in bfloat16 or wider, within the bound.
A program may use at most 64 MiB of HBM per device.

```python
import jax
import jax.numpy as jnp
from jax import lax

C = 256
HID = 32
PAIR = 128
SEQS = 128
N = 128


def with_ends(values, rng, smallest, high):
    place = [jax.random.randint(jax.random.fold_in(rng, axis), (), 0, length) for axis, length in enumerate(values.shape)]
    widest = values.shape.index(max(values.shape))
    next_to = place[:widest] + [(place[widest] + 1) % values.shape[widest]] + place[widest + 1:]
    return values.at[tuple(place)].set(smallest).at[tuple(next_to)].set(high)


def block_levels(stream_key, extent, split, smallest, largest):
    def one(dim, shards_of):
        steps = jax.random.uniform(jax.random.fold_in(jax.random.fold_in(stream_key, 6), dim), (shards_of,), jnp.float32, smallest / len(split), largest / len(split))
        return jnp.repeat(jnp.exp(steps), extent[dim] // shards_of).reshape((-1,) + (1,) * (len(extent) - dim - 1))

    loudness = one(*split[0])
    for cut in split[1:]:
        loudness = loudness * one(*cut)
    return loudness


def bell_draw(own_key, dims, spread, most, shards=(), kind=jnp.bfloat16):
    level = block_levels(own_key, dims, shards, -0.22, 0.18) if shards else 1.0
    entries = jax.random.normal(own_key, dims, jnp.float32) * spread * level
    return jnp.minimum(jnp.maximum(entries, -most), most).astype(kind)


def setup_inputs(seed: int = 0, part: int = 0) -> dict:
    arg_keys = jax.random.split(jax.random.key(seed), 11)
    own_keys = jax.random.split(jax.random.fold_in(arg_keys[10], part), 11)
    return {
        "alignment": bell_draw(own_keys[0], (SEQS, N, C), 1.0, 6.0, ((0, 4), (1, 4))),
        "sequence_mask": with_ends((jax.random.randint(own_keys[1], (SEQS,), 0, 4) < 3).astype(jnp.int32), jax.random.fold_in(own_keys[1], 1), 0, 1),
        "residue_mask": with_ends((jax.random.randint(own_keys[2], (N,), 0, 8) < 7).astype(jnp.int32), jax.random.fold_in(own_keys[2], 1), 0, 1),
        "layer_norm_gain": jnp.clip(1.0 + 0.1 * jax.random.normal(arg_keys[3], (C,), jnp.float32), 0.5, 1.5),
        "norm_shift": bell_draw(arg_keys[4], (C,), 0.5, 3.0, (), jnp.float32),
        "proj_weight": bell_draw(arg_keys[5], (C, 2 * HID), C ** -0.5, 0.375),
        "proj_bias": bell_draw(arg_keys[6], (2 * HID,), 0.5, 3.0, (), jnp.float32),
        "out_weight": bell_draw(arg_keys[7], (HID * HID, PAIR), (max(1, HID * HID // SEQS)) ** -0.5, 2.0),
        "out_bias": bell_draw(arg_keys[8], (PAIR,), 1.0, 4.0, (), jnp.float32),
        "cotangent": bell_draw(own_keys[9], (N, N, PAIR), 0.3, 2.0, ((0, 4), (1, 4))),
    }


EPSILON = 1e-05

def normalize(values, layer_norm_gain, norm_shift):
    widened = values.astype(jnp.float32)
    centred = widened - lax.optimization_barrier(jnp.mean(widened, axis=-1, keepdims=True))
    inverse_deviation = lax.rsqrt(lax.optimization_barrier(jnp.mean(centred * centred, axis=-1, keepdims=True)) + EPSILON)
    scaled_product = centred * inverse_deviation
    return (scaled_product, inverse_deviation, (scaled_product * layer_norm_gain + norm_shift).astype(jnp.bfloat16))

def layer_norm_backward_pass(normalized_input_gradient, scaled_product, inverse_deviation, layer_norm_gain):
    grad_scaled = normalized_input_gradient * layer_norm_gain
    first = lax.optimization_barrier(jnp.mean(grad_scaled, axis=-1, keepdims=True))
    second = lax.optimization_barrier(jnp.mean(grad_scaled * scaled_product, axis=-1, keepdims=True))
    return inverse_deviation * (grad_scaled - first - scaled_product * second)

def outer_block(left_block, right_flat, hidden, width_j):
    product = lax.dot_general(left_block, right_flat, (((0,), (0,)), ((), ())), preferred_element_type=jnp.float32)
    count_i = left_block.shape[1] // hidden
    product = product.reshape(count_i, hidden, width_j, hidden).transpose(0, 2, 1, 3)
    return product.reshape(count_i * width_j, hidden * hidden).astype(jnp.bfloat16)

def outer_adjoint(grad_outer, count_i, width_j, hidden):
    arranged = grad_outer.reshape(count_i, width_j, hidden, hidden).transpose(0, 2, 1, 3)
    return arranged.reshape(count_i * hidden, width_j * hidden)

def reference(alignment, sequence_mask, residue_mask, layer_norm_gain, norm_shift, proj_weight, proj_bias, out_weight, out_bias, cotangent):
    scaled_product, inverse_deviation, normed = normalize(alignment, layer_norm_gain, norm_shift)
    live = (sequence_mask[:, None] * residue_mask[None, :]).astype(jnp.float32)
    projected = jnp.dot(normed.reshape(SEQS * N, C), proj_weight, preferred_element_type=jnp.float32)
    projected = projected.reshape(SEQS, N, 2 * HID) + proj_bias
    masked = (projected * live[:, :, None]).astype(jnp.bfloat16)
    left_flat = masked[:, :, :HID].reshape(SEQS, N * HID)
    right_flat = masked[:, :, HID:].reshape(SEQS, N * HID)
    kept_count = jnp.sum(sequence_mask).astype(jnp.float32)
    residue_live = residue_mask.astype(jnp.float32)
    block_rows = min(N, 64)

    def advance(running, block_index):
        grad_out_w, grad_right = running
        offset = block_index * block_rows
        left_block = lax.dynamic_slice_in_dim(left_flat, offset * HID, block_rows * HID, 1)
        products = outer_block(left_block, right_flat, HID, N)
        preact = jnp.dot(products, out_weight, preferred_element_type=jnp.float32) + out_bias
        live_rows = lax.dynamic_slice_in_dim(residue_live, offset, block_rows)
        divisor = jnp.maximum(kept_count * live_rows[:, None] * residue_live[None, :], 1.0).reshape(-1, 1)
        pair_block = (preact / divisor).astype(jnp.bfloat16)
        cot_block = lax.dynamic_slice_in_dim(cotangent, offset, block_rows, 0).reshape(-1, PAIR).astype(jnp.float32)
        grad_pre = (cot_block / divisor).astype(jnp.bfloat16)
        grad_out_w = grad_out_w + lax.dot_general(products, grad_pre, (((0,), (0,)), ((), ())), preferred_element_type=jnp.float32)
        grad_outer = jnp.dot(grad_pre, out_weight.T, preferred_element_type=jnp.float32).astype(jnp.bfloat16)
        grad_pairs = outer_adjoint(grad_outer, block_rows, N, HID)
        grad_left = lax.dot_general(right_flat, grad_pairs, (((1,), (1,)), ((), ())), preferred_element_type=jnp.float32)
        grad_right = grad_right + jnp.dot(left_block, grad_pairs, preferred_element_type=jnp.float32)
        return ((grad_out_w, grad_right), (pair_block, grad_left))
    initial = (jnp.zeros((HID * HID, PAIR), jnp.float32), jnp.zeros((SEQS, N * HID), jnp.float32))
    (output_weight_gradient, grad_right), (pair_blocks, grad_lefts) = lax.scan(advance, initial, jnp.arange(N // block_rows, dtype=jnp.int32))
    pair_output_update = pair_blocks.reshape(N, N, PAIR)
    grad_left = grad_lefts.transpose(1, 0, 2).reshape(SEQS, N, HID)
    grad_projected = jnp.concatenate([grad_left, grad_right.reshape(SEQS, N, HID)], axis=-1) * live[:, :, None]
    grad_low = grad_projected.astype(jnp.bfloat16)
    normalized_input_gradient = jnp.dot(grad_low.reshape(-1, 2 * HID), proj_weight.T, preferred_element_type=jnp.float32).reshape(SEQS, N, C)
    projection_weight_gradient = lax.dot_general(normed.reshape(-1, C), grad_low.reshape(-1, 2 * HID), (((0,), (0,)), ((), ())), preferred_element_type=jnp.float32)
    projection_bias_gradient = lax.optimization_barrier(jnp.sum(grad_projected, axis=(0, 1)))
    norm_gain_gradient = lax.optimization_barrier(jnp.sum(normalized_input_gradient * scaled_product, axis=(0, 1)))
    norm_shift_gradient = lax.optimization_barrier(jnp.sum(normalized_input_gradient, axis=(0, 1)))
    alignment_gradient = layer_norm_backward_pass(normalized_input_gradient, scaled_product, inverse_deviation, layer_norm_gain).astype(jnp.bfloat16)
    return (pair_output_update, alignment_gradient, norm_gain_gradient, norm_shift_gradient, projection_weight_gradient, projection_bias_gradient, output_weight_gradient)
```

```python
import functools

import jax
import jax.numpy as jnp
from jax import lax
from jax.experimental import pallas as pl
from jax.experimental.pallas import tpu as pltpu
from jax.sharding import PartitionSpec as P

EPSILON = 1e-05
LANES = 128
WIDE = 256
MESH = pl.DeviceIdType.MESH
F32 = jnp.float32
BF16 = jnp.bfloat16


def lane_group_swap(blocks, width):
    lane = lax.broadcasted_iota(jnp.int32, blocks[0].shape, 1)
    span = len(blocks) // 2
    while span:
        low = (lane // (width * span)) % 2 == 0
        out = list(blocks)
        for a in range(len(blocks)):
            if a & span:
                continue
            first, second = blocks[a], blocks[a + span]
            shift = width * span
            out[a] = jnp.where(low, first, pltpu.roll(second, shift, 1))
            out[a + span] = jnp.where(low, pltpu.roll(first, LANES - shift, 1), second)
        blocks = out
        span //= 2
    return blocks


def place_groups(pieces, shifts, width):
    group = lax.broadcasted_iota(jnp.int32, pieces[0].shape, 1) // width
    out = None
    for k, (piece, shift) in enumerate(zip(pieces, shifts)):
        rolled = pltpu.roll(piece, shift % LANES, 1) if shift % LANES else piece
        out = rolled if out is None else jnp.where(group == k, rolled, out)
    return out


def nt(a, b):
    return lax.dot_general(a, b, (((1,), (1,)), ((), ())), preferred_element_type=F32)


def tn(a, b):
    return lax.dot_general(a, b, (((0,), (0,)), ((), ())), preferred_element_type=F32)


def nn(a, b):
    return jnp.dot(a, b, preferred_element_type=F32)


def aligned(start, size, step=None):
    return pl.ds(pl.multiple_of(start, step or size), size)


def fused_kernel(dims, *refs):
    rows, cols, seq_local, res_local, hidden, channels, width = dims
    (x_hbm, seq_ref, res_ref, gain_ref, shift_ref, w_ref, pb_ref, ow_hbm, ob_ref, cot_hbm) = refs[:10]
    (pair_hbm, ag_hbm, gw_ref, gpw_ref, vec_ref) = refs[10:15]
    (
        x_ref,
        ow_ref,
        cot_ref,
        pair_ref,
        ag_ref,
        scaled_ref,
        inv_ref,
        normed_ref,
        prj_ref,
        tr_ref,
        u_ref,
        seqcol_ref,
        lsend_ref,
        lbuf_ref,
        rbuf_ref,
        owf_ref,
        wp_ref,
        gpre_ref,
        gp_ref,
        prod_ref,
        gls_ref,
        glr_ref,
        glmid_ref,
        glfin_ref,
        grs_ref,
        grr_ref,
        gws_ref,
        gwr_ref,
        gwc_ref,
        gwcr_ref,
        gwg_ref,
        low_ref,
        sw_ref,
        swr_ref,
        swc_ref,
        swcr_ref,
        sv_ref,
        svr_ref,
        svc_ref,
        svcr_ref,
        local_sems,
        one_sems,
        col_send,
        col_recv,
        row_send,
        row_recv,
    ) = refs[15:]
    r = lax.axis_index("row")
    c = lax.axis_index("col")
    factor = cols // rows
    seqs = seq_local * rows
    tile_rows = res_local * factor
    n = seq_local * res_local
    pairs = tile_rows * res_local
    block = res_local * hidden
    fold = LANES // res_local
    chunks = n // LANES
    majors = block // LANES
    total = rows * cols
    barrier = pltpu.get_barrier_semaphore()

    def greet(t, carry):
        other = lax.rem(r * cols + c + t, total)
        pl.semaphore_signal(
            barrier,
            inc=1,
            device_id={"row": other // cols, "col": lax.rem(other, cols)},
            device_id_type=MESH,
        )
        return carry

    lax.fori_loop(1, total, greet, 0)
    load_x = pltpu.make_async_copy(x_hbm, x_ref, local_sems.at[0])
    load_w = pltpu.make_async_copy(ow_hbm, ow_ref, local_sems.at[1])
    load_c = pltpu.make_async_copy(cot_hbm, cot_ref, local_sems.at[2])
    load_x.start()
    load_w.start()
    load_c.start()

    def remote(src, dst, send_sem, recv_sem, trow, tcol):
        return pltpu.make_async_remote_copy(
            src_ref=src,
            dst_ref=dst,
            send_sem=send_sem,
            recv_sem=recv_sem,
            device_id={"row": trow, "col": tcol},
            device_id_type=MESH,
        )

    def over(kind, plane):
        if kind == "col":
            return cols, c, col_send.at[plane], col_recv.at[plane], lambda k: (r, k)
        return rows, r, row_send.at[plane], row_recv.at[plane], lambda k: (k, c)

    def start(kind, plane, src, dst):
        count, me, send, recv, where = over(kind, plane)

        def body(t, carry):
            k = lax.rem(me + t, count)
            remote(src(k), dst(me), send.at[k], recv.at[me], *where(k)).start()
            return carry

        lax.fori_loop(1, count, body, 0)

    def receive(kind, plane, src, dst):
        count, me, send, recv, where = over(kind, plane)

        def body(t, carry):
            k = lax.rem(me + t, count)
            remote(dst(k), dst(k), send.at[k], recv.at[k], *where(k)).wait_recv()
            return carry

        lax.fori_loop(1, count, body, 0)

    def drain(kind, plane, src, dst):
        count, me, send, recv, where = over(kind, plane)

        def body(t, carry):
            k = lax.rem(me + t, count)
            remote(src(k), dst(me), send.at[k], recv.at[me], *where(k)).wait_send()
            return carry

        lax.fori_loop(1, count, body, 0)

    def column(mask_ref, count, offset):
        size = mask_ref.shape[1]
        shape = (count, size)
        hit = lax.broadcasted_iota(jnp.int32, shape, 1) == lax.broadcasted_iota(jnp.int32, shape, 0) + offset
        values = jnp.broadcast_to(mask_ref[...].astype(F32), shape)
        return jnp.sum(jnp.where(hit, values, 0.0), axis=1, keepdims=True)

    seqcol_ref[...] = jnp.broadcast_to(column(seq_ref, seq_local, r * seq_local), seqcol_ref.shape)
    rescol = column(res_ref, res_local, c * res_local)
    tilecol = column(res_ref, tile_rows, r * tile_rows)
    kept = jnp.sum(seq_ref[...].astype(F32), axis=1, keepdims=True)

    def live_column(k):
        parts = []
        for q in range(fold):
            parts.append(rescol * seqcol_ref[pl.ds(k * fold + q, 1), 0:1])
        return jnp.concatenate(parts, axis=0)

    w = w_ref[...].astype(F32)
    w = jnp.concatenate([w, jnp.zeros((channels, LANES - 2 * hidden), F32)], axis=1)
    w_wide = w.astype(BF16)
    w_turned = w.T.astype(BF16)
    bias = pb_ref[...]
    bias = jnp.concatenate([bias, jnp.zeros((1, LANES - 2 * hidden), F32)], axis=1)
    gain = gain_ref[...]
    shift = shift_ref[...]

    load_x.wait()

    def layer_norm(k, carry):
        here = aligned(k * LANES, LANES)
        widened = x_ref[here, :].astype(F32)
        centred = widened - jnp.mean(widened, axis=-1, keepdims=True)
        inverse = lax.rsqrt(jnp.mean(centred * centred, axis=-1, keepdims=True) + EPSILON)
        scaled = centred * inverse
        normed = (scaled * gain + shift).astype(BF16)
        scaled_ref[here, :] = scaled
        inv_ref[here, :] = inverse
        normed_ref[here, :] = normed
        prj = (nn(normed, w_wide) + bias) * live_column(k)
        prj_ref[here, :] = prj
        tr_ref[here, :] = prj.T
        return carry

    lax.fori_loop(0, chunks, layer_norm, 0)

    for im in range(majors):
        pieces = [prj_ref[pl.ds(im * fold + k, seq_local, stride=res_local), :] for k in range(fold)]
        left = place_groups(pieces, [k * hidden for k in range(fold)], hidden)
        lsend_ref[:, im * LANES : (im + 1) * LANES] = left.astype(BF16)
    for sb in range(chunks):
        pieces = [
            tr_ref[pl.ds(sb * LANES + hidden + k, majors, stride=fold), :] for k in range(fold)
        ]
        for q in range(fold):
            turned = place_groups(pieces, [(k - q) * res_local for k in range(fold)], res_local)
            u_ref[pl.ds(sb * fold + q, majors, stride=seq_local), :] = turned
    my_seqs = aligned(r * seq_local, seq_local)
    for dm in range(majors):
        rbuf_ref[my_seqs, dm * LANES : (dm + 1) * LANES] = u_ref[
            dm * seq_local : (dm + 1) * seq_local, :
        ].astype(BF16)

    pl.semaphore_wait(barrier, total - 1)

    def left_slot(k):
        return lbuf_ref.at[aligned((k // factor) * seq_local, seq_local), aligned(lax.rem(k, factor) * block, block)]

    relay_row = c // factor
    relay_col = r * factor + lax.rem(c, factor)
    at_home = jnp.logical_and(relay_row == r, relay_col == c)
    left_out = remote(
        lsend_ref, left_slot(relay_col), one_sems.at[0], one_sems.at[1], relay_row, relay_col
    )
    left_home = pltpu.make_async_copy(lsend_ref, left_slot(c), local_sems.at[3])

    @pl.when(at_home)
    def _():
        left_home.start()

    @pl.when(jnp.logical_not(at_home))
    def _():
        left_out.start()

    def right_block(k):
        return rbuf_ref.at[aligned(k * seq_local, seq_local), :]

    right_args = ("row", 0, lambda k: right_block(r), right_block)
    start(*right_args)

    load_w.wait()
    load_c.wait()
    owf_ref[...] = ow_ref[...].astype(F32)
    for d in range(hidden):
        wp_ref[d * hidden : (d + 1) * hidden, :] = owf_ref[pl.ds(d, hidden, stride=hidden), :].astype(BF16)

    def inverse_divisor(i):
        return 1.0 / jnp.maximum(kept * tilecol[i : i + 1, :] * rescol, 1.0)

    for i in range(tile_rows):
        here = slice(i * res_local, (i + 1) * res_local)
        gpre_ref[here, :] = (cot_ref[here, :].astype(F32) * inverse_divisor(i)).astype(BF16)

    half = WIDE // LANES

    def grad_products(ip, carry):
        upstream = gpre_ref[aligned(ip * WIDE, WIDE), :]
        for dm in range(majors):
            tile = nt(wp_ref[dm * LANES : (dm + 1) * LANES, :], upstream)
            for h in range(half):
                blocks = [
                    tile[a * hidden : (a + 1) * hidden, h * LANES : (h + 1) * LANES] for a in range(fold)
                ]
                for a, swapped in enumerate(lane_group_swap(blocks, res_local)):
                    gp_ref[
                        aligned(((ip * half + h) * fold + a) * hidden, hidden), dm * LANES : (dm + 1) * LANES
                    ] = swapped.astype(BF16)
        return carry

    steps = pairs // WIDE
    lax.fori_loop(0, steps // 2, grad_products, 0)

    @pl.when(at_home)
    def _():
        left_home.wait()

    @pl.when(jnp.logical_not(at_home))
    def _():
        remote(
            left_slot(c), left_slot(c), one_sems.at[0], one_sems.at[1], relay_row, relay_col
        ).wait_recv()

    left_args = ("col", 0, lambda k: left_slot(c), left_slot)
    start(*left_args)
    lax.fori_loop(steps // 2, steps, grad_products, 0)
    receive(*right_args)
    receive(*left_args)

    def gl_part(k):
        return gls_ref.at[aligned((k // factor) * seq_local, seq_local), aligned(lax.rem(k, factor) * block, block)]

    for k in range(tile_rows * hidden // WIDE):
        gls_ref[:, k * WIDE : (k + 1) * WIDE] = nt(rbuf_ref[...], gp_ref[k * WIDE : (k + 1) * WIDE, :]).astype(BF16)
    gl_args = ("col", 1, gl_part, lambda k: glr_ref.at[k])
    start(*gl_args)
    for k in range(block // WIDE):
        grs_ref[:, k * WIDE : (k + 1) * WIDE] = nn(lbuf_ref[...], gp_ref[:, k * WIDE : (k + 1) * WIDE]).astype(BF16)
    gr_args = (
        "row",
        1,
        lambda k: grs_ref.at[aligned(k * seq_local, seq_local), :],
        lambda k: grr_ref.at[k],
    )
    start(*gr_args)

    def products(im, carry):
        left = lbuf_ref[:, aligned(im * LANES, LANES)]
        for k in range(block // WIDE):
            tile = tn(left, rbuf_ref[:, k * WIDE : (k + 1) * WIDE])
            for h in range(half):
                blocks = [
                    tile[a * hidden : (a + 1) * hidden, h * LANES : (h + 1) * LANES] for a in range(fold)
                ]
                for a, swapped in enumerate(lane_group_swap(blocks, res_local)):
                    at = ((k * half + h) * fold + a) * hidden
                    prod_ref[at : at + hidden, aligned(im * LANES, LANES)] = swapped.astype(BF16)
        return carry

    steps = tile_rows // fold
    lax.fori_loop(0, steps // 2, products, 0)

    receive(*gl_args)
    mine = gls_ref[aligned((c // factor) * seq_local, seq_local), aligned(lax.rem(c, factor) * block, block)]

    def add_left(t, carry):
        return carry + glr_ref[lax.rem(c + t, cols)].astype(F32)

    glmid_ref[...] = lax.fori_loop(1, cols, add_left, mine.astype(F32)).astype(BF16)
    gl_out = remote(glmid_ref, glfin_ref, one_sems.at[2], one_sems.at[3], relay_row, relay_col)
    gl_home = pltpu.make_async_copy(glmid_ref, glfin_ref, local_sems.at[4])

    @pl.when(at_home)
    def _():
        gl_home.start()

    @pl.when(jnp.logical_not(at_home))
    def _():
        gl_out.start()

    lax.fori_loop(steps // 2, steps, products, 0)

    for k in range(hidden * hidden // WIDE):
        owf_ref[k * WIDE : (k + 1) * WIDE, :] = nn(prod_ref[k * WIDE : (k + 1) * WIDE, :], gpre_ref[...])
    for k in range(hidden):
        gws_ref[k * hidden : (k + 1) * hidden, :] = owf_ref[pl.ds(k, hidden, stride=hidden), :].astype(BF16)
    w_block = hidden * hidden // cols
    gw_row_args = (
        "col",
        2,
        lambda k: gws_ref.at[aligned(k * w_block, w_block), :],
        lambda k: gwr_ref.at[k],
    )
    start(*gw_row_args)

    out_bias = ob_ref[...]
    for k in range(pairs // WIDE):
        pre = tn(wp_ref[...], prod_ref[:, k * WIDE : (k + 1) * WIDE]).T + out_bias
        for q in range(WIDE // res_local):
            i = k * (WIDE // res_local) + q
            pair_ref[i * res_local : (i + 1) * res_local, :] = (
                pre[q * res_local : (q + 1) * res_local, :] * inverse_divisor(i)
            ).astype(BF16)
    store_pair = pltpu.make_async_copy(pair_ref, pair_hbm, local_sems.at[5])
    store_pair.start()

    w_small = w_block // rows
    receive(*gw_row_args)
    summed = gws_ref[aligned(c * w_block, w_block), :].astype(F32)

    def add_w(t, carry):
        return carry + gwr_ref[lax.rem(c + t, cols)].astype(F32)

    summed = lax.fori_loop(1, cols, add_w, summed).astype(BF16)
    for k in range(rows):
        gwc_ref[k] = summed[k * w_small : (k + 1) * w_small, :]
    gw_col_args = ("row", 2, lambda k: gwc_ref.at[k], lambda k: gwcr_ref.at[k])
    start(*gw_col_args)

    receive(*gr_args)
    for dm in range(majors):
        part = slice(dm * LANES, (dm + 1) * LANES)
        total_right = grs_ref[my_seqs, part].astype(F32)

        def add_right(t, carry, part=part):
            return carry + grr_ref[lax.rem(r + t, rows), :, part].astype(F32)

        u_ref[dm * seq_local : (dm + 1) * seq_local, :] = lax.fori_loop(1, rows, add_right, total_right)
    for sb in range(chunks):
        pieces = [u_ref[pl.ds(sb * fold + q, majors, stride=seq_local), :] for q in range(fold)]
        for k in range(fold):
            turned = place_groups(pieces, [(q - k) * res_local for q in range(fold)], res_local)
            tr_ref[pl.ds(sb * LANES + hidden + k, majors, stride=fold), :] = turned

    @pl.when(at_home)
    def _():
        gl_home.wait()

    @pl.when(jnp.logical_not(at_home))
    def _():
        remote(glmid_ref, glfin_ref, one_sems.at[2], one_sems.at[3], relay_row, relay_col).wait_recv()

    for im in range(majors):
        piece = glfin_ref[:, im * LANES : (im + 1) * LANES].astype(F32)
        for k in range(fold):
            rolled = pltpu.roll(piece, LANES - k * hidden, 1) if k else piece
            prj_ref[pl.ds(im * fold + k, seq_local, stride=res_local), :] = rolled

    lane = lax.broadcasted_iota(jnp.int32, (LANES, LANES), 1)

    def backward(k, carry):
        bias_sum, gain_sum, shift_sum = carry
        here = aligned(k * LANES, LANES)
        projected = jnp.where(lane < hidden, prj_ref[here, :], tr_ref[here, :].T)
        projected = jnp.where(lane < 2 * hidden, projected * live_column(k), 0.0)
        low = projected.astype(BF16)
        low_ref[here, :] = low
        upstream = nn(low, w_turned)
        scaled = scaled_ref[here, :]
        bias_sum = bias_sum + jnp.sum(projected, axis=0, keepdims=True)
        gain_sum = gain_sum + jnp.sum(upstream * scaled, axis=0, keepdims=True)
        shift_sum = shift_sum + jnp.sum(upstream, axis=0, keepdims=True)
        grad_scaled = upstream * gain
        first = jnp.mean(grad_scaled, axis=-1, keepdims=True)
        second = jnp.mean(grad_scaled * scaled, axis=-1, keepdims=True)
        ag_ref[here, :] = (inv_ref[here, :] * (grad_scaled - first - scaled * second)).astype(BF16)
        return bias_sum, gain_sum, shift_sum

    bias_sum, gain_sum, shift_sum = lax.fori_loop(
        0,
        chunks,
        backward,
        (jnp.zeros((1, LANES), F32), jnp.zeros((1, channels), F32), jnp.zeros((1, channels), F32)),
    )
    store_ag = pltpu.make_async_copy(ag_ref, ag_hbm, local_sems.at[6])
    store_ag.start()
    sw_ref[...] = tn(low_ref[...], normed_ref[...])[: 2 * hidden, :].astype(BF16)
    sv_ref[0:1, :] = gain_sum
    sv_ref[1:2, :] = shift_sum
    sv_ref[2:3, :] = jnp.concatenate([bias_sum, jnp.zeros((1, channels - LANES), F32)], axis=1)
    sv_ref[3:8, :] = jnp.zeros((5, channels), F32)
    sw_row_args = ("col", 3, lambda k: sw_ref, lambda k: swr_ref.at[k])
    sv_row_args = ("col", 4, lambda k: sv_ref, lambda k: svr_ref.at[k])
    start(*sw_row_args)
    start(*sv_row_args)

    receive(*gw_col_args)

    def add_w_col(t, carry):
        return carry + gwcr_ref[lax.rem(r + t, rows)].astype(F32)

    gwg_ref[r] = lax.fori_loop(1, rows, add_w_col, gwc_ref[r].astype(F32)).astype(BF16)
    gw_up_args = ("row", 3, lambda k: gwg_ref.at[r], lambda k: gwg_ref.at[k])
    start(*gw_up_args)

    receive(*sw_row_args)
    receive(*sv_row_args)

    def add_sw(t, carry):
        return carry + swr_ref[lax.rem(c + t, cols)].astype(F32)

    def add_sv(t, carry):
        return carry + svr_ref[lax.rem(c + t, cols)]

    swc_ref[...] = lax.fori_loop(1, cols, add_sw, sw_ref[...].astype(F32)).astype(BF16)
    svc_ref[...] = lax.fori_loop(1, cols, add_sv, sv_ref[...])
    sw_col_args = ("row", 4, lambda k: swc_ref, lambda k: swcr_ref.at[k])
    sv_col_args = ("row", 5, lambda k: svc_ref, lambda k: svcr_ref.at[k])
    start(*sw_col_args)
    start(*sv_col_args)

    receive(*gw_up_args)
    gw_ref[c] = gwg_ref[...]
    gw_out_args = ("col", 5, lambda k: gwg_ref, lambda k: gw_ref.at[k])
    start(*gw_out_args)

    receive(*sw_col_args)
    receive(*sv_col_args)

    def add_swc(t, carry):
        return carry + swcr_ref[t].astype(F32)

    def add_svc(t, carry):
        return carry + svcr_ref[t]

    swcr_ref[r] = swc_ref[...]
    svcr_ref[r] = svc_ref[...]
    gpw_ref[...] = lax.fori_loop(0, rows, add_swc, jnp.zeros(gpw_ref.shape, F32))
    vec_ref[...] = lax.fori_loop(0, rows, add_svc, jnp.zeros(vec_ref.shape, F32))
    receive(*gw_out_args)

    @pl.when(jnp.logical_not(at_home))
    def _():
        left_out.wait_send()
        gl_out.wait_send()

    for args in (
        right_args,
        left_args,
        gl_args,
        gr_args,
        gw_row_args,
        gw_col_args,
        sw_row_args,
        sv_row_args,
        gw_up_args,
        sw_col_args,
        sv_col_args,
        gw_out_args,
    ):
        drain(*args)
    store_pair.wait()
    store_ag.wait()


def shards(
    alignment,
    sequence_mask,
    residue_mask,
    layer_norm_gain,
    norm_shift,
    proj_weight,
    proj_bias,
    out_weight,
    out_bias,
    cotangent,
):
    rows = lax.axis_size("row")
    cols = lax.axis_size("col")
    factor = cols // rows
    seq_local, res_local, channels = alignment.shape
    seqs = seq_local * rows
    hidden = proj_weight.shape[1] // 2
    width = out_weight.shape[1]
    tile_rows = res_local * factor
    n = seq_local * res_local
    pairs = tile_rows * res_local
    block = res_local * hidden
    majors = block // LANES
    inner = tile_rows * hidden
    w_block = hidden * hidden // cols
    w_small = w_block // rows
    dims = (rows, cols, seq_local, res_local, hidden, channels, width)
    vmem = pl.BlockSpec(memory_space=pltpu.VMEM)
    anywhere = pl.BlockSpec(memory_space=pl.ANY)
    pair, grad_alignment, grad_w, grad_pw, vectors = pl.pallas_call(
        functools.partial(fused_kernel, dims),
        out_shape=[
            jax.ShapeDtypeStruct((pairs, width), BF16),
            jax.ShapeDtypeStruct((n, channels), BF16),
            jax.ShapeDtypeStruct((cols, rows, w_small, width), BF16),
            jax.ShapeDtypeStruct((2 * hidden, channels), F32),
            jax.ShapeDtypeStruct((8, channels), F32),
        ],
        in_specs=[anywhere, vmem, vmem, vmem, vmem, vmem, vmem, anywhere, vmem, anywhere],
        out_specs=[anywhere, anywhere, vmem, vmem, vmem],
        scratch_shapes=[
            pltpu.VMEM((n, channels), BF16),
            pltpu.VMEM((hidden * hidden, width), BF16),
            pltpu.VMEM((pairs, width), BF16),
            pltpu.VMEM((pairs, width), BF16),
            pltpu.VMEM((n, channels), BF16),
            pltpu.VMEM((n, channels), F32),
            pltpu.VMEM((n, 1), F32),
            pltpu.VMEM((n, channels), BF16),
            pltpu.VMEM((n, LANES), F32),
            pltpu.VMEM((n, LANES), F32),
            pltpu.VMEM((majors * seq_local, LANES), F32),
            pltpu.VMEM((seq_local, LANES), F32),
            pltpu.VMEM((seq_local, block), BF16),
            pltpu.VMEM((seqs, inner), BF16),
            pltpu.VMEM((seqs, block), BF16),
            pltpu.VMEM((hidden * hidden, width), F32),
            pltpu.VMEM((hidden * hidden, width), BF16),
            pltpu.VMEM((pairs, width), BF16),
            pltpu.VMEM((inner, block), BF16),
            pltpu.VMEM((hidden * hidden, pairs), BF16),
            pltpu.VMEM((seqs, inner), BF16),
            pltpu.VMEM((cols, seq_local, block), BF16),
            pltpu.VMEM((seq_local, block), BF16),
            pltpu.VMEM((seq_local, block), BF16),
            pltpu.VMEM((seqs, block), BF16),
            pltpu.VMEM((rows, seq_local, block), BF16),
            pltpu.VMEM((hidden * hidden, width), BF16),
            pltpu.VMEM((cols, w_block, width), BF16),
            pltpu.VMEM((rows, w_small, width), BF16),
            pltpu.VMEM((rows, w_small, width), BF16),
            pltpu.VMEM((rows, w_small, width), BF16),
            pltpu.VMEM((n, LANES), BF16),
            pltpu.VMEM((2 * hidden, channels), BF16),
            pltpu.VMEM((cols, 2 * hidden, channels), BF16),
            pltpu.VMEM((2 * hidden, channels), BF16),
            pltpu.VMEM((rows, 2 * hidden, channels), BF16),
            pltpu.VMEM((8, channels), F32),
            pltpu.VMEM((cols, 8, channels), F32),
            pltpu.VMEM((8, channels), F32),
            pltpu.VMEM((rows, 8, channels), F32),
            pltpu.SemaphoreType.DMA((7,)),
            pltpu.SemaphoreType.DMA((4,)),
            pltpu.SemaphoreType.DMA((6, cols)),
            pltpu.SemaphoreType.DMA((6, cols)),
            pltpu.SemaphoreType.DMA((6, rows)),
            pltpu.SemaphoreType.DMA((6, rows)),
        ],
        compiler_params=pltpu.CompilerParams(
            collective_id=0, has_side_effects=True, vmem_limit_bytes=48 * 1024 * 1024
        ),
    )(
        alignment.reshape(n, channels),
        sequence_mask.reshape(1, -1),
        residue_mask.reshape(1, -1),
        layer_norm_gain.reshape(1, -1),
        norm_shift.reshape(1, -1),
        proj_weight,
        proj_bias.reshape(1, -1),
        out_weight,
        out_bias.reshape(1, -1),
        cotangent.reshape(pairs, width),
    )
    return (
        pair.reshape(tile_rows, res_local, width),
        grad_alignment.reshape(seq_local, res_local, channels),
        vectors[0],
        vectors[1],
        grad_pw.T,
        vectors[2, : 2 * hidden],
        grad_w.reshape(hidden * hidden, width).astype(F32),
    )


def solution(mesh):
    return jax.shard_map(
        shards,
        mesh=mesh,
        in_specs=(
            P(("groups", "row"), "col", None),
            P("groups"),
            P("groups"),
            P(),
            P(),
            P(),
            P(),
            P(),
            P(),
            P(("groups", "row"), "col", None),
        ),
        out_specs=(
            P(("groups", "row"), "col", None),
            P(("groups", "row"), "col", None),
            P("groups"),
            P("groups"),
            P("groups", None),
            P("groups"),
            P("groups", None),
        ),
        check_vma=False,
    )
```

```python
import functools

import jax
import jax.numpy as jnp
from jax import lax
from jax.experimental import pallas as pl
from jax.experimental.pallas import tpu as pltpu
from jax.sharding import PartitionSpec as P

EPSILON = 1e-05
LANES = 128
WIDE = 256
UNROLL = 4
MESH = pl.DeviceIdType.MESH
F32 = jnp.float32
BF16 = jnp.bfloat16


def lane_group_swap(blocks, width):
    lane = lax.broadcasted_iota(jnp.int32, blocks[0].shape, 1)
    span = len(blocks) // 2
    while span:
        low = (lane // (width * span)) % 2 == 0
        out = list(blocks)
        for a in range(len(blocks)):
            if a & span:
                continue
            first, second = blocks[a], blocks[a + span]
            shift = width * span
            out[a] = jnp.where(low, first, pltpu.roll(second, shift, 1))
            out[a + span] = jnp.where(low, pltpu.roll(first, LANES - shift, 1), second)
        blocks = out
        span //= 2
    return blocks


def place_groups(pieces, shifts, width):
    group = lax.broadcasted_iota(jnp.int32, pieces[0].shape, 1) // width
    out = None
    for k, (piece, shift) in enumerate(zip(pieces, shifts)):
        rolled = pltpu.roll(piece, shift % LANES, 1) if shift % LANES else piece
        out = rolled if out is None else jnp.where(group == k, rolled, out)
    return out


def nt(a, b):
    return lax.dot_general(a, b, (((1,), (1,)), ((), ())), preferred_element_type=F32)


def tn(a, b):
    return lax.dot_general(a, b, (((0,), (0,)), ((), ())), preferred_element_type=F32)


def nn(a, b):
    return jnp.dot(a, b, preferred_element_type=F32)


def aligned(start, size, step=None):
    return pl.ds(pl.multiple_of(start, step or size), size)


def fused_kernel(dims, *refs):
    rows, cols, seq_local, res_local, hidden, channels, width = dims
    inputs = refs[:10]
    (pair_ref, ag_ref, gw_ref, gpw_ref, vec_ref) = refs[10:15]
    (
        x_ref,
        seq_ref,
        res_ref,
        gain_ref,
        shift_ref,
        w_ref,
        pb_ref,
        ow_ref,
        ob_ref,
        cot_ref,
        scaled_ref,
        inv_ref,
        normed_ref,
        prj_ref,
        tr_ref,
        u_ref,
        seqcol_ref,
        lsend_ref,
        lbuf_ref,
        rbuf_ref,
        owf_ref,
        wp_ref,
        gpre_ref,
        gp_ref,
        prod_ref,
        gls_ref,
        glr_ref,
        glmid_ref,
        glfin_ref,
        grs_ref,
        grr_ref,
        gws_ref,
        gwr_ref,
        gwc_ref,
        gwcr_ref,
        gwg_ref,
        low_ref,
        sw_ref,
        swr_ref,
        swf_ref,
        sv_ref,
        svr_ref,
        svc_ref,
        svcr_ref,
        local_sems,
        one_sems,
        send_sems,
        recv_sems,
    ) = refs[15:]
    r = lax.axis_index("row")
    c = lax.axis_index("col")
    factor = cols // rows
    seqs = seq_local * rows
    tile_rows = res_local * factor
    n = seq_local * res_local
    pairs = tile_rows * res_local
    block = res_local * hidden
    fold = LANES // res_local
    chunks = n // LANES
    majors = block // LANES
    total = rows * cols
    barrier = pltpu.get_barrier_semaphore()

    def greet(t, carry):
        other = lax.rem(r * cols + c + t, total)
        pl.semaphore_signal(
            barrier,
            inc=1,
            device_id={"row": other // cols, "col": lax.rem(other, cols)},
            device_id_type=MESH,
        )
        return carry

    staged = (x_ref, seq_ref, res_ref, gain_ref, shift_ref, w_ref, pb_ref, ow_ref, ob_ref, cot_ref)
    loads = [
        pltpu.make_async_copy(source, target, local_sems.at[2 + k])
        for k, (source, target) in enumerate(zip(inputs, staged))
    ]
    late = (7, 8, 9)
    for k, load in enumerate(loads):
        if k not in late:
            load.start()
    for k in late:
        loads[k].start()
    lax.fori_loop(1, total, greet, 0)

    def remote(src, dst, send_sem, recv_sem, trow, tcol):
        return pltpu.make_async_remote_copy(
            src_ref=src,
            dst_ref=dst,
            send_sem=send_sem,
            recv_sem=recv_sem,
            device_id={"row": trow, "col": tcol},
            device_id_type=MESH,
        )

    def over(kind):
        if kind == "col":
            return cols, c, lambda k: (r, k)
        if kind == "row":
            return rows, r, lambda k: (k, c)
        return total, r * cols + c, lambda k: (k // cols, lax.rem(k, cols))

    def send_to(args, k):
        kind, plane, src, dst, bulk = args
        _, me, where = over(kind)
        remote(src(k), dst(me), send_sems.at[plane], recv_sems.at[plane], *where(k)).start()

    def start(*args):
        kind = args[0]
        count, me, _ = over(kind)

        def body(t, carry):
            if kind != "row":
                send_to(args, lax.rem(me + t, count))
            else:
                @pl.when(me + t < count)
                def _():
                    send_to(args, lax.rem(me + t, count))

                @pl.when(me >= t)
                def _():
                    send_to(args, lax.rem(me - t + count, count))

            return carry

        lax.fori_loop(1, count, body, 0)

    def everything(kind, plane, bulk):
        count, me, where = over(kind)
        part = bulk.at[pl.ds(0, count - 1)]
        return remote(part, part, send_sems.at[plane], recv_sems.at[plane], *where(lax.rem(me + 1, count)))

    def receive(kind, plane, src, dst, bulk):
        everything(kind, plane, bulk).wait_recv()

    def drain(kind, plane, src, dst, bulk):
        everything(kind, plane, bulk).wait_send()

    for k in range(1, 7):
        loads[k].wait()

    def column(mask_ref, count, offset):
        size = mask_ref.shape[1]
        shape = (count, size)
        hit = lax.broadcasted_iota(jnp.int32, shape, 1) == lax.broadcasted_iota(jnp.int32, shape, 0) + offset
        values = jnp.broadcast_to(mask_ref[...].astype(F32), shape)
        return jnp.sum(jnp.where(hit, values, 0.0), axis=1, keepdims=True)

    seqcol_ref[...] = jnp.broadcast_to(column(seq_ref, seq_local, r * seq_local), seqcol_ref.shape)
    rescol = column(res_ref, res_local, c * res_local)
    tilecol = column(res_ref, tile_rows, r * tile_rows)
    kept = jnp.sum(seq_ref[...].astype(F32), axis=1, keepdims=True)

    def live_column(k):
        parts = []
        for q in range(fold):
            parts.append(rescol * seqcol_ref[pl.ds(k * fold + q, 1), 0:1])
        return jnp.concatenate(parts, axis=0)

    w = w_ref[...].astype(F32)
    w = jnp.concatenate([w, jnp.zeros((LANES - 2 * hidden, channels), F32)], axis=0)
    w_wide = w.T.astype(BF16)
    w_turned = w.astype(BF16)
    bias = pb_ref[...]
    bias = jnp.concatenate([bias, jnp.zeros((1, LANES - 2 * hidden), F32)], axis=1)
    gain = gain_ref[...]
    shift = shift_ref[...]

    loads[0].wait()

    def layer_norm(k, carry):
        here = aligned(k * LANES, LANES)
        widened = x_ref[here, :].astype(F32)
        centred = widened - jnp.mean(widened, axis=-1, keepdims=True)
        inverse = lax.rsqrt(jnp.mean(centred * centred, axis=-1, keepdims=True) + EPSILON)
        scaled = centred * inverse
        normed = (scaled * gain + shift).astype(BF16)
        scaled_ref[here, :] = scaled
        inv_ref[here, :] = inverse
        normed_ref[here, :] = normed
        prj = (nn(normed, w_wide) + bias) * live_column(k)
        prj_ref[here, :] = prj
        tr_ref[here, :] = prj.T
        return carry

    lax.fori_loop(0, chunks, layer_norm, 0, unroll=UNROLL)

    for im in range(majors):
        pieces = [prj_ref[pl.ds(im * fold + k, seq_local, stride=res_local), :] for k in range(fold)]
        left = place_groups(pieces, [k * hidden for k in range(fold)], hidden)
        lsend_ref[:, im * LANES : (im + 1) * LANES] = left.astype(BF16)
    for sb in range(chunks):
        pieces = [
            tr_ref[pl.ds(sb * LANES + hidden + k, majors, stride=fold), :] for k in range(fold)
        ]
        for q in range(fold):
            turned = place_groups(pieces, [(k - q) * res_local for k in range(fold)], res_local)
            u_ref[pl.ds(sb * fold + q, majors, stride=seq_local), :] = turned
    my_seqs = aligned(r * seq_local, seq_local)
    for dm in range(majors):
        rbuf_ref[my_seqs, dm * LANES : (dm + 1) * LANES] = u_ref[
            dm * seq_local : (dm + 1) * seq_local, :
        ].astype(BF16)

    pl.semaphore_wait(barrier, total - 1)

    def left_slot(k):
        return lbuf_ref.at[aligned((k // factor) * seq_local, seq_local), aligned(lax.rem(k, factor) * block, block)]

    relay_row = c // factor
    relay_col = r * factor + lax.rem(c, factor)
    at_home = jnp.logical_and(relay_row == r, relay_col == c)
    left_out = remote(
        lsend_ref, left_slot(relay_col), one_sems.at[0], one_sems.at[1], relay_row, relay_col
    )
    left_home = pltpu.make_async_copy(lsend_ref, left_slot(c), local_sems.at[0])

    @pl.when(at_home)
    def _():
        left_home.start()

    @pl.when(jnp.logical_not(at_home))
    def _():
        left_out.start()

    def right_block(k):
        return rbuf_ref.at[aligned(k * seq_local, seq_local), :]

    right_args = ("row", 0, lambda k: right_block(r), right_block, grr_ref)

    start(*right_args)
    for k in late:
        loads[k].wait()
    owf_ref[...] = ow_ref[...].astype(F32)
    for d in range(hidden):
        wp_ref[d * hidden : (d + 1) * hidden, :] = owf_ref[pl.ds(d, hidden, stride=hidden), :].astype(BF16)

    def inverse_divisor(i):
        return 1.0 / jnp.maximum(kept * tilecol[i : i + 1, :] * rescol, 1.0)

    for i in range(tile_rows):
        here = slice(i * res_local, (i + 1) * res_local)
        gpre_ref[here, :] = (cot_ref[here, :].astype(F32) * inverse_divisor(i)).astype(BF16)

    half = WIDE // LANES

    def grad_products(ip, carry):
        upstream = gpre_ref[aligned(ip * WIDE, WIDE), :]
        for dm in range(majors):
            tile = nt(wp_ref[dm * LANES : (dm + 1) * LANES, :], upstream)
            for h in range(half):
                blocks = [
                    tile[a * hidden : (a + 1) * hidden, h * LANES : (h + 1) * LANES] for a in range(fold)
                ]
                for a, swapped in enumerate(lane_group_swap(blocks, res_local)):
                    gp_ref[
                        aligned(((ip * half + h) * fold + a) * hidden, hidden), dm * LANES : (dm + 1) * LANES
                    ] = swapped.astype(BF16)
        return carry

    steps = pairs // WIDE
    lax.fori_loop(0, steps, grad_products, 0)

    @pl.when(at_home)
    def _():
        left_home.wait()

    @pl.when(jnp.logical_not(at_home))
    def _():
        remote(
            left_slot(c), left_slot(c), one_sems.at[0], one_sems.at[1], relay_row, relay_col
        ).wait_recv()

    left_args = ("col", 1, lambda k: left_slot(c), left_slot, glr_ref)
    start(*left_args)
    receive(*left_args)
    for k in range(block // WIDE):
        grs_ref[:, k * WIDE : (k + 1) * WIDE] = nn(lbuf_ref[...], gp_ref[:, k * WIDE : (k + 1) * WIDE]).astype(BF16)
    gr_args = (
        "row",
        3,
        lambda k: grs_ref.at[aligned(k * seq_local, seq_local), :],
        lambda k: grr_ref.at[k],
        grr_ref,
    )
    receive(*right_args)
    start(*gr_args)

    def gl_part(k):
        return gls_ref.at[aligned((k // factor) * seq_local, seq_local), aligned(lax.rem(k, factor) * block, block)]

    for k in range(tile_rows * hidden // WIDE):
        gls_ref[:, k * WIDE : (k + 1) * WIDE] = nt(rbuf_ref[...], gp_ref[k * WIDE : (k + 1) * WIDE, :]).astype(BF16)
    gl_args = ("col", 2, gl_part, lambda k: glr_ref.at[k], glr_ref)
    start(*gl_args)

    w_block = hidden * hidden // cols
    gw_row_args = (
        "col",
        4,
        lambda k: gws_ref.at[aligned(k * w_block, w_block), :],
        lambda k: gwr_ref.at[k],
        gwr_ref,
    )
    for k in range(hidden * hidden // WIDE):
        rows_here = slice(k * WIDE, (k + 1) * WIDE)
        right = rbuf_ref[:, k * (WIDE // hidden) * res_local : (k + 1) * (WIDE // hidden) * res_local]

        def products(im, carry, k=k, right=right):
            tile = tn(lbuf_ref[:, aligned(im * LANES, LANES)], right)
            for h in range(half):
                blocks = [
                    tile[a * hidden : (a + 1) * hidden, h * LANES : (h + 1) * LANES] for a in range(fold)
                ]
                for a, swapped in enumerate(lane_group_swap(blocks, res_local)):
                    at = ((k * half + h) * fold + a) * hidden
                    prod_ref[at : at + hidden, aligned(im * LANES, LANES)] = swapped.astype(BF16)
            return carry

        lax.fori_loop(0, tile_rows // fold, products, 0, unroll=8)
        gws_ref[rows_here, :] = nn(prod_ref[rows_here, :], gpre_ref[...]).astype(BF16)
        for target in range(k * WIDE // w_block, (k + 1) * WIDE // w_block):

            @pl.when(c != target)
            def _(target=target):
                send_to(gw_row_args, target)

    receive(*gl_args)
    mine = gls_ref[aligned((c // factor) * seq_local, seq_local), aligned(lax.rem(c, factor) * block, block)]

    def add_left(t, carry):
        return carry + glr_ref[lax.rem(c + t, cols)].astype(F32)

    glmid_ref[...] = lax.fori_loop(1, cols, add_left, mine.astype(F32)).astype(BF16)
    gl_out = remote(glmid_ref, glfin_ref, one_sems.at[2], one_sems.at[3], relay_row, relay_col)
    gl_home = pltpu.make_async_copy(glmid_ref, glfin_ref, local_sems.at[1])

    @pl.when(at_home)
    def _():
        gl_home.start()

    @pl.when(jnp.logical_not(at_home))
    def _():
        gl_out.start()

    out_bias = ob_ref[...]
    for k in range(pairs // WIDE):
        pre = tn(wp_ref[...], prod_ref[:, k * WIDE : (k + 1) * WIDE]).T + out_bias
        for q in range(WIDE // res_local):
            i = k * (WIDE // res_local) + q
            pair_ref[i * res_local : (i + 1) * res_local, :] = (
                pre[q * res_local : (q + 1) * res_local, :] * inverse_divisor(i)
            ).astype(BF16)

    w_small = w_block // rows
    receive(*gw_row_args)
    summed = gws_ref[aligned(c * w_block, w_block), :].astype(F32)

    def add_w(t, carry):
        return carry + gwr_ref[lax.rem(c + t, cols)].astype(F32)

    summed = lax.fori_loop(1, cols, add_w, summed).astype(BF16)
    for k in range(rows):
        gwc_ref[k] = summed[k * w_small : (k + 1) * w_small, :]
    gw_col_args = ("row", 5, lambda k: gwc_ref.at[k], lambda k: gwcr_ref.at[k], gwcr_ref)
    start(*gw_col_args)

    receive(*gr_args)
    for dm in range(majors):
        part = slice(dm * LANES, (dm + 1) * LANES)
        total_right = grs_ref[my_seqs, part].astype(F32)

        def add_right(t, carry, part=part):
            return carry + grr_ref[lax.rem(r + t, rows), :, part].astype(F32)

        u_ref[dm * seq_local : (dm + 1) * seq_local, :] = lax.fori_loop(1, rows, add_right, total_right)
    for sb in range(chunks):
        pieces = [u_ref[pl.ds(sb * fold + q, majors, stride=seq_local), :] for q in range(fold)]
        for k in range(fold):
            turned = place_groups(pieces, [(q - k) * res_local for q in range(fold)], res_local)
            tr_ref[pl.ds(sb * LANES + hidden + k, majors, stride=fold), :] = turned

    @pl.when(at_home)
    def _():
        gl_home.wait()

    @pl.when(jnp.logical_not(at_home))
    def _():
        remote(glmid_ref, glfin_ref, one_sems.at[2], one_sems.at[3], relay_row, relay_col).wait_recv()

    for im in range(majors):
        piece = glfin_ref[:, im * LANES : (im + 1) * LANES].astype(F32)
        for k in range(fold):
            rolled = pltpu.roll(piece, LANES - k * hidden, 1) if k else piece
            prj_ref[pl.ds(im * fold + k, seq_local, stride=res_local), :] = rolled

    lane = lax.broadcasted_iota(jnp.int32, (LANES, LANES), 1)

    def backward(k, carry):
        bias_sum, gain_sum, shift_sum = carry
        here = aligned(k * LANES, LANES)
        projected = jnp.where(lane < hidden, prj_ref[here, :], tr_ref[here, :].T)
        projected = jnp.where(lane < 2 * hidden, projected * live_column(k), 0.0)
        low = projected.astype(BF16)
        low_ref[here, :] = low
        upstream = nn(low, w_turned)
        scaled = scaled_ref[here, :]
        bias_sum = bias_sum + jnp.sum(projected, axis=0, keepdims=True)
        gain_sum = gain_sum + jnp.sum(upstream * scaled, axis=0, keepdims=True)
        shift_sum = shift_sum + jnp.sum(upstream, axis=0, keepdims=True)
        grad_scaled = upstream * gain
        first = jnp.mean(grad_scaled, axis=-1, keepdims=True)
        second = jnp.mean(grad_scaled * scaled, axis=-1, keepdims=True)
        ag_ref[here, :] = (inv_ref[here, :] * (grad_scaled - first - scaled * second)).astype(BF16)
        return bias_sum, gain_sum, shift_sum

    sums = (jnp.zeros((1, LANES), F32), jnp.zeros((1, channels), F32), jnp.zeros((1, channels), F32))
    split = chunks // 2
    sums = lax.fori_loop(0, split, backward, sums, unroll=min(UNROLL, split))
    receive(*gw_col_args)

    def add_w_col(t, carry):
        return carry + gwcr_ref[lax.rem(r + t, rows)].astype(F32)

    gwg_ref[r] = lax.fori_loop(1, rows, add_w_col, gwc_ref[r].astype(F32)).astype(BF16)
    gw_up_args = ("row", 9, lambda k: gwg_ref.at[r], lambda k: gwg_ref.at[k], gwcr_ref)
    start(*gw_up_args)

    bias_sum, gain_sum, shift_sum = lax.fori_loop(
        split, chunks, backward, sums, unroll=min(UNROLL, chunks - split)
    )
    grad_w_in = tn(low_ref[...], normed_ref[...])
    quarter = 2 * hidden // cols
    for k in range(cols):
        sw_ref[k] = grad_w_in[k * quarter : (k + 1) * quarter, :].astype(BF16)
    sv_ref[0:1, :] = gain_sum
    sv_ref[1:2, :] = shift_sum
    sv_ref[2:3, :] = jnp.concatenate([bias_sum, jnp.zeros((1, channels - LANES), F32)], axis=1)
    sv_ref[3:8, :] = jnp.zeros((5, channels), F32)
    sw_args = ("all", 6, lambda k: sw_ref.at[lax.rem(k, cols)], lambda k: swr_ref.at[k], swr_ref)
    sv_row_args = ("col", 7, lambda k: sv_ref, lambda k: svr_ref.at[k], svr_ref)
    start(*sv_row_args)
    start(*sw_args)

    def ordered(received, count):
        def add(t, carry):
            return carry + received[t].astype(F32)

        return lax.fori_loop(1, count, add, received[0].astype(F32))

    svr_ref[c] = sv_ref[...]
    receive(*sv_row_args)
    svc_ref[...] = ordered(svr_ref, cols)
    sv_col_args = ("row", 8, lambda k: svc_ref, lambda k: svcr_ref.at[k], svcr_ref)
    start(*sv_col_args)

    receive(*gw_up_args)
    gw_ref[c] = gwg_ref[...]
    gw_out_args = ("col", 10, lambda k: gwg_ref, lambda k: gw_ref.at[k], gw_ref)
    start(*gw_out_args)

    swr_ref[r * cols + c] = sw_ref[c]
    receive(*sw_args)
    swf_ref[...] = ordered(swr_ref, total)
    gpw_ref[c] = swf_ref[...]
    sw_out_args = ("col", 11, lambda k: swf_ref, lambda k: gpw_ref.at[k], gpw_ref)
    start(*sw_out_args)
    svcr_ref[r] = svc_ref[...]
    receive(*sv_col_args)
    vec_ref[...] = ordered(svcr_ref, rows)
    receive(*gw_out_args)
    receive(*sw_out_args)

    @pl.when(jnp.logical_not(at_home))
    def _():
        left_out.wait_send()
        gl_out.wait_send()

    for args in (
        right_args,
        left_args,
        gl_args,
        gr_args,
        gw_row_args,
        gw_col_args,
        sw_args,
        sv_row_args,
        gw_up_args,
        sv_col_args,
        gw_out_args,
        sw_out_args,
    ):
        drain(*args)


def finish_kernel(pair_ref, ag_ref, gw_ref, gpw_ref, vec_ref, pair_hbm, ag_hbm, gain_ref, shift_ref, gpw_out, bias_ref, gw_hbm, gwf_ref, mixed_ref, sems):
    copies = [
        pltpu.make_async_copy(ag_ref, ag_hbm, sems.at[0]),
        pltpu.make_async_copy(pair_ref, pair_hbm, sems.at[1]),
        pltpu.make_async_copy(gwf_ref, gw_hbm, sems.at[2]),
    ]
    copies[0].start()
    copies[1].start()
    mixed_ref[...] = gw_ref[...].astype(F32)
    hidden = bias_ref.shape[1] // 2
    for k in range(hidden):
        gwf_ref[k * hidden : (k + 1) * hidden, :] = mixed_ref[pl.ds(k, hidden, stride=hidden), :]
    copies[2].start()
    gain_ref[...] = vec_ref[0:1, :]
    shift_ref[...] = vec_ref[1:2, :]
    bias_ref[...] = vec_ref[2:3, : bias_ref.shape[1]]
    gpw_out[...] = gpw_ref[...]
    for copy in copies:
        copy.wait()


def shards(
    alignment,
    sequence_mask,
    residue_mask,
    layer_norm_gain,
    norm_shift,
    proj_weight,
    proj_bias,
    out_weight,
    out_bias,
    cotangent,
):
    rows = lax.axis_size("row")
    cols = lax.axis_size("col")
    factor = cols // rows
    seq_local, res_local, channels = alignment.shape
    seqs = seq_local * rows
    hidden = proj_weight.shape[1] // 2
    width = out_weight.shape[1]
    tile_rows = res_local * factor
    n = seq_local * res_local
    pairs = tile_rows * res_local
    block = res_local * hidden
    majors = block // LANES
    inner = tile_rows * hidden
    w_block = hidden * hidden // cols
    w_small = w_block // rows
    quarter = 2 * hidden // cols
    dims = (rows, cols, seq_local, res_local, hidden, channels, width)
    vmem = pl.BlockSpec(memory_space=pltpu.VMEM)
    hbm = pl.BlockSpec(memory_space=pltpu.HBM)
    operands = [
        alignment.reshape(n, channels),
        sequence_mask.reshape(1, -1),
        residue_mask.reshape(1, -1),
        layer_norm_gain.reshape(1, -1),
        norm_shift.reshape(1, -1),
        proj_weight.T,
        proj_bias.reshape(1, -1),
        out_weight,
        out_bias.reshape(1, -1),
        cotangent.reshape(pairs, width),
    ]
    operands = [pltpu.with_memory_space_constraint(array, pltpu.HBM) for array in operands]
    pair, grad_alignment, grad_w, grad_pw, vectors = pl.pallas_call(
        functools.partial(fused_kernel, dims),
        out_shape=[
            jax.ShapeDtypeStruct((pairs, width), BF16),
            jax.ShapeDtypeStruct((n, channels), BF16),
            jax.ShapeDtypeStruct((cols, rows, w_small, width), BF16),
            jax.ShapeDtypeStruct((cols, quarter, channels), F32),
            jax.ShapeDtypeStruct((8, channels), F32),
        ],
        in_specs=[hbm] * 10,
        out_specs=[vmem] * 5,
        scratch_shapes=[
            *[pltpu.VMEM(array.shape, array.dtype) for array in operands],
            pltpu.VMEM((n, channels), F32),
            pltpu.VMEM((n, 1), F32),
            pltpu.VMEM((n, channels), BF16),
            pltpu.VMEM((n, LANES), F32),
            pltpu.VMEM((n, LANES), F32),
            pltpu.VMEM((majors * seq_local, LANES), F32),
            pltpu.VMEM((seq_local, LANES), F32),
            pltpu.VMEM((seq_local, block), BF16),
            pltpu.VMEM((seqs, inner), BF16),
            pltpu.VMEM((seqs, block), BF16),
            pltpu.VMEM((hidden * hidden, width), F32),
            pltpu.VMEM((hidden * hidden, width), BF16),
            pltpu.VMEM((pairs, width), BF16),
            pltpu.VMEM((inner, block), BF16),
            pltpu.VMEM((hidden * hidden, pairs), BF16),
            pltpu.VMEM((seqs, inner), BF16),
            pltpu.VMEM((cols, seq_local, block), BF16),
            pltpu.VMEM((seq_local, block), BF16),
            pltpu.VMEM((seq_local, block), BF16),
            pltpu.VMEM((seqs, block), BF16),
            pltpu.VMEM((rows, seq_local, block), BF16),
            pltpu.VMEM((hidden * hidden, width), BF16),
            pltpu.VMEM((cols, w_block, width), BF16),
            pltpu.VMEM((rows, w_small, width), BF16),
            pltpu.VMEM((rows, w_small, width), BF16),
            pltpu.VMEM((rows, w_small, width), BF16),
            pltpu.VMEM((n, LANES), BF16),
            pltpu.VMEM((cols, quarter, channels), BF16),
            pltpu.VMEM((rows * cols, quarter, channels), BF16),
            pltpu.VMEM((quarter, channels), F32),
            pltpu.VMEM((8, channels), F32),
            pltpu.VMEM((cols, 8, channels), F32),
            pltpu.VMEM((8, channels), F32),
            pltpu.VMEM((rows, 8, channels), F32),
            pltpu.SemaphoreType.DMA((12,)),
            pltpu.SemaphoreType.DMA((4,)),
            pltpu.SemaphoreType.DMA((12,)),
            pltpu.SemaphoreType.DMA((12,)),
        ],
        compiler_params=pltpu.CompilerParams(
            collective_id=0, has_side_effects=True, vmem_limit_bytes=48 * 1024 * 1024
        ),
    )(*operands)
    pair, grad_alignment, gain, shift, grad_pw, bias, grad_w = pl.pallas_call(
        finish_kernel,
        out_shape=[
            jax.ShapeDtypeStruct((pairs, width), BF16),
            jax.ShapeDtypeStruct((n, channels), BF16),
            jax.ShapeDtypeStruct((1, channels), F32),
            jax.ShapeDtypeStruct((1, channels), F32),
            jax.ShapeDtypeStruct((2 * hidden, channels), F32),
            jax.ShapeDtypeStruct((1, 2 * hidden), F32),
            jax.ShapeDtypeStruct((hidden * hidden, width), F32),
        ],
        in_specs=[vmem] * 5,
        out_specs=[hbm, hbm, vmem, vmem, vmem, vmem, hbm],
        scratch_shapes=[
            pltpu.VMEM((hidden * hidden, width), F32),
            pltpu.VMEM((hidden * hidden, width), F32),
            pltpu.SemaphoreType.DMA((3,)),
        ],
        compiler_params=pltpu.CompilerParams(vmem_limit_bytes=16 * 1024 * 1024),
    )(pair, grad_alignment, grad_w.reshape(hidden * hidden, width), grad_pw.reshape(-1, channels), vectors)
    return (
        pair.reshape(tile_rows, res_local, width),
        grad_alignment.reshape(seq_local, res_local, channels),
        gain.reshape(-1),
        shift.reshape(-1),
        grad_pw.T,
        bias.reshape(-1),
        grad_w,
    )


def solution(mesh):
    return jax.shard_map(
        shards,
        mesh=mesh,
        in_specs=(
            P(("groups", "row"), "col", None),
            P("groups"),
            P("groups"),
            P(),
            P(),
            P(),
            P(),
            P(),
            P(),
            P(("groups", "row"), "col", None),
        ),
        out_specs=(
            P(("groups", "row"), "col", None),
            P(("groups", "row"), "col", None),
            P("groups"),
            P("groups"),
            P("groups", None),
            P("groups"),
            P("groups", None),
        ),
        check_vma=False,
    )
```

```python
import functools

import jax
import jax.numpy as jnp
from jax import lax
from jax.experimental import pallas as pl
from jax.experimental.pallas import tpu as pltpu
from jax.sharding import PartitionSpec as P

EPSILON = 1e-05
LANES = 128
WIDE = 256
UNROLL = 4
MESH = pl.DeviceIdType.MESH
F32 = jnp.float32
BF16 = jnp.bfloat16


def lane_group_swap(blocks, width):
    lane = lax.broadcasted_iota(jnp.int32, blocks[0].shape, 1)
    span = len(blocks) // 2
    while span:
        low = (lane // (width * span)) % 2 == 0
        out = list(blocks)
        for a in range(len(blocks)):
            if a & span:
                continue
            first, second = blocks[a], blocks[a + span]
            shift = width * span
            out[a] = jnp.where(low, first, pltpu.roll(second, shift, 1))
            out[a + span] = jnp.where(low, pltpu.roll(first, LANES - shift, 1), second)
        blocks = out
        span //= 2
    return blocks


def place_groups(pieces, shifts, width):
    group = lax.broadcasted_iota(jnp.int32, pieces[0].shape, 1) // width
    out = None
    for k, (piece, shift) in enumerate(zip(pieces, shifts)):
        rolled = pltpu.roll(piece, shift % LANES, 1) if shift % LANES else piece
        out = rolled if out is None else jnp.where(group == k, rolled, out)
    return out


def nt(a, b):
    return lax.dot_general(a, b, (((1,), (1,)), ((), ())), preferred_element_type=F32)


def tn(a, b):
    return lax.dot_general(a, b, (((0,), (0,)), ((), ())), preferred_element_type=F32)


def nn(a, b):
    return jnp.dot(a, b, preferred_element_type=F32)


def aligned(start, size, step=None):
    return pl.ds(pl.multiple_of(start, step or size), size)


def fused_kernel(dims, *refs):
    rows, cols, seq_local, res_local, hidden, channels, width = dims
    inputs = refs[:10]
    (pair_ref, ag_ref, gwf_ref, gpw_ref, vec_ref) = refs[10:15]
    (
        x_ref,
        seq_ref,
        res_ref,
        gain_ref,
        shift_ref,
        w_ref,
        pb_ref,
        ow_ref,
        ob_ref,
        cot_ref,
        scaled_ref,
        inv_ref,
        both_ref,
        prj_ref,
        tr_ref,
        u_ref,
        seqcol_ref,
        lsend_ref,
        lbuf_ref,
        lt_ref,
        rbuf_ref,
        owf_ref,
        wp_ref,
        wpt_ref,
        gpre_ref,
        gp_ref,
        prod_ref,
        gls_ref,
        glr_ref,
        glp_ref,
        glx_ref,
        glmid_ref,
        glfin_ref,
        grs_ref,
        grr_ref,
        gws_ref,
        gwr_ref,
        gwp_ref,
        gwx_ref,
        gwc_ref,
        gwcr_ref,
        gw_ref,
        low_ref,
        sw_ref,
        swp_ref,
        swx_ref,
        swr_ref,
        swf_ref,
        sv_ref,
        svr_ref,
        svc_ref,
        svcr_ref,
        local_sems,
        one_sems,
        send_sems,
        recv_sems,
        left_send,
        left_recv,
    ) = refs[15:]
    r = lax.axis_index("row")
    c = lax.axis_index("col")
    factor = cols // rows
    seqs = seq_local * rows
    tile_rows = res_local * factor
    n = seq_local * res_local
    pairs = tile_rows * res_local
    block = res_local * hidden
    fold = LANES // res_local
    chunks = n // LANES
    majors = block // LANES
    total = rows * cols
    chips = cols // 2
    chip = c // 2
    core = lax.rem(c, 2)
    partner = chip * 2 + 1 - core
    barrier = pltpu.get_barrier_semaphore()

    def greet(t, carry):
        other = lax.rem(r * cols + c + t, total)
        pl.semaphore_signal(
            barrier,
            inc=1,
            device_id={"row": other // cols, "col": lax.rem(other, cols)},
            device_id_type=MESH,
        )
        return carry

    staged = (x_ref, seq_ref, res_ref, gain_ref, shift_ref, w_ref, pb_ref, ow_ref, ob_ref, cot_ref)
    loads = [
        pltpu.make_async_copy(source, target, local_sems.at[2 + k])
        for k, (source, target) in enumerate(zip(inputs, staged))
    ]
    late = (7, 8, 9)
    for k, load in enumerate(loads):
        if k not in late:
            load.start()
    for k in late:
        loads[k].start()
    lax.fori_loop(1, total, greet, 0)

    def remote(src, dst, send_sem, recv_sem, trow, tcol):
        return pltpu.make_async_remote_copy(
            src_ref=src,
            dst_ref=dst,
            send_sem=send_sem,
            recv_sem=recv_sem,
            device_id={"row": trow, "col": tcol},
            device_id_type=MESH,
        )

    gw_bulk = gws_ref.at[pl.ds(0, (rows * chips - 1) * (hidden * hidden // total)), :]

    def over(kind):
        if kind == "col":
            return cols, c, lambda k: (r, k)
        if kind == "row":
            return rows, r, lambda k: (k, c)
        if kind == "chip":
            return chips, chip, lambda k: (r, 2 * k + core)
        return rows * chips, r * chips + chip, lambda k: (k // chips, 2 * lax.rem(k, chips) + core)

    def send_to(args, k):
        kind, plane, src, dst, bulk = args
        _, me, where = over(kind)
        remote(src(k), dst(me), send_sems.at[plane], recv_sems.at[plane], *where(k)).start()

    def start(*args):
        kind = args[0]
        count, me, _ = over(kind)

        def body(t, carry):
            if kind != "row":
                send_to(args, lax.rem(me + t, count))
            else:
                @pl.when(me + t < count)
                def _():
                    send_to(args, lax.rem(me + t, count))

                @pl.when(me >= t)
                def _():
                    send_to(args, lax.rem(me - t + count, count))

            return carry

        lax.fori_loop(1, count, body, 0)

    def everything(kind, plane, bulk):
        count, me, where = over(kind)
        part = bulk if bulk is gw_bulk else bulk.at[pl.ds(0, count - 1)]
        return remote(part, part, send_sems.at[plane], recv_sems.at[plane], *where(lax.rem(me + 1, count)))

    def hand(plane, src, dst):
        remote(src, dst, send_sems.at[plane], recv_sems.at[plane], r, partner).start()

    def handed(plane, bulk):
        return remote(bulk, bulk, send_sems.at[plane], recv_sems.at[plane], r, partner)

    def receive(kind, plane, src, dst, bulk):
        everything(kind, plane, bulk).wait_recv()

    def drain(kind, plane, src, dst, bulk):
        everything(kind, plane, bulk).wait_send()

    for k in range(1, 7):
        loads[k].wait()

    def column(mask_ref, count, offset):
        size = mask_ref.shape[1]
        shape = (count, size)
        hit = lax.broadcasted_iota(jnp.int32, shape, 1) == lax.broadcasted_iota(jnp.int32, shape, 0) + offset
        values = jnp.broadcast_to(mask_ref[...].astype(F32), shape)
        return jnp.sum(jnp.where(hit, values, 0.0), axis=1, keepdims=True)

    seqcol_ref[...] = jnp.broadcast_to(column(seq_ref, seq_local, r * seq_local), seqcol_ref.shape)
    rescol = column(res_ref, res_local, c * res_local)
    tilecol = column(res_ref, tile_rows, r * tile_rows)
    kept = jnp.sum(seq_ref[...].astype(F32), axis=1, keepdims=True)

    def live_column(k):
        parts = []
        for q in range(fold):
            parts.append(rescol * seqcol_ref[pl.ds(k * fold + q, 1), 0:1])
        return jnp.concatenate(parts, axis=0)

    w = w_ref[...].astype(F32)
    w = jnp.concatenate([w, jnp.zeros((LANES - 2 * hidden, channels), F32)], axis=0)
    w_wide = w.T.astype(BF16)
    w_turned = w.astype(BF16)
    bias = pb_ref[...]
    bias = jnp.concatenate([bias, jnp.zeros((1, LANES - 2 * hidden), F32)], axis=1)
    gain = gain_ref[...]
    shift = shift_ref[...]

    loads[0].wait()

    def layer_norm(k, carry):
        here = aligned(k * LANES, LANES)
        widened = x_ref[here, :].astype(F32)
        centred = widened - jnp.mean(widened, axis=-1, keepdims=True)
        inverse = lax.rsqrt(jnp.mean(centred * centred, axis=-1, keepdims=True) + EPSILON)
        scaled = centred * inverse
        normed = (scaled * gain + shift).astype(BF16)
        scaled_ref[here, :] = scaled
        inv_ref[here, :] = inverse
        both_ref[here, :channels] = normed
        both_ref[here, channels:] = scaled.astype(BF16)
        prj = (nn(normed, w_wide) + bias) * live_column(k)
        prj_ref[here, :] = prj
        tr_ref[here, :] = prj.T
        return carry

    lax.fori_loop(0, chunks, layer_norm, 0, unroll=min(2 * UNROLL, chunks))

    for im in range(majors):
        pieces = [prj_ref[pl.ds(im * fold + k, seq_local, stride=res_local), :] for k in range(fold)]
        left = place_groups(pieces, [k * hidden for k in range(fold)], hidden)
        lsend_ref[:, im * LANES : (im + 1) * LANES] = left.astype(BF16)
    for sb in range(chunks):
        pieces = [
            tr_ref[pl.ds(sb * LANES + hidden + k, majors, stride=fold), :] for k in range(fold)
        ]
        for q in range(fold):
            turned = place_groups(pieces, [(k - q) * res_local for k in range(fold)], res_local)
            u_ref[pl.ds(sb * fold + q, majors, stride=seq_local), :] = turned
    my_seqs = aligned(r * seq_local, seq_local)
    for dm in range(majors):
        rbuf_ref[my_seqs, dm * LANES : (dm + 1) * LANES] = u_ref[
            dm * seq_local : (dm + 1) * seq_local, :
        ].astype(BF16)

    pl.semaphore_wait(barrier, total - 1)

    def left_slot(k):
        return lbuf_ref.at[aligned((k // factor) * seq_local, seq_local), aligned(lax.rem(k, factor) * block, block)]

    relay_row = c // factor
    relay_col = r * factor + lax.rem(c, factor)
    left_col = chip * 2 + lax.rem(r, 2)
    left_stays = jnp.logical_and(relay_row == r, left_col == c)
    left_out = remote(
        lsend_ref, left_slot(relay_col), one_sems.at[0], left_recv.at[relay_col], relay_row, left_col
    )
    left_home = pltpu.make_async_copy(lsend_ref, left_slot(relay_col), local_sems.at[0])

    @pl.when(left_stays)
    def _():
        left_home.start()

    @pl.when(jnp.logical_not(left_stays))
    def _():
        left_out.start()

    HAND_GL, HAND_A, HAND_B, HAND_LEFT, HAND_OUT, HAND_SW = 12, 13, 14, 15, 16, 10

    def passed(i, q):
        row = 2 * lax.rem(r // 2 + i, rows // 2) + core
        near = (r * factor + q) // 2 == chip
        return row * factor + q, near, jnp.logical_and(row == r, r * factor + q == c)

    def pass_left(i):
        for q in range(factor):
            k, near, own = passed(i, q)
            slot = left_slot(k)

            @pl.when(own)
            def _():
                left_home.wait()

            @pl.when(jnp.logical_not(own))
            def _():
                remote(slot, slot, one_sems.at[0], left_recv.at[k], r, partner).wait_recv()

            @pl.when(near)
            def _():
                def body(t, carry):
                    other = lax.rem(chip + t, chips)
                    remote(slot, slot, left_send.at[k], left_recv.at[k], r, 2 * other + core).start()
                    return carry

                lax.fori_loop(1, chips, body, 0)

            hand(HAND_LEFT, slot, slot)

    def right_block(k):
        return rbuf_ref.at[aligned(k * seq_local, seq_local), :]

    right_args = ("row", 0, lambda k: right_block(r), right_block, grr_ref)

    start(*right_args)
    for k in late:
        loads[k].wait()
    owf_ref[...] = ow_ref[...].astype(F32)
    for d in range(hidden):
        wp_ref[d * hidden : (d + 1) * hidden, :] = owf_ref[pl.ds(d, hidden, stride=hidden), :].astype(BF16)

    def inverse_divisor(i):
        return 1.0 / jnp.maximum(kept * tilecol[i : i + 1, :] * rescol, 1.0)

    for i in range(tile_rows):
        here = slice(i * res_local, (i + 1) * res_local)
        gpre_ref[here, :] = (cot_ref[here, :].astype(F32) * inverse_divisor(i)).astype(BF16)

    half = WIDE // LANES

    def grad_products(ip, carry):
        upstream = gpre_ref[aligned(ip * WIDE, WIDE), :]
        for dm in range(majors):
            tile = nt(wp_ref[dm * LANES : (dm + 1) * LANES, :], upstream)
            for h in range(half):
                blocks = [
                    tile[a * hidden : (a + 1) * hidden, h * LANES : (h + 1) * LANES] for a in range(fold)
                ]
                for a, swapped in enumerate(lane_group_swap(blocks, res_local)):
                    gp_ref[
                        aligned(((ip * half + h) * fold + a) * hidden, hidden), dm * LANES : (dm + 1) * LANES
                    ] = swapped.astype(BF16)
        return carry

    steps = pairs // WIDE
    lax.fori_loop(0, steps // 2, grad_products, 0)
    pass_left(0)
    lax.fori_loop(steps // 2, steps, grad_products, 0)

    for i in range(1, rows // 2):
        pass_left(i)
    handed(HAND_LEFT, glp_ref).wait_recv()
    for k in range(block // WIDE):
        grs_ref[:, k * WIDE : (k + 1) * WIDE] = nn(lbuf_ref[...], gp_ref[:, k * WIDE : (k + 1) * WIDE]).astype(BF16)
    gr_args = (
        "row",
        3,
        lambda k: grs_ref.at[aligned(k * seq_local, seq_local), :],
        lambda k: grr_ref.at[k],
        grr_ref,
    )
    for im in range(tile_rows * hidden // LANES):
        lt_ref[im * LANES : (im + 1) * LANES, :] = lbuf_ref[:, im * LANES : (im + 1) * LANES].T
    for k in range(hidden * hidden // LANES):
        wpt_ref[:, k * LANES : (k + 1) * LANES] = wp_ref[k * LANES : (k + 1) * LANES, :].T
    receive(*right_args)
    start(*gr_args)

    def gl_part(k):
        return gls_ref.at[aligned((k // factor) * seq_local, seq_local), aligned(lax.rem(k, factor) * block, block)]

    for k in range(tile_rows * hidden // WIDE):
        gls_ref[:, k * WIDE : (k + 1) * WIDE] = nt(rbuf_ref[...], gp_ref[k * WIDE : (k + 1) * WIDE, :]).astype(BF16)

    def hand_left(k, carry):
        hand(HAND_GL, gl_part((1 - core) * chips + k), glp_ref.at[k])
        return carry

    lax.fori_loop(0, chips, hand_left, 0)
    gl_args = ("chip", 2, lambda k: glx_ref.at[k], lambda k: glr_ref.at[k], glr_ref)

    def sum_left():
        handed(HAND_GL, glp_ref).wait_recv()

        def add(k, carry):
            t = core * chips + k
            mine = gls_ref[aligned((t // factor) * seq_local, seq_local), aligned(lax.rem(t, factor) * block, block)]
            glx_ref[k] = (mine.astype(F32) + glp_ref[k].astype(F32)).astype(BF16)
            return carry

        lax.fori_loop(0, chips, add, 0)
        start(*gl_args)


    w_block = hidden * hidden // cols
    gw_row_args = ("chip", 4, lambda k: gwx_ref.at[k], lambda k: gwr_ref.at[k], gwr_ref)
    strips = hidden * hidden // WIDE
    per = WIDE // w_block
    first = lax.rem((chip + 1) * 2 * w_block // WIDE, strips)

    def sum_weight(later):
        plane = HAND_B if later else HAND_A
        some = chips // 2
        offset = some if later else 0
        handed(plane, gwp_ref.at[pl.ds(0, some)]).wait_recv()

        def add(k, carry):
            k = lax.rem(first * per // 2 + offset + k, chips)
            t = 2 * k + core
            mine = gws_ref[aligned(t * w_block, w_block), :]
            gwx_ref[k] = (mine.astype(F32) + gwp_ref[k].astype(F32)).astype(BF16)

            @pl.when(k != chip)
            def _():
                send_to(gw_row_args, k)

            return carry

        lax.fori_loop(0, some, add, 0)

    for k in range(strips):
        strip = lax.rem(first + k, strips)
        right = rbuf_ref[:, aligned(strip * WIDE, WIDE)]

        def products(im, carry, strip=strip, right=right):
            tile = nn(lt_ref[aligned(im * LANES, LANES), :], right)
            for h in range(half):
                blocks = [
                    tile[a * hidden : (a + 1) * hidden, h * LANES : (h + 1) * LANES] for a in range(fold)
                ]
                for a, swapped in enumerate(lane_group_swap(blocks, res_local)):
                    at = strip * WIDE + (h * fold + a) * hidden
                    prod_ref[aligned(at, hidden), aligned(im * LANES, LANES)] = swapped.astype(BF16)
            return carry

        lax.fori_loop(0, tile_rows // fold, products, 0, unroll=8)
        here = aligned(strip * WIDE, WIDE)
        gws_ref[here, :] = nn(prod_ref[here, :], gpre_ref[...]).astype(BF16)
        for j in range(per):
            target = strip * per + j

            @pl.when(lax.rem(target, 2) != core)
            def _(target=target, k=k):
                hand(
                    HAND_A if k < strips // 2 else HAND_B,
                    gws_ref.at[aligned(target * w_block, w_block), :],
                    gwp_ref.at[target // 2],
                )

        if k == 0:
            sum_left()
        if k == strips // 2:
            sum_weight(False)

    receive(*gl_args)

    def add_left(t, carry):
        return carry + glr_ref[lax.rem(chip + t, chips)].astype(F32)

    glmid_ref[...] = lax.fori_loop(1, chips, add_left, glx_ref[chip].astype(F32)).astype(BF16)
    gathered = core * chips + chip
    owner_row = gathered // factor
    owner_col = r * factor + lax.rem(gathered, factor)
    at_home = jnp.logical_and(owner_row == r, owner_col == c)
    gl_out = remote(glmid_ref, glfin_ref, one_sems.at[2], one_sems.at[3], owner_row, owner_col)
    gl_home = pltpu.make_async_copy(glmid_ref, glfin_ref, local_sems.at[1])

    @pl.when(at_home)
    def _():
        gl_home.start()

    @pl.when(jnp.logical_not(at_home))
    def _():
        gl_out.start()

    out_bias = ob_ref[...]
    for k in range(pairs // WIDE):
        pre = nn(wpt_ref[...], prod_ref[:, k * WIDE : (k + 1) * WIDE]).T + out_bias
        for q in range(WIDE // res_local):
            i = k * (WIDE // res_local) + q
            pair_ref[i * res_local : (i + 1) * res_local, :] = (
                pre[q * res_local : (q + 1) * res_local, :] * inverse_divisor(i)
            ).astype(BF16)

    sum_weight(True)
    w_small = w_block // rows
    receive(*gw_row_args)

    def add_w(t, carry):
        return carry + gwr_ref[lax.rem(chip + t, chips)].astype(F32)

    summed = lax.fori_loop(1, chips, add_w, gwx_ref[chip].astype(F32)).astype(BF16)
    for k in range(rows):
        gwc_ref[k] = summed[k * w_small : (k + 1) * w_small, :]
    gw_col_args = ("row", 5, lambda k: gwc_ref.at[k], lambda k: gwcr_ref.at[k], gwcr_ref)
    start(*gw_col_args)

    receive(*gr_args)
    for dm in range(majors):
        part = slice(dm * LANES, (dm + 1) * LANES)
        total_right = grs_ref[my_seqs, part].astype(F32)

        def add_right(t, carry, part=part):
            return carry + grr_ref[lax.rem(r + t, rows), :, part].astype(F32)

        u_ref[dm * seq_local : (dm + 1) * seq_local, :] = lax.fori_loop(1, rows, add_right, total_right)
    for sb in range(chunks):
        pieces = [u_ref[pl.ds(sb * fold + q, majors, stride=seq_local), :] for q in range(fold)]
        for k in range(fold):
            turned = place_groups(pieces, [(q - k) * res_local for q in range(fold)], res_local)
            tr_ref[pl.ds(sb * LANES + hidden + k, majors, stride=fold), :] = turned

    giver = r * factor + lax.rem(c, factor)
    giver_row = c // factor
    giver_col = 2 * lax.rem(giver, chips) + giver // chips
    kept_here = jnp.logical_and(giver_row == r, giver_col == c)

    @pl.when(kept_here)
    def _():
        gl_home.wait()

    @pl.when(jnp.logical_not(kept_here))
    def _():
        remote(glmid_ref, glfin_ref, one_sems.at[2], one_sems.at[3], giver_row, giver_col).wait_recv()

    for im in range(majors):
        piece = glfin_ref[:, im * LANES : (im + 1) * LANES].astype(F32)
        for k in range(fold):
            rolled = pltpu.roll(piece, LANES - k * hidden, 1) if k else piece
            prj_ref[pl.ds(im * fold + k, seq_local, stride=res_local), :] = rolled

    lane = lax.broadcasted_iota(jnp.int32, (LANES, LANES), 1)

    def lower(k, bias_sum):
        here = aligned(k * LANES, LANES)
        projected = jnp.where(lane < hidden, prj_ref[here, :], tr_ref[here, :].T)
        projected = jnp.where(lane < 2 * hidden, projected * live_column(k), 0.0)
        low_ref[here, :] = projected.astype(BF16)
        return bias_sum + jnp.sum(projected, axis=0, keepdims=True)

    bias_sum = lax.fori_loop(0, chunks, lower, jnp.zeros((1, LANES), F32), unroll=min(2 * UNROLL, chunks))
    joined = tn(low_ref[...], both_ref[...])
    grad_w_in = joined[:, :channels]
    low_sum = jnp.sum(low_ref[...].astype(F32), axis=0, keepdims=True)
    turned = w_turned.astype(F32)
    sv_ref[0:1, :] = jnp.sum(joined[:, channels:] * turned, axis=0, keepdims=True)
    sv_ref[1:2, :] = jnp.sum(low_sum.T * turned, axis=0, keepdims=True)
    quarter = 2 * hidden // cols
    for k in range(cols):
        sw_ref[k] = grad_w_in[k * quarter : (k + 1) * quarter, :].astype(BF16)
    sv_ref[2:3, :] = jnp.concatenate([bias_sum, jnp.zeros((1, channels - LANES), F32)], axis=1)
    sv_ref[3:8, :] = jnp.zeros((5, channels), F32)
    sv_row_args = ("col", 7, lambda k: sv_ref, lambda k: svr_ref.at[k], svr_ref)
    start(*sv_row_args)

    def hand_sw(k, carry):
        hand(HAND_SW, sw_ref.at[2 * k + 1 - core], swp_ref.at[k])
        return carry

    lax.fori_loop(0, chips, hand_sw, 0)

    def backward(k, carry):
        here = aligned(k * LANES, LANES)
        scaled = scaled_ref[here, :]
        grad_scaled = nn(low_ref[here, :], w_turned) * gain
        first = jnp.mean(grad_scaled, axis=-1, keepdims=True)
        second = jnp.mean(grad_scaled * scaled, axis=-1, keepdims=True)
        ag_ref[here, :] = (inv_ref[here, :] * (grad_scaled - first - scaled * second)).astype(BF16)
        return carry

    split = chunks // 2
    lax.fori_loop(0, split, backward, 0, unroll=min(UNROLL, split))
    handed(HAND_SW, swp_ref).wait_recv()

    def add_sw(k, carry):
        swx_ref[k] = (sw_ref[2 * k + core].astype(F32) + swp_ref[k].astype(F32)).astype(BF16)
        return carry

    lax.fori_loop(0, chips, add_sw, 0)
    sw_args = ("core", 6, lambda k: swx_ref.at[lax.rem(k, chips)], lambda k: swr_ref.at[k], swr_ref)
    start(*sw_args)
    receive(*gw_col_args)

    def add_w_col(t, carry):
        return carry + gwcr_ref[lax.rem(r + t, rows)].astype(F32)

    gw_ref[c, r] = lax.fori_loop(1, rows, add_w_col, gwc_ref[r].astype(F32)).astype(BF16)
    gw_all_args = (
        "core",
        9,
        lambda k: gw_ref.at[c, r],
        lambda k: gw_ref.at[2 * lax.rem(k, chips) + core, k // chips],
        gw_bulk,
    )
    start(*gw_all_args)

    lax.fori_loop(split, chunks, backward, 0, unroll=min(UNROLL, chunks - split))

    def ordered(received, count):
        def add(t, carry):
            return carry + received[t].astype(F32)

        return lax.fori_loop(1, count, add, received[0].astype(F32))

    svr_ref[c] = sv_ref[...]
    receive(*sv_row_args)
    svc_ref[...] = ordered(svr_ref, cols)
    sv_col_args = ("row", 8, lambda k: svc_ref, lambda k: svcr_ref.at[k], svcr_ref)
    start(*sv_col_args)

    receive(*gw_all_args)

    def hand_out(k, carry):
        slot = gw_ref.at[2 * k + core]
        hand(HAND_OUT, slot, slot)
        return carry

    lax.fori_loop(0, chips, hand_out, 0)
    swr_ref[r * chips + chip] = swx_ref[chip]
    receive(*sw_args)
    swf_ref[...] = ordered(swr_ref, rows * chips)
    gpw_ref[c] = swf_ref[...]
    sw_out_args = ("col", 11, lambda k: swf_ref, lambda k: gpw_ref.at[k], gpw_ref)
    start(*sw_out_args)
    svcr_ref[r] = svc_ref[...]
    receive(*sv_col_args)
    vec_ref[...] = ordered(svcr_ref, rows)
    handed(HAND_OUT, gw_ref.at[pl.ds(0, chips)]).wait_recv()
    for t in range(cols):
        for k in range(rows):
            at = (t * rows + k) * w_small
            owf_ref[at : at + w_small, :] = gw_ref[t, k].astype(F32)
    for k in range(hidden):
        gwf_ref[k * hidden : (k + 1) * hidden, :] = owf_ref[pl.ds(k, hidden, stride=hidden), :]
    receive(*sw_out_args)

    @pl.when(jnp.logical_not(at_home))
    def _():
        gl_out.wait_send()

    @pl.when(jnp.logical_not(left_stays))
    def _():
        left_out.wait_send()

    for i in range(rows // 2):
        for q in range(factor):
            k, near, _ = passed(i, q)

            @pl.when(near)
            def _():
                rest = glr_ref.at[pl.ds(0, chips - 1)]
                remote(rest, rest, left_send.at[k], left_recv.at[k], r, partner).wait_send()

    handed(HAND_LEFT, glp_ref).wait_send()
    handed(HAND_SW, swp_ref).wait_send()
    handed(HAND_GL, glp_ref).wait_send()
    handed(HAND_OUT, gw_ref.at[pl.ds(0, chips)]).wait_send()
    for plane in (HAND_A, HAND_B):
        handed(plane, gwp_ref.at[pl.ds(0, chips // 2)]).wait_send()
    for args in (
        right_args,
        gl_args,
        gr_args,
        gw_row_args,
        gw_col_args,
        sw_args,
        sv_row_args,
        gw_all_args,
        sv_col_args,
        sw_out_args,
    ):
        drain(*args)


def finish_kernel(pair_ref, ag_ref, gw_ref, gpw_ref, vec_ref, pair_hbm, ag_hbm, gain_ref, shift_ref, gpw_out, bias_ref, gw_hbm, sems):
    copies = []

    def send(source, target, parts, part):
        size = source.shape[0] // parts
        here = pl.ds(part * size, size)
        copy = pltpu.make_async_copy(source.at[here, :], target.at[here, :], sems.at[len(copies)])
        copy.start()
        copies.append(copy)

    for part in range(4):
        send(ag_ref, ag_hbm, 4, part)
    for part in range(2):
        send(pair_ref, pair_hbm, 2, part)
    for part in range(4):
        send(gw_ref, gw_hbm, 4, part)
    gain_ref[...] = vec_ref[0:1, :]
    shift_ref[...] = vec_ref[1:2, :]
    bias_ref[...] = vec_ref[2:3, : bias_ref.shape[1]]
    gpw_out[...] = gpw_ref[...]
    for copy in copies:
        copy.wait()


def shards(
    alignment,
    sequence_mask,
    residue_mask,
    layer_norm_gain,
    norm_shift,
    proj_weight,
    proj_bias,
    out_weight,
    out_bias,
    cotangent,
):
    rows = lax.axis_size("row")
    cols = lax.axis_size("col")
    factor = cols // rows
    seq_local, res_local, channels = alignment.shape
    seqs = seq_local * rows
    hidden = proj_weight.shape[1] // 2
    width = out_weight.shape[1]
    tile_rows = res_local * factor
    n = seq_local * res_local
    pairs = tile_rows * res_local
    block = res_local * hidden
    majors = block // LANES
    inner = tile_rows * hidden
    w_block = hidden * hidden // cols
    w_small = w_block // rows
    quarter = 2 * hidden // cols
    dims = (rows, cols, seq_local, res_local, hidden, channels, width)
    vmem = pl.BlockSpec(memory_space=pltpu.VMEM)
    hbm = pl.BlockSpec(memory_space=pltpu.HBM)
    operands = [
        alignment.reshape(n, channels),
        sequence_mask.reshape(1, -1),
        residue_mask.reshape(1, -1),
        layer_norm_gain.reshape(1, -1),
        norm_shift.reshape(1, -1),
        proj_weight.T,
        proj_bias.reshape(1, -1),
        out_weight,
        out_bias.reshape(1, -1),
        cotangent.reshape(pairs, width),
    ]
    operands = [pltpu.with_memory_space_constraint(array, pltpu.HBM) for array in operands]
    pair, grad_alignment, grad_w, grad_pw, vectors = pl.pallas_call(
        functools.partial(fused_kernel, dims),
        out_shape=[
            jax.ShapeDtypeStruct((pairs, width), BF16),
            jax.ShapeDtypeStruct((n, channels), BF16),
            jax.ShapeDtypeStruct((hidden * hidden, width), F32),
            jax.ShapeDtypeStruct((cols, quarter, channels), F32),
            jax.ShapeDtypeStruct((8, channels), F32),
        ],
        in_specs=[hbm] * 10,
        out_specs=[vmem] * 5,
        scratch_shapes=[
            *[pltpu.VMEM(array.shape, array.dtype) for array in operands],
            pltpu.VMEM((n, channels), F32),
            pltpu.VMEM((n, 1), F32),
            pltpu.VMEM((n, 2 * channels), BF16),
            pltpu.VMEM((n, LANES), F32),
            pltpu.VMEM((n, LANES), F32),
            pltpu.VMEM((majors * seq_local, LANES), F32),
            pltpu.VMEM((seq_local, LANES), F32),
            pltpu.VMEM((seq_local, block), BF16),
            pltpu.VMEM((seqs, inner), BF16),
            pltpu.VMEM((inner, seqs), BF16),
            pltpu.VMEM((seqs, block), BF16),
            pltpu.VMEM((hidden * hidden, width), F32),
            pltpu.VMEM((hidden * hidden, width), BF16),
            pltpu.VMEM((width, hidden * hidden), BF16),
            pltpu.VMEM((pairs, width), BF16),
            pltpu.VMEM((inner, block), BF16),
            pltpu.VMEM((hidden * hidden, pairs), BF16),
            pltpu.VMEM((seqs, inner), BF16),
            pltpu.VMEM((cols, seq_local, block), BF16),
            pltpu.VMEM((cols // 2, seq_local, block), BF16),
            pltpu.VMEM((cols // 2, seq_local, block), BF16),
            pltpu.VMEM((seq_local, block), BF16),
            pltpu.VMEM((seq_local, block), BF16),
            pltpu.VMEM((seqs, block), BF16),
            pltpu.VMEM((rows, seq_local, block), BF16),
            pltpu.VMEM((hidden * hidden, width), BF16),
            pltpu.VMEM((cols // 2, w_block, width), BF16),
            pltpu.VMEM((cols // 2, w_block, width), BF16),
            pltpu.VMEM((cols // 2, w_block, width), BF16),
            pltpu.VMEM((rows, w_small, width), BF16),
            pltpu.VMEM((rows, w_small, width), BF16),
            pltpu.VMEM((cols, rows, w_small, width), BF16),
            pltpu.VMEM((n, LANES), BF16),
            pltpu.VMEM((cols, quarter, channels), BF16),
            pltpu.VMEM((cols // 2, quarter, channels), BF16),
            pltpu.VMEM((cols // 2, quarter, channels), BF16),
            pltpu.VMEM((rows * cols // 2, quarter, channels), BF16),
            pltpu.VMEM((quarter, channels), F32),
            pltpu.VMEM((8, channels), F32),
            pltpu.VMEM((cols, 8, channels), F32),
            pltpu.VMEM((8, channels), F32),
            pltpu.VMEM((rows, 8, channels), F32),
            pltpu.SemaphoreType.DMA((12,)),
            pltpu.SemaphoreType.DMA((4,)),
            pltpu.SemaphoreType.DMA((17,)),
            pltpu.SemaphoreType.DMA((17,)),
            pltpu.SemaphoreType.DMA((cols,)),
            pltpu.SemaphoreType.DMA((cols,)),
        ],
        compiler_params=pltpu.CompilerParams(
            collective_id=0, has_side_effects=True, vmem_limit_bytes=48 * 1024 * 1024
        ),
    )(*operands)
    pair, grad_alignment, gain, shift, grad_pw, bias, grad_w = pl.pallas_call(
        finish_kernel,
        out_shape=[
            jax.ShapeDtypeStruct((pairs, width), BF16),
            jax.ShapeDtypeStruct((n, channels), BF16),
            jax.ShapeDtypeStruct((1, channels), F32),
            jax.ShapeDtypeStruct((1, channels), F32),
            jax.ShapeDtypeStruct((2 * hidden, channels), F32),
            jax.ShapeDtypeStruct((1, 2 * hidden), F32),
            jax.ShapeDtypeStruct((hidden * hidden, width), F32),
        ],
        in_specs=[vmem] * 5,
        out_specs=[hbm, hbm, vmem, vmem, vmem, vmem, hbm],
        scratch_shapes=[
            pltpu.SemaphoreType.DMA((10,)),
        ],
        compiler_params=pltpu.CompilerParams(vmem_limit_bytes=16 * 1024 * 1024),
    )(pair, grad_alignment, grad_w, grad_pw.reshape(-1, channels), vectors)
    return (
        pair.reshape(tile_rows, res_local, width),
        grad_alignment.reshape(seq_local, res_local, channels),
        gain.reshape(-1),
        shift.reshape(-1),
        grad_pw.T,
        bias.reshape(-1),
        grad_w,
    )


def solution(mesh):
    return jax.shard_map(
        shards,
        mesh=mesh,
        in_specs=(
            P(("groups", "row"), "col", None),
            P("groups"),
            P("groups"),
            P(),
            P(),
            P(),
            P(),
            P(),
            P(),
            P(("groups", "row"), "col", None),
        ),
        out_specs=(
            P(("groups", "row"), "col", None),
            P(("groups", "row"), "col", None),
            P("groups"),
            P("groups"),
            P("groups", None),
            P("groups"),
            P("groups", None),
        ),
        check_vma=False,
    )
```

```python
import functools

import jax
import jax.numpy as jnp
from jax import lax
from jax.experimental import pallas as pl
from jax.experimental.pallas import tpu as pltpu
from jax.sharding import PartitionSpec as P

EPSILON = 1e-05
LANES = 128
WIDE = 256
UNROLL = 4
MESH = pl.DeviceIdType.MESH
F32 = jnp.float32
BF16 = jnp.bfloat16


def lane_group_swap(blocks, width):
    lane = lax.broadcasted_iota(jnp.int32, blocks[0].shape, 1)
    span = len(blocks) // 2
    while span:
        low = (lane // (width * span)) % 2 == 0
        out = list(blocks)
        for a in range(len(blocks)):
            if a & span:
                continue
            first, second = blocks[a], blocks[a + span]
            shift = width * span
            out[a] = jnp.where(low, first, pltpu.roll(second, shift, 1))
            out[a + span] = jnp.where(low, pltpu.roll(first, LANES - shift, 1), second)
        blocks = out
        span //= 2
    return blocks


def place_groups(pieces, shifts, width):
    group = lax.broadcasted_iota(jnp.int32, pieces[0].shape, 1) // width
    out = None
    for k, (piece, shift) in enumerate(zip(pieces, shifts)):
        rolled = pltpu.roll(piece, shift % LANES, 1) if shift % LANES else piece
        out = rolled if out is None else jnp.where(group == k, rolled, out)
    return out


def nt(a, b):
    return lax.dot_general(a, b, (((1,), (1,)), ((), ())), preferred_element_type=F32)


def tn(a, b):
    return lax.dot_general(a, b, (((0,), (0,)), ((), ())), preferred_element_type=F32)


def nn(a, b):
    return jnp.dot(a, b, preferred_element_type=F32)


def aligned(start, size, step=None):
    return pl.ds(pl.multiple_of(start, step or size), size)


def fused_kernel(dims, *refs):
    rows, cols, seq_local, res_local, hidden, channels, width = dims
    inputs = refs[:10]
    (pair_ref, ag_ref, gwf_ref, gpw_ref, vec_ref) = refs[10:15]
    (
        x_ref,
        seq_ref,
        res_ref,
        gain_ref,
        shift_ref,
        w_ref,
        pb_ref,
        ow_ref,
        ob_ref,
        cot_ref,
        scaled_ref,
        inv_ref,
        both_ref,
        prj_ref,
        tr_ref,
        u_ref,
        seqcol_ref,
        lsend_ref,
        lbuf_ref,
        lt_ref,
        rbuf_ref,
        owf_ref,
        wp_ref,
        wpt_ref,
        gpre_ref,
        gp_ref,
        prod_ref,
        gls_ref,
        glr_ref,
        glp_ref,
        glx_ref,
        glmid_ref,
        glfin_ref,
        grs_ref,
        grr_ref,
        gws_ref,
        gwr_ref,
        gwp_ref,
        gwx_ref,
        gwc_ref,
        gwcr_ref,
        gw_ref,
        low_ref,
        sw_ref,
        swp_ref,
        swx_ref,
        swr_ref,
        swf_ref,
        sv_ref,
        svr_ref,
        svp_ref,
        svc_ref,
        local_sems,
        one_sems,
        send_sems,
        recv_sems,
        left_send,
        left_recv,
    ) = refs[15:]
    r = lax.axis_index("row")
    c = lax.axis_index("col")
    factor = cols // rows
    seqs = seq_local * rows
    tile_rows = res_local * factor
    n = seq_local * res_local
    pairs = tile_rows * res_local
    block = res_local * hidden
    fold = LANES // res_local
    chunks = n // LANES
    majors = block // LANES
    total = rows * cols
    chips = cols // 2
    chip = c // 2
    core = lax.rem(c, 2)
    partner = chip * 2 + 1 - core
    barrier = pltpu.get_barrier_semaphore()

    def greet(t, carry):
        other = lax.rem(r * cols + c + t, total)
        pl.semaphore_signal(
            barrier,
            inc=1,
            device_id={"row": other // cols, "col": lax.rem(other, cols)},
            device_id_type=MESH,
        )
        return carry

    staged = (x_ref, seq_ref, res_ref, gain_ref, shift_ref, w_ref, pb_ref, ow_ref, ob_ref, cot_ref)
    loads = [
        pltpu.make_async_copy(source, target, local_sems.at[2 + k])
        for k, (source, target) in enumerate(zip(inputs, staged))
    ]
    late = (7, 8, 9)
    for load in loads[: late[0]]:
        load.start()
    lax.fori_loop(1, total, greet, 0)
    for k in late:
        loads[k].start()

    def remote(src, dst, send_sem, recv_sem, trow, tcol):
        return pltpu.make_async_remote_copy(
            src_ref=src,
            dst_ref=dst,
            send_sem=send_sem,
            recv_sem=recv_sem,
            device_id={"row": trow, "col": tcol},
            device_id_type=MESH,
        )

    gw_bulk = gws_ref.at[pl.ds(0, (rows * chips - 1) * (hidden * hidden // total)), :]

    def over(kind):
        if kind == "col":
            return cols, c, lambda k: (r, k)
        if kind == "row":
            return rows, r, lambda k: (k, c)
        if kind == "chip":
            return chips, chip, lambda k: (r, 2 * k + core)
        return rows * chips, r * chips + chip, lambda k: (k // chips, 2 * lax.rem(k, chips) + core)

    def send_to(args, k):
        kind, plane, src, dst, bulk = args
        _, me, where = over(kind)
        remote(src(k), dst(me), send_sems.at[plane], recv_sems.at[plane], *where(k)).start()

    def start(*args, first=1, last=None):
        kind = args[0]
        count, me, _ = over(kind)

        def body(t, carry):
            if kind != "row":
                send_to(args, lax.rem(me + t, count))
            else:
                @pl.when(me + t < count)
                def _():
                    send_to(args, lax.rem(me + t, count))

                @pl.when(me >= t)
                def _():
                    send_to(args, lax.rem(me - t + count, count))

            return carry

        lax.fori_loop(first, last or count, body, 0)

    def everything(kind, plane, bulk):
        count, me, where = over(kind)
        part = bulk if bulk is gw_bulk else bulk.at[pl.ds(0, count - 1)]
        return remote(part, part, send_sems.at[plane], recv_sems.at[plane], *where(lax.rem(me + 1, count)))

    def hand(plane, src, dst):
        remote(src, dst, send_sems.at[plane], recv_sems.at[plane], r, partner).start()

    def handed(plane, bulk):
        return remote(bulk, bulk, send_sems.at[plane], recv_sems.at[plane], r, partner)

    def receive(kind, plane, src, dst, bulk):
        everything(kind, plane, bulk).wait_recv()

    def drain(kind, plane, src, dst, bulk):
        everything(kind, plane, bulk).wait_send()

    for k in range(1, 7):
        loads[k].wait()

    def column(mask_ref, count, offset):
        size = mask_ref.shape[1]
        shape = (count, size)
        hit = lax.broadcasted_iota(jnp.int32, shape, 1) == lax.broadcasted_iota(jnp.int32, shape, 0) + offset
        values = jnp.broadcast_to(mask_ref[...].astype(F32), shape)
        return jnp.sum(jnp.where(hit, values, 0.0), axis=1, keepdims=True)

    seqcol_ref[...] = jnp.broadcast_to(column(seq_ref, seq_local, r * seq_local), seqcol_ref.shape)
    rescol = column(res_ref, res_local, c * res_local)
    tilecol = column(res_ref, tile_rows, r * tile_rows)
    kept = jnp.sum(seq_ref[...].astype(F32), axis=1, keepdims=True)

    def live_column(k):
        parts = []
        for q in range(fold):
            parts.append(rescol * seqcol_ref[pl.ds(k * fold + q, 1), 0:1])
        return jnp.concatenate(parts, axis=0)

    w = w_ref[...].astype(F32)
    w = jnp.concatenate([w, jnp.zeros((LANES - 2 * hidden, channels), F32)], axis=0)
    w_wide = w.T.astype(BF16)
    w_turned = w.astype(BF16)
    bias = pb_ref[...]
    bias = jnp.concatenate([bias, jnp.zeros((1, LANES - 2 * hidden), F32)], axis=1)
    gain = gain_ref[...]
    shift = shift_ref[...]

    loads[0].wait()

    def layer_norm(k, carry):
        here = aligned(k * LANES, LANES)
        widened = x_ref[here, :].astype(F32)
        centred = widened - jnp.mean(widened, axis=-1, keepdims=True)
        inverse = lax.rsqrt(jnp.mean(centred * centred, axis=-1, keepdims=True) + EPSILON)
        scaled = centred * inverse
        normed = (scaled * gain + shift).astype(BF16)
        scaled_ref[here, :] = scaled
        inv_ref[here, :] = inverse
        both_ref[here, :channels] = normed
        both_ref[here, channels:] = scaled.astype(BF16)
        prj = (nn(normed, w_wide) + bias) * live_column(k)
        prj_ref[here, :] = prj
        tr_ref[here, :] = prj.T
        return carry

    lax.fori_loop(0, chunks, layer_norm, 0, unroll=min(2 * UNROLL, chunks))

    for im in range(majors):
        pieces = [prj_ref[pl.ds(im * fold + k, seq_local, stride=res_local), :] for k in range(fold)]
        left = place_groups(pieces, [k * hidden for k in range(fold)], hidden)
        lsend_ref[:, im * LANES : (im + 1) * LANES] = left.astype(BF16)
    for sb in range(chunks):
        pieces = [
            tr_ref[pl.ds(sb * LANES + hidden + k, majors, stride=fold), :] for k in range(fold)
        ]
        for q in range(fold):
            turned = place_groups(pieces, [(k - q) * res_local for k in range(fold)], res_local)
            u_ref[pl.ds(sb * fold + q, majors, stride=seq_local), :] = turned
    my_seqs = aligned(r * seq_local, seq_local)
    for dm in range(majors):
        rbuf_ref[my_seqs, dm * LANES : (dm + 1) * LANES] = u_ref[
            dm * seq_local : (dm + 1) * seq_local, :
        ].astype(BF16)

    pl.semaphore_wait(barrier, total - 1)

    def left_slot(k):
        return lbuf_ref.at[aligned((k // factor) * seq_local, seq_local), aligned(lax.rem(k, factor) * block, block)]

    relay_row = c // factor
    relay_col = r * factor + lax.rem(c, factor)
    left_col = chip * 2 + lax.rem(r, 2)
    left_stays = jnp.logical_and(relay_row == r, left_col == c)
    left_out = remote(
        lsend_ref, left_slot(relay_col), one_sems.at[0], left_recv.at[relay_col], relay_row, left_col
    )
    left_home = pltpu.make_async_copy(lsend_ref, left_slot(relay_col), local_sems.at[0])

    @pl.when(left_stays)
    def _():
        left_home.start()

    @pl.when(jnp.logical_not(left_stays))
    def _():
        left_out.start()

    HAND_GL, HAND_A, HAND_B, HAND_LEFT, HAND_OUT, HAND_SW, HAND_SV = 12, 13, 14, 15, 1, 10, 7

    def passed(i, q):
        begin = jnp.minimum((r + 1 - core) // 2, rows // 2 - 1)
        row = 2 * lax.rem(begin + i, rows // 2) + core
        near = (r * factor + q) // 2 == chip
        return row * factor + q, near, jnp.logical_and(row == r, r * factor + q == c)

    def pass_left(i):
        for q in range(factor):
            k, near, own = passed(i, q)
            slot = left_slot(k)

            @pl.when(own)
            def _():
                left_home.wait()

            @pl.when(jnp.logical_not(own))
            def _():
                remote(slot, slot, one_sems.at[0], left_recv.at[k], r, partner).wait_recv()

            @pl.when(near)
            def _():
                def body(t, carry):
                    other = lax.rem(chip + t, chips)
                    remote(slot, slot, left_send.at[k], left_recv.at[k], r, 2 * other + core).start()
                    return carry

                lax.fori_loop(1, chips, body, 0)

            hand(HAND_LEFT, slot, slot)

    def right_block(k):
        return rbuf_ref.at[aligned(k * seq_local, seq_local), :]

    right_args = ("row", 0, lambda k: right_block(r), right_block, grr_ref)

    start(*right_args, last=2)
    for k in late:
        loads[k].wait()
    owf_ref[...] = ow_ref[...].astype(F32)
    for d in range(hidden):
        wp_ref[d * hidden : (d + 1) * hidden, :] = owf_ref[pl.ds(d, hidden, stride=hidden), :].astype(BF16)

    def inverse_divisor(i):
        return 1.0 / jnp.maximum(kept * tilecol[i : i + 1, :] * rescol, 1.0)

    for i in range(tile_rows):
        here = slice(i * res_local, (i + 1) * res_local)
        gpre_ref[here, :] = (cot_ref[here, :].astype(F32) * inverse_divisor(i)).astype(BF16)

    half = WIDE // LANES

    def grad_products(ip, carry):
        upstream = gpre_ref[aligned(ip * WIDE, WIDE), :]
        for dm in range(majors):
            tile = nt(wp_ref[dm * LANES : (dm + 1) * LANES, :], upstream)
            for h in range(half):
                blocks = [
                    tile[a * hidden : (a + 1) * hidden, h * LANES : (h + 1) * LANES] for a in range(fold)
                ]
                for a, swapped in enumerate(lane_group_swap(blocks, res_local)):
                    gp_ref[
                        aligned(((ip * half + h) * fold + a) * hidden, hidden), dm * LANES : (dm + 1) * LANES
                    ] = swapped.astype(BF16)
        return carry

    steps = pairs // WIDE
    lax.fori_loop(0, steps // 2, grad_products, 0)
    start(*right_args, first=2)
    pass_left(0)
    lax.fori_loop(steps // 2, steps, grad_products, 0)

    for i in range(1, rows // 2):
        pass_left(i)
    handed(HAND_LEFT, glp_ref).wait_recv()
    for k in range(block // WIDE):
        grs_ref[:, k * WIDE : (k + 1) * WIDE] = nn(lbuf_ref[...], gp_ref[:, k * WIDE : (k + 1) * WIDE]).astype(BF16)
    gr_args = (
        "row",
        3,
        lambda k: grs_ref.at[aligned(k * seq_local, seq_local), :],
        lambda k: grr_ref.at[k],
        grr_ref,
    )
    for im in range(tile_rows * hidden // LANES):
        lt_ref[im * LANES : (im + 1) * LANES, :] = lbuf_ref[:, im * LANES : (im + 1) * LANES].T
    for k in range(hidden * hidden // LANES):
        wpt_ref[:, k * LANES : (k + 1) * LANES] = wp_ref[k * LANES : (k + 1) * LANES, :].T
    receive(*right_args)
    start(*gr_args)

    def gl_part(k):
        return gls_ref.at[aligned((k // factor) * seq_local, seq_local), aligned(lax.rem(k, factor) * block, block)]

    for k in range(tile_rows * hidden // WIDE):
        gls_ref[:, k * WIDE : (k + 1) * WIDE] = nt(rbuf_ref[...], gp_ref[k * WIDE : (k + 1) * WIDE, :]).astype(BF16)

    def hand_left(k, carry):
        hand(HAND_GL, gl_part((1 - core) * chips + k), glp_ref.at[k])
        return carry

    lax.fori_loop(0, chips, hand_left, 0)
    gl_args = ("chip", 2, lambda k: glx_ref.at[k], lambda k: glr_ref.at[k], glr_ref)

    def sum_left():
        handed(HAND_GL, glp_ref).wait_recv()

        def add(k, carry):
            t = core * chips + k
            mine = gls_ref[aligned((t // factor) * seq_local, seq_local), aligned(lax.rem(t, factor) * block, block)]
            glx_ref[k] = (mine.astype(F32) + glp_ref[k].astype(F32)).astype(BF16)
            return carry

        lax.fori_loop(0, chips, add, 0)
        start(*gl_args)


    w_block = hidden * hidden // cols
    gw_row_args = ("chip", 4, lambda k: gwx_ref.at[k], lambda k: gwr_ref.at[k], gwr_ref)
    strips = hidden * hidden // WIDE
    per = WIDE // w_block
    first = lax.rem((chip + 1) * 2 * w_block // WIDE, strips)

    def sum_weight(later):
        plane = HAND_B if later else HAND_A
        some = chips // 2
        offset = some if later else 0
        handed(plane, gwp_ref.at[pl.ds(0, some)]).wait_recv()

        def add(k, carry):
            k = lax.rem(first * per // 2 + offset + k, chips)
            t = 2 * k + core
            mine = gws_ref[aligned(t * w_block, w_block), :]
            gwx_ref[k] = (mine.astype(F32) + gwp_ref[k].astype(F32)).astype(BF16)

            @pl.when(k != chip)
            def _():
                send_to(gw_row_args, k)

            return carry

        lax.fori_loop(0, some, add, 0)

    for k in range(strips):
        strip = lax.rem(first + k, strips)
        right = rbuf_ref[:, aligned(strip * WIDE, WIDE)]

        def products(im, carry, strip=strip, right=right):
            tile = nn(lt_ref[aligned(im * LANES, LANES), :], right)
            for h in range(half):
                blocks = [
                    tile[a * hidden : (a + 1) * hidden, h * LANES : (h + 1) * LANES] for a in range(fold)
                ]
                for a, swapped in enumerate(lane_group_swap(blocks, res_local)):
                    at = strip * WIDE + (h * fold + a) * hidden
                    prod_ref[aligned(at, hidden), aligned(im * LANES, LANES)] = swapped.astype(BF16)
            return carry

        lax.fori_loop(0, tile_rows // fold, products, 0, unroll=8)
        here = aligned(strip * WIDE, WIDE)
        gws_ref[here, :] = nn(prod_ref[here, :], gpre_ref[...]).astype(BF16)
        for j in range(per):
            target = strip * per + j

            @pl.when(lax.rem(target, 2) != core)
            def _(target=target, k=k):
                hand(
                    HAND_A if k < strips // 2 else HAND_B,
                    gws_ref.at[aligned(target * w_block, w_block), :],
                    gwp_ref.at[target // 2],
                )

        if k == 0:
            sum_left()
        if k == strips // 2:
            sum_weight(False)

    receive(*gl_args)

    def add_left(t, carry):
        return carry + glr_ref[lax.rem(chip + t, chips)].astype(F32)

    glmid_ref[...] = lax.fori_loop(1, chips, add_left, glx_ref[chip].astype(F32)).astype(BF16)
    gathered = core * chips + chip
    owner_row = gathered // factor
    owner_col = r * factor + lax.rem(gathered, factor)
    at_home = jnp.logical_and(owner_row == r, owner_col == c)
    gl_out = remote(glmid_ref, glfin_ref, one_sems.at[2], one_sems.at[3], owner_row, owner_col)
    gl_home = pltpu.make_async_copy(glmid_ref, glfin_ref, local_sems.at[1])

    @pl.when(at_home)
    def _():
        gl_home.start()

    @pl.when(jnp.logical_not(at_home))
    def _():
        gl_out.start()

    out_bias = ob_ref[...]
    for k in range(pairs // WIDE):
        pre = nn(wpt_ref[...], prod_ref[:, k * WIDE : (k + 1) * WIDE]).T + out_bias
        for q in range(WIDE // res_local):
            i = k * (WIDE // res_local) + q
            pair_ref[i * res_local : (i + 1) * res_local, :] = (
                pre[q * res_local : (q + 1) * res_local, :] * inverse_divisor(i)
            ).astype(BF16)

    sum_weight(True)
    w_small = w_block // rows
    receive(*gw_row_args)

    def add_w(t, carry):
        return carry + gwr_ref[lax.rem(chip + t, chips)].astype(F32)

    summed = lax.fori_loop(1, chips, add_w, gwx_ref[chip].astype(F32)).astype(BF16)
    for k in range(rows):
        gwc_ref[k] = summed[k * w_small : (k + 1) * w_small, :]
    gw_col_args = ("row", 5, lambda k: gwc_ref.at[k], lambda k: gwcr_ref.at[k], gwcr_ref)
    start(*gw_col_args)

    receive(*gr_args)
    for dm in range(majors):
        part = slice(dm * LANES, (dm + 1) * LANES)
        total_right = grs_ref[my_seqs, part].astype(F32)

        def add_right(t, carry, part=part):
            return carry + grr_ref[lax.rem(r + t, rows), :, part].astype(F32)

        u_ref[dm * seq_local : (dm + 1) * seq_local, :] = lax.fori_loop(1, rows, add_right, total_right)
    for sb in range(chunks):
        pieces = [u_ref[pl.ds(sb * fold + q, majors, stride=seq_local), :] for q in range(fold)]
        for k in range(fold):
            turned = place_groups(pieces, [(q - k) * res_local for q in range(fold)], res_local)
            tr_ref[pl.ds(sb * LANES + hidden + k, majors, stride=fold), :] = turned

    giver = r * factor + lax.rem(c, factor)
    giver_row = c // factor
    giver_col = 2 * lax.rem(giver, chips) + giver // chips
    kept_here = jnp.logical_and(giver_row == r, giver_col == c)

    @pl.when(kept_here)
    def _():
        gl_home.wait()

    @pl.when(jnp.logical_not(kept_here))
    def _():
        remote(glmid_ref, glfin_ref, one_sems.at[2], one_sems.at[3], giver_row, giver_col).wait_recv()

    for im in range(majors):
        piece = glfin_ref[:, im * LANES : (im + 1) * LANES].astype(F32)
        for k in range(fold):
            rolled = pltpu.roll(piece, LANES - k * hidden, 1) if k else piece
            prj_ref[pl.ds(im * fold + k, seq_local, stride=res_local), :] = rolled

    lane = lax.broadcasted_iota(jnp.int32, (LANES, LANES), 1)

    def lower(k, bias_sum):
        here = aligned(k * LANES, LANES)
        projected = jnp.where(lane < hidden, prj_ref[here, :], tr_ref[here, :].T)
        projected = jnp.where(lane < 2 * hidden, projected * live_column(k), 0.0)
        low_ref[here, :] = projected.astype(BF16)
        return bias_sum + jnp.sum(projected, axis=0, keepdims=True)

    bias_sum = lax.fori_loop(0, chunks, lower, jnp.zeros((1, LANES), F32), unroll=min(2 * UNROLL, chunks))
    joined = tn(low_ref[...], both_ref[...])
    grad_w_in = joined[:, :channels]
    low_sum = jnp.sum(low_ref[...].astype(F32), axis=0, keepdims=True)
    turned = w_turned.astype(F32)
    gain_sum = jnp.sum(joined[:, channels:] * turned, axis=0, keepdims=True)
    shift_sum = jnp.sum(low_sum.T * turned, axis=0, keepdims=True)
    parts = channels // LANES
    sv_ref[...] = jnp.zeros(sv_ref.shape, F32)
    for k in range(parts):
        sv_ref[k : k + 1, :] = gain_sum[:, k * LANES : (k + 1) * LANES]
        sv_ref[parts + k : parts + k + 1, :] = shift_sum[:, k * LANES : (k + 1) * LANES]
    sv_ref[2 * parts : 2 * parts + 1, :] = bias_sum
    quarter = 2 * hidden // cols
    for k in range(cols):
        sw_ref[k] = grad_w_in[k * quarter : (k + 1) * quarter, :].astype(BF16)
    hand(HAND_SV, sv_ref, svp_ref.at[0])

    def hand_sw(k, carry):
        hand(HAND_SW, sw_ref.at[2 * k + 1 - core], swp_ref.at[k])
        return carry

    lax.fori_loop(0, chips, hand_sw, 0)

    def backward(k, carry):
        here = aligned(k * LANES, LANES)
        scaled = scaled_ref[here, :]
        grad_scaled = nn(low_ref[here, :], w_turned) * gain
        first = jnp.mean(grad_scaled, axis=-1, keepdims=True)
        second = jnp.mean(grad_scaled * scaled, axis=-1, keepdims=True)
        ag_ref[here, :] = (inv_ref[here, :] * (grad_scaled - first - scaled * second)).astype(BF16)
        return carry

    split = chunks // 2
    lax.fori_loop(0, split, backward, 0, unroll=min(UNROLL, split))
    handed(HAND_SW, swp_ref).wait_recv()

    def add_sw(k, carry):
        swx_ref[k] = (sw_ref[2 * k + core].astype(F32) + swp_ref[k].astype(F32)).astype(BF16)
        return carry

    lax.fori_loop(0, chips, add_sw, 0)
    sw_args = ("core", 6, lambda k: swx_ref.at[lax.rem(k, chips)], lambda k: swr_ref.at[k], swr_ref)
    start(*sw_args)
    handed(HAND_SV, svp_ref).wait_recv()
    svc_ref[...] = sv_ref[...] + svp_ref[0]
    sv_args = ("core", 8, lambda k: svc_ref, lambda k: svr_ref.at[k], svr_ref)
    start(*sv_args)
    receive(*gw_col_args)

    def add_w_col(t, carry):
        return carry + gwcr_ref[lax.rem(r + t, rows)].astype(F32)

    gw_ref[c, r] = lax.fori_loop(1, rows, add_w_col, gwc_ref[r].astype(F32)).astype(BF16)
    gw_all_args = (
        "core",
        9,
        lambda k: gw_ref.at[c, r],
        lambda k: gw_ref.at[2 * lax.rem(k, chips) + core, k // chips],
        gw_bulk,
    )
    start(*gw_all_args)

    lax.fori_loop(split, chunks, backward, 0, unroll=min(UNROLL, chunks - split))

    def ordered(received, count):
        def add(t, carry):
            return carry + received[t].astype(F32)

        return lax.fori_loop(1, count, add, received[0].astype(F32))

    swr_ref[r * chips + chip] = swx_ref[chip]
    receive(*sw_args)
    swf_ref[...] = ordered(swr_ref, rows * chips)
    gpw_ref[c] = swf_ref[...]
    sw_out_args = ("col", 11, lambda k: swf_ref, lambda k: gpw_ref.at[k], gpw_ref)
    start(*sw_out_args)
    receive(*gw_all_args)

    def hand_out(k, carry):
        slot = gw_ref.at[2 * k + core]
        hand(HAND_OUT, slot, slot)
        return carry

    lax.fori_loop(0, chips, hand_out, 0)
    svr_ref[r * chips + chip] = svc_ref[...]
    receive(*sv_args)
    vec_ref[...] = ordered(svr_ref, rows * chips)
    handed(HAND_OUT, gw_ref.at[pl.ds(0, chips)]).wait_recv()
    for t in range(cols):
        for k in range(rows):
            at = (t * rows + k) * w_small
            owf_ref[at : at + w_small, :] = gw_ref[t, k].astype(F32)
    for k in range(hidden):
        gwf_ref[k * hidden : (k + 1) * hidden, :] = owf_ref[pl.ds(k, hidden, stride=hidden), :]
    receive(*sw_out_args)

    @pl.when(jnp.logical_not(at_home))
    def _():
        gl_out.wait_send()

    @pl.when(jnp.logical_not(left_stays))
    def _():
        left_out.wait_send()

    for i in range(rows // 2):
        for q in range(factor):
            k, near, _ = passed(i, q)

            @pl.when(near)
            def _():
                rest = glr_ref.at[pl.ds(0, chips - 1)]
                remote(rest, rest, left_send.at[k], left_recv.at[k], r, partner).wait_send()

    handed(HAND_LEFT, glp_ref).wait_send()
    handed(HAND_SW, swp_ref).wait_send()
    handed(HAND_SV, svp_ref).wait_send()
    handed(HAND_GL, glp_ref).wait_send()
    handed(HAND_OUT, gw_ref.at[pl.ds(0, chips)]).wait_send()
    for plane in (HAND_A, HAND_B):
        handed(plane, gwp_ref.at[pl.ds(0, chips // 2)]).wait_send()
    for args in (
        right_args,
        gl_args,
        gr_args,
        gw_row_args,
        gw_col_args,
        sw_args,
        sv_args,
        gw_all_args,
        sw_out_args,
    ):
        drain(*args)


def finish_kernel(*refs):
    pair_ref, ag_ref, gw_ref, gpw_ref, vec_ref = refs[:5]
    pair_hbm, ag_hbm, gain_hbm, shift_hbm, gpw_hbm, bias_hbm, gw_hbm = refs[5:12]
    gain_ref, shift_ref, bias_ref, sems = refs[12:]
    copies = []

    def send(source, target):
        copy = pltpu.make_async_copy(source, target, sems.at[len(copies)])
        copy.start()
        copies.append(copy)

    send(gw_ref, gw_hbm)
    send(ag_ref, ag_hbm)
    send(pair_ref, pair_hbm)
    send(gpw_ref, gpw_hbm)
    parts = gain_ref.shape[1] // LANES
    for k in range(parts):
        gain_ref[:, k * LANES : (k + 1) * LANES] = vec_ref[k : k + 1, :]
        shift_ref[:, k * LANES : (k + 1) * LANES] = vec_ref[parts + k : parts + k + 1, :]
    bias_ref[...] = vec_ref[2 * parts : 2 * parts + 1, : bias_ref.shape[1]]
    send(gain_ref, gain_hbm)
    send(shift_ref, shift_hbm)
    send(bias_ref, bias_hbm)
    for copy in copies:
        copy.wait()


def shards(
    alignment,
    sequence_mask,
    residue_mask,
    layer_norm_gain,
    norm_shift,
    proj_weight,
    proj_bias,
    out_weight,
    out_bias,
    cotangent,
):
    rows = lax.axis_size("row")
    cols = lax.axis_size("col")
    factor = cols // rows
    seq_local, res_local, channels = alignment.shape
    seqs = seq_local * rows
    hidden = proj_weight.shape[1] // 2
    width = out_weight.shape[1]
    tile_rows = res_local * factor
    n = seq_local * res_local
    pairs = tile_rows * res_local
    block = res_local * hidden
    majors = block // LANES
    inner = tile_rows * hidden
    w_block = hidden * hidden // cols
    w_small = w_block // rows
    quarter = 2 * hidden // cols
    dims = (rows, cols, seq_local, res_local, hidden, channels, width)
    vmem = pl.BlockSpec(memory_space=pltpu.VMEM)
    hbm = pl.BlockSpec(memory_space=pltpu.HBM)
    operands = [
        alignment.reshape(n, channels),
        sequence_mask.reshape(1, -1),
        residue_mask.reshape(1, -1),
        layer_norm_gain.reshape(1, -1),
        norm_shift.reshape(1, -1),
        proj_weight.T,
        proj_bias.reshape(1, -1),
        out_weight,
        out_bias.reshape(1, -1),
        cotangent.reshape(pairs, width),
    ]
    operands = [pltpu.with_memory_space_constraint(array, pltpu.HBM) for array in operands]
    pair, grad_alignment, grad_w, grad_pw, vectors = pl.pallas_call(
        functools.partial(fused_kernel, dims),
        out_shape=[
            jax.ShapeDtypeStruct((pairs, width), BF16),
            jax.ShapeDtypeStruct((n, channels), BF16),
            jax.ShapeDtypeStruct((hidden * hidden, width), F32),
            jax.ShapeDtypeStruct((cols, quarter, channels), F32),
            jax.ShapeDtypeStruct((8, LANES), F32),
        ],
        in_specs=[hbm] * 10,
        out_specs=[vmem] * 5,
        scratch_shapes=[
            *[pltpu.VMEM(array.shape, array.dtype) for array in operands],
            pltpu.VMEM((n, channels), F32),
            pltpu.VMEM((n, 1), F32),
            pltpu.VMEM((n, 2 * channels), BF16),
            pltpu.VMEM((n, LANES), F32),
            pltpu.VMEM((n, LANES), F32),
            pltpu.VMEM((majors * seq_local, LANES), F32),
            pltpu.VMEM((seq_local, LANES), F32),
            pltpu.VMEM((seq_local, block), BF16),
            pltpu.VMEM((seqs, inner), BF16),
            pltpu.VMEM((inner, seqs), BF16),
            pltpu.VMEM((seqs, block), BF16),
            pltpu.VMEM((hidden * hidden, width), F32),
            pltpu.VMEM((hidden * hidden, width), BF16),
            pltpu.VMEM((width, hidden * hidden), BF16),
            pltpu.VMEM((pairs, width), BF16),
            pltpu.VMEM((inner, block), BF16),
            pltpu.VMEM((hidden * hidden, pairs), BF16),
            pltpu.VMEM((seqs, inner), BF16),
            pltpu.VMEM((cols, seq_local, block), BF16),
            pltpu.VMEM((cols // 2, seq_local, block), BF16),
            pltpu.VMEM((cols // 2, seq_local, block), BF16),
            pltpu.VMEM((seq_local, block), BF16),
            pltpu.VMEM((seq_local, block), BF16),
            pltpu.VMEM((seqs, block), BF16),
            pltpu.VMEM((rows, seq_local, block), BF16),
            pltpu.VMEM((hidden * hidden, width), BF16),
            pltpu.VMEM((cols // 2, w_block, width), BF16),
            pltpu.VMEM((cols // 2, w_block, width), BF16),
            pltpu.VMEM((cols // 2, w_block, width), BF16),
            pltpu.VMEM((rows, w_small, width), BF16),
            pltpu.VMEM((rows, w_small, width), BF16),
            pltpu.VMEM((cols, rows, w_small, width), BF16),
            pltpu.VMEM((n, LANES), BF16),
            pltpu.VMEM((cols, quarter, channels), BF16),
            pltpu.VMEM((cols // 2, quarter, channels), BF16),
            pltpu.VMEM((cols // 2, quarter, channels), BF16),
            pltpu.VMEM((rows * cols // 2, quarter, channels), BF16),
            pltpu.VMEM((quarter, channels), F32),
            pltpu.VMEM((8, LANES), F32),
            pltpu.VMEM((rows * cols // 2, 8, LANES), F32),
            pltpu.VMEM((1, 8, LANES), F32),
            pltpu.VMEM((8, LANES), F32),
            pltpu.SemaphoreType.DMA((12,)),
            pltpu.SemaphoreType.DMA((4,)),
            pltpu.SemaphoreType.DMA((16,)),
            pltpu.SemaphoreType.DMA((16,)),
            pltpu.SemaphoreType.DMA((cols,)),
            pltpu.SemaphoreType.DMA((cols,)),
        ],
        compiler_params=pltpu.CompilerParams(
            collective_id=0, has_side_effects=True, vmem_limit_bytes=48 * 1024 * 1024
        ),
    )(*operands)
    pair, grad_alignment, gain, shift, grad_pw, bias, grad_w = pl.pallas_call(
        finish_kernel,
        out_shape=[
            jax.ShapeDtypeStruct((pairs, width), BF16),
            jax.ShapeDtypeStruct((n, channels), BF16),
            jax.ShapeDtypeStruct((1, channels), F32),
            jax.ShapeDtypeStruct((1, channels), F32),
            jax.ShapeDtypeStruct((2 * hidden, channels), F32),
            jax.ShapeDtypeStruct((1, 2 * hidden), F32),
            jax.ShapeDtypeStruct((hidden * hidden, width), F32),
        ],
        in_specs=[vmem] * 5,
        out_specs=[hbm] * 7,
        scratch_shapes=[
            pltpu.VMEM((1, channels), F32),
            pltpu.VMEM((1, channels), F32),
            pltpu.VMEM((1, 2 * hidden), F32),
            pltpu.SemaphoreType.DMA((7,)),
        ],
        compiler_params=pltpu.CompilerParams(vmem_limit_bytes=16 * 1024 * 1024),
    )(pair, grad_alignment, grad_w, grad_pw.reshape(-1, channels), vectors)
    return (
        pair.reshape(tile_rows, res_local, width),
        grad_alignment.reshape(seq_local, res_local, channels),
        gain.reshape(-1),
        shift.reshape(-1),
        grad_pw.T,
        bias.reshape(-1),
        grad_w,
    )


def solution(mesh):
    return jax.shard_map(
        shards,
        mesh=mesh,
        in_specs=(
            P(("groups", "row"), "col", None),
            P("groups"),
            P("groups"),
            P(),
            P(),
            P(),
            P(),
            P(),
            P(),
            P(("groups", "row"), "col", None),
        ),
        out_specs=(
            P(("groups", "row"), "col", None),
            P(("groups", "row"), "col", None),
            P("groups"),
            P("groups"),
            P("groups", None),
            P("groups"),
            P("groups", None),
        ),
        check_vma=False,
    )
```

```python
import functools

import jax
import jax.numpy as jnp
from jax import lax
from jax.experimental import pallas as pl
from jax.experimental.pallas import tpu as pltpu
from jax.sharding import PartitionSpec as P

EPSILON = 1e-05
LANES = 128
WIDE = 256
UNROLL = 4
MESH = pl.DeviceIdType.MESH
F32 = jnp.float32
BF16 = jnp.bfloat16


def lane_group_swap(blocks, width):
    lane = lax.broadcasted_iota(jnp.int32, blocks[0].shape, 1)
    span = len(blocks) // 2
    while span:
        low = (lane // (width * span)) % 2 == 0
        out = list(blocks)
        for a in range(len(blocks)):
            if a & span:
                continue
            first, second = blocks[a], blocks[a + span]
            shift = width * span
            out[a] = jnp.where(low, first, pltpu.roll(second, shift, 1))
            out[a + span] = jnp.where(low, pltpu.roll(first, LANES - shift, 1), second)
        blocks = out
        span //= 2
    return blocks


def place_groups(pieces, shifts, width):
    group = lax.broadcasted_iota(jnp.int32, pieces[0].shape, 1) // width
    out = None
    for k, (piece, shift) in enumerate(zip(pieces, shifts)):
        rolled = pltpu.roll(piece, shift % LANES, 1) if shift % LANES else piece
        out = rolled if out is None else jnp.where(group == k, rolled, out)
    return out


def nt(a, b):
    return lax.dot_general(a, b, (((1,), (1,)), ((), ())), preferred_element_type=F32)


def tn(a, b):
    return lax.dot_general(a, b, (((0,), (0,)), ((), ())), preferred_element_type=F32)


def nn(a, b):
    return jnp.dot(a, b, preferred_element_type=F32)


def aligned(start, size, step=None):
    return pl.ds(pl.multiple_of(start, step or size), size)


def fused_kernel(dims, *refs):
    rows, cols, seq_local, res_local, hidden, channels, width = dims
    inputs = refs[:10]
    (pair_ref, ag_ref, gwf_ref, gpw_ref, vec_ref) = refs[10:15]
    (
        x_ref,
        seq_ref,
        res_ref,
        gain_ref,
        shift_ref,
        w_ref,
        pb_ref,
        ow_ref,
        ob_ref,
        cot_ref,
        scaled_ref,
        inv_ref,
        both_ref,
        prj_ref,
        tr_ref,
        u_ref,
        seqcol_ref,
        lsend_ref,
        lbuf_ref,
        lt_ref,
        rbuf_ref,
        owf_ref,
        wp_ref,
        wpt_ref,
        gpre_ref,
        gp_ref,
        prod_ref,
        gls_ref,
        glr_ref,
        glp_ref,
        glx_ref,
        glmid_ref,
        glfin_ref,
        grs_ref,
        grr_ref,
        gws_ref,
        gwr_ref,
        gwp_ref,
        gwx_ref,
        gwc_ref,
        gwcr_ref,
        gw_ref,
        low_ref,
        sw_ref,
        swp_ref,
        swx_ref,
        swr_ref,
        swf_ref,
        sv_ref,
        svr_ref,
        svp_ref,
        svc_ref,
        local_sems,
        one_sems,
        send_sems,
        recv_sems,
        left_send,
        left_recv,
    ) = refs[15:]
    r = lax.axis_index("row")
    c = lax.axis_index("col")
    factor = cols // rows
    seqs = seq_local * rows
    tile_rows = res_local * factor
    n = seq_local * res_local
    pairs = tile_rows * res_local
    block = res_local * hidden
    fold = LANES // res_local
    chunks = n // LANES
    majors = block // LANES
    total = rows * cols
    chips = cols // 2
    chip = c // 2
    core = lax.rem(c, 2)
    partner = chip * 2 + 1 - core
    barrier = pltpu.get_barrier_semaphore()

    def greet(t, carry):
        other = lax.rem(r * cols + c + t, total)
        pl.semaphore_signal(
            barrier,
            inc=1,
            device_id={"row": other // cols, "col": lax.rem(other, cols)},
            device_id_type=MESH,
        )
        return carry

    staged = (x_ref, seq_ref, res_ref, gain_ref, shift_ref, w_ref, pb_ref, ow_ref, ob_ref, cot_ref)
    loads = [
        pltpu.make_async_copy(source, target, local_sems.at[2 + k])
        for k, (source, target) in enumerate(zip(inputs, staged))
    ]
    late = (7, 8, 9)
    for load in loads[: late[0]]:
        load.start()
    lax.fori_loop(1, total, greet, 0)
    for k in late:
        loads[k].start()

    def remote(src, dst, send_sem, recv_sem, trow, tcol):
        return pltpu.make_async_remote_copy(
            src_ref=src,
            dst_ref=dst,
            send_sem=send_sem,
            recv_sem=recv_sem,
            device_id={"row": trow, "col": tcol},
            device_id_type=MESH,
        )

    gw_bulk = gws_ref.at[pl.ds(0, (rows * chips - 1) * (hidden * hidden // total)), :]

    def over(kind):
        if kind == "col":
            return cols, c, lambda k: (r, k)
        if kind == "row":
            return rows, r, lambda k: (k, c)
        if kind == "chip":
            return chips, chip, lambda k: (r, 2 * k + core)
        return rows * chips, r * chips + chip, lambda k: (k // chips, 2 * lax.rem(k, chips) + core)

    def send_to(args, k):
        kind, plane, src, dst, bulk = args
        _, me, where = over(kind)
        remote(src(k), dst(me), send_sems.at[plane], recv_sems.at[plane], *where(k)).start()

    def start(*args, first=1, last=None):
        kind = args[0]
        count, me, _ = over(kind)

        def body(t, carry):
            if kind != "row":
                send_to(args, lax.rem(me + t, count))
            else:
                @pl.when(me + t < count)
                def _():
                    send_to(args, lax.rem(me + t, count))

                @pl.when(me >= t)
                def _():
                    send_to(args, lax.rem(me - t + count, count))

            return carry

        lax.fori_loop(first, last or count, body, 0)

    def everything(kind, plane, bulk):
        count, me, where = over(kind)
        part = bulk if bulk is gw_bulk else bulk.at[pl.ds(0, count - 1)]
        return remote(part, part, send_sems.at[plane], recv_sems.at[plane], *where(lax.rem(me + 1, count)))

    def hand(plane, src, dst):
        remote(src, dst, send_sems.at[plane], recv_sems.at[plane], r, partner).start()

    def handed(plane, bulk):
        return remote(bulk, bulk, send_sems.at[plane], recv_sems.at[plane], r, partner)

    def receive(kind, plane, src, dst, bulk):
        everything(kind, plane, bulk).wait_recv()

    def drain(kind, plane, src, dst, bulk):
        everything(kind, plane, bulk).wait_send()

    for k in range(1, 7):
        loads[k].wait()

    def column(mask_ref, count, offset):
        size = mask_ref.shape[1]
        shape = (count, size)
        hit = lax.broadcasted_iota(jnp.int32, shape, 1) == lax.broadcasted_iota(jnp.int32, shape, 0) + offset
        values = jnp.broadcast_to(mask_ref[...].astype(F32), shape)
        return jnp.sum(jnp.where(hit, values, 0.0), axis=1, keepdims=True)

    seqcol_ref[...] = jnp.broadcast_to(column(seq_ref, seq_local, r * seq_local), seqcol_ref.shape)
    rescol = column(res_ref, res_local, c * res_local)
    tilecol = column(res_ref, tile_rows, r * tile_rows)
    kept = jnp.sum(seq_ref[...].astype(F32), axis=1, keepdims=True)

    def live_column(k):
        parts = []
        for q in range(fold):
            parts.append(rescol * seqcol_ref[pl.ds(k * fold + q, 1), 0:1])
        return jnp.concatenate(parts, axis=0)

    w = w_ref[...].astype(F32)
    w = jnp.concatenate([w, jnp.zeros((LANES - 2 * hidden, channels), F32)], axis=0)
    w_wide = w.T.astype(BF16)
    w_turned = w.astype(BF16)
    bias = pb_ref[...]
    bias = jnp.concatenate([bias, jnp.zeros((1, LANES - 2 * hidden), F32)], axis=1)
    gain = gain_ref[...]
    shift = shift_ref[...]

    loads[0].wait()

    def layer_norm(k, carry):
        here = aligned(k * LANES, LANES)
        widened = x_ref[here, :].astype(F32)
        centred = widened - jnp.mean(widened, axis=-1, keepdims=True)
        inverse = lax.rsqrt(jnp.mean(centred * centred, axis=-1, keepdims=True) + EPSILON)
        scaled = centred * inverse
        normed = (scaled * gain + shift).astype(BF16)
        scaled_ref[here, :] = scaled
        inv_ref[here, :] = inverse
        both_ref[here, :channels] = normed
        both_ref[here, channels:] = scaled.astype(BF16)
        prj = (nn(normed, w_wide) + bias) * live_column(k)
        prj_ref[here, :] = prj
        tr_ref[here, :] = prj.T
        return carry

    lax.fori_loop(0, chunks, layer_norm, 0, unroll=min(2 * UNROLL, chunks))

    for im in range(majors):
        pieces = [prj_ref[pl.ds(im * fold + k, seq_local, stride=res_local), :] for k in range(fold)]
        left = place_groups(pieces, [k * hidden for k in range(fold)], hidden)
        lsend_ref[:, im * LANES : (im + 1) * LANES] = left.astype(BF16)
    for sb in range(chunks):
        pieces = [
            tr_ref[pl.ds(sb * LANES + hidden + k, majors, stride=fold), :] for k in range(fold)
        ]
        for q in range(fold):
            turned = place_groups(pieces, [(k - q) * res_local for k in range(fold)], res_local)
            u_ref[pl.ds(sb * fold + q, majors, stride=seq_local), :] = turned
    my_seqs = aligned(r * seq_local, seq_local)
    for dm in range(majors):
        rbuf_ref[my_seqs, dm * LANES : (dm + 1) * LANES] = u_ref[
            dm * seq_local : (dm + 1) * seq_local, :
        ].astype(BF16)

    pl.semaphore_wait(barrier, total - 1)

    def left_slot(k):
        return lbuf_ref.at[aligned((k // factor) * seq_local, seq_local), aligned(lax.rem(k, factor) * block, block)]

    relay_row = c // factor
    relay_col = r * factor + lax.rem(c, factor)
    left_col = chip * 2 + lax.rem(r, 2)
    left_stays = jnp.logical_and(relay_row == r, left_col == c)
    left_out = remote(
        lsend_ref, left_slot(relay_col), one_sems.at[0], left_recv.at[relay_col], relay_row, left_col
    )
    left_home = pltpu.make_async_copy(lsend_ref, left_slot(relay_col), local_sems.at[0])

    @pl.when(left_stays)
    def _():
        left_home.start()

    @pl.when(jnp.logical_not(left_stays))
    def _():
        left_out.start()

    HAND_GL, HAND_A, HAND_B, HAND_LEFT, HAND_OUT, HAND_SW, HAND_SV = 12, 13, 14, 15, 1, 10, 7

    def passed(i, q):
        begin = jnp.minimum((r + 1 - core) // 2, rows // 2 - 1)
        row = 2 * lax.rem(begin + i, rows // 2) + core
        near = (r * factor + q) // 2 == chip
        return row * factor + q, near, jnp.logical_and(row == r, r * factor + q == c)

    def pass_left(i):
        for q in range(factor):
            k, near, own = passed(i, q)
            slot = left_slot(k)

            @pl.when(own)
            def _():
                left_home.wait()

            @pl.when(jnp.logical_not(own))
            def _():
                remote(slot, slot, one_sems.at[0], left_recv.at[k], r, partner).wait_recv()

            @pl.when(near)
            def _():
                def body(t, carry):
                    other = lax.rem(chip + t, chips)
                    remote(slot, slot, left_send.at[k], left_recv.at[k], r, 2 * other + core).start()
                    return carry

                lax.fori_loop(1, chips, body, 0)

            hand(HAND_LEFT, slot, slot)

    def right_block(k):
        return rbuf_ref.at[aligned(k * seq_local, seq_local), :]

    right_args = ("row", 0, lambda k: right_block(r), right_block, grr_ref)

    start(*right_args, last=2)
    for k in late:
        loads[k].wait()
    owf_ref[...] = ow_ref[...].astype(F32)
    for d in range(hidden):
        wp_ref[d * hidden : (d + 1) * hidden, :] = owf_ref[pl.ds(d, hidden, stride=hidden), :].astype(BF16)

    def inverse_divisor(i):
        return 1.0 / jnp.maximum(kept * tilecol[i : i + 1, :] * rescol, 1.0)

    for i in range(tile_rows):
        here = slice(i * res_local, (i + 1) * res_local)
        gpre_ref[here, :] = (cot_ref[here, :].astype(F32) * inverse_divisor(i)).astype(BF16)

    half = WIDE // LANES

    def grad_products(ip, carry):
        upstream = gpre_ref[aligned(ip * WIDE, WIDE), :]
        for dm in range(majors):
            tile = nt(wp_ref[dm * LANES : (dm + 1) * LANES, :], upstream)
            for h in range(half):
                blocks = [
                    tile[a * hidden : (a + 1) * hidden, h * LANES : (h + 1) * LANES] for a in range(fold)
                ]
                for a, swapped in enumerate(lane_group_swap(blocks, res_local)):
                    gp_ref[
                        aligned(((ip * half + h) * fold + a) * hidden, hidden), dm * LANES : (dm + 1) * LANES
                    ] = swapped.astype(BF16)
        return carry

    steps = pairs // WIDE
    lax.fori_loop(0, steps // 2, grad_products, 0)
    start(*right_args, first=2)
    pass_left(0)
    lax.fori_loop(steps // 2, steps, grad_products, 0)

    for i in range(1, rows // 2):
        pass_left(i)
    handed(HAND_LEFT, glp_ref).wait_recv()
    for k in range(block // WIDE):
        grs_ref[:, k * WIDE : (k + 1) * WIDE] = nn(lbuf_ref[...], gp_ref[:, k * WIDE : (k + 1) * WIDE]).astype(BF16)
    gr_args = (
        "row",
        3,
        lambda k: grs_ref.at[aligned(k * seq_local, seq_local), :],
        lambda k: grr_ref.at[k],
        grr_ref,
    )
    for im in range(tile_rows * hidden // LANES):
        lt_ref[im * LANES : (im + 1) * LANES, :] = lbuf_ref[:, im * LANES : (im + 1) * LANES].T
    for k in range(hidden * hidden // LANES):
        wpt_ref[:, k * LANES : (k + 1) * LANES] = wp_ref[k * LANES : (k + 1) * LANES, :].T
    receive(*right_args)
    start(*gr_args)

    def gl_part(k):
        return gls_ref.at[aligned((k // factor) * seq_local, seq_local), aligned(lax.rem(k, factor) * block, block)]

    for k in range(tile_rows * hidden // WIDE):
        gls_ref[:, k * WIDE : (k + 1) * WIDE] = nt(rbuf_ref[...], gp_ref[k * WIDE : (k + 1) * WIDE, :]).astype(BF16)

    def left_block(k, of_core):
        return of_core * chips + k

    def hand_left(k, carry):
        hand(HAND_GL, gl_part(left_block(k, 1 - core)), glp_ref.at[k])
        return carry

    lax.fori_loop(0, chips, hand_left, 0)
    gl_args = ("chip", 2, lambda k: glx_ref.at[k], lambda k: glr_ref.at[k], glr_ref)

    def sum_left():
        handed(HAND_GL, glp_ref).wait_recv()

        def add(k, carry):
            t = left_block(k, core)
            mine = gls_ref[aligned((t // factor) * seq_local, seq_local), aligned(lax.rem(t, factor) * block, block)]
            glx_ref[k] = (mine.astype(F32) + glp_ref[k].astype(F32)).astype(BF16)
            return carry

        lax.fori_loop(0, chips, add, 0)
        start(*gl_args)


    w_block = hidden * hidden // cols
    gw_row_args = ("chip", 4, lambda k: gwx_ref.at[k], lambda k: gwr_ref.at[k], gwr_ref)
    strips = hidden * hidden // WIDE
    per = WIDE // w_block
    first = lax.rem((chip + 1) * 2 * w_block // WIDE, strips)

    def sum_weight(later):
        plane = HAND_B if later else HAND_A
        some = chips // 2
        offset = some if later else 0
        handed(plane, gwp_ref.at[pl.ds(0, some)]).wait_recv()

        def add(k, carry):
            k = lax.rem(first * per // 2 + offset + k, chips)
            t = 2 * k + core
            mine = gws_ref[aligned(t * w_block, w_block), :]
            gwx_ref[k] = (mine.astype(F32) + gwp_ref[k].astype(F32)).astype(BF16)

            @pl.when(k != chip)
            def _():
                send_to(gw_row_args, k)

            return carry

        lax.fori_loop(0, some, add, 0)

    for k in range(strips):
        strip = lax.rem(first + k, strips)
        right = rbuf_ref[:, aligned(strip * WIDE, WIDE)]

        def products(im, carry, strip=strip, right=right):
            tile = nn(lt_ref[aligned(im * LANES, LANES), :], right)
            for h in range(half):
                blocks = [
                    tile[a * hidden : (a + 1) * hidden, h * LANES : (h + 1) * LANES] for a in range(fold)
                ]
                for a, swapped in enumerate(lane_group_swap(blocks, res_local)):
                    at = strip * WIDE + (h * fold + a) * hidden
                    prod_ref[aligned(at, hidden), aligned(im * LANES, LANES)] = swapped.astype(BF16)
            return carry

        lax.fori_loop(0, tile_rows // fold, products, 0, unroll=8)
        here = aligned(strip * WIDE, WIDE)
        gws_ref[here, :] = nn(prod_ref[here, :], gpre_ref[...]).astype(BF16)
        for j in range(per):
            target = strip * per + j

            @pl.when(lax.rem(target, 2) != core)
            def _(target=target, k=k):
                hand(
                    HAND_A if k < strips // 2 else HAND_B,
                    gws_ref.at[aligned(target * w_block, w_block), :],
                    gwp_ref.at[target // 2],
                )

        if k == 0:
            sum_left()
        if k == strips // 2:
            sum_weight(False)

    receive(*gl_args)

    def add_left(t, carry):
        return carry + glr_ref[lax.rem(chip + t, chips)].astype(F32)

    glmid_ref[...] = lax.fori_loop(1, chips, add_left, glx_ref[chip].astype(F32)).astype(BF16)
    gathered = left_block(chip, core)
    owner_row = gathered // factor
    owner_col = r * factor + lax.rem(gathered, factor)
    at_home = jnp.logical_and(owner_row == r, owner_col == c)
    gl_out = remote(glmid_ref, glfin_ref, one_sems.at[2], one_sems.at[3], owner_row, owner_col)
    gl_home = pltpu.make_async_copy(glmid_ref, glfin_ref, local_sems.at[1])

    @pl.when(at_home)
    def _():
        gl_home.start()

    @pl.when(jnp.logical_not(at_home))
    def _():
        gl_out.start()

    out_bias = ob_ref[...]
    for k in range(pairs // WIDE):
        pre = nn(wpt_ref[...], prod_ref[:, k * WIDE : (k + 1) * WIDE]).T + out_bias
        for q in range(WIDE // res_local):
            i = k * (WIDE // res_local) + q
            pair_ref[i * res_local : (i + 1) * res_local, :] = (
                pre[q * res_local : (q + 1) * res_local, :] * inverse_divisor(i)
            ).astype(BF16)

    sum_weight(True)
    w_small = w_block // rows
    receive(*gw_row_args)

    def add_w(t, carry):
        return carry + gwr_ref[lax.rem(chip + t, chips)].astype(F32)

    summed = lax.fori_loop(1, chips, add_w, gwx_ref[chip].astype(F32)).astype(BF16)
    for k in range(rows):
        gwc_ref[k] = summed[k * w_small : (k + 1) * w_small, :]
    gw_col_args = ("row", 5, lambda k: gwc_ref.at[k], lambda k: gwcr_ref.at[k], gwcr_ref)
    start(*gw_col_args)

    receive(*gr_args)
    for dm in range(majors):
        part = slice(dm * LANES, (dm + 1) * LANES)
        total_right = grs_ref[my_seqs, part].astype(F32)

        def add_right(t, carry, part=part):
            return carry + grr_ref[lax.rem(r + t, rows), :, part].astype(F32)

        u_ref[dm * seq_local : (dm + 1) * seq_local, :] = lax.fori_loop(1, rows, add_right, total_right)
    for sb in range(chunks):
        pieces = [u_ref[pl.ds(sb * fold + q, majors, stride=seq_local), :] for q in range(fold)]
        for k in range(fold):
            turned = place_groups(pieces, [(q - k) * res_local for q in range(fold)], res_local)
            tr_ref[pl.ds(sb * LANES + hidden + k, majors, stride=fold), :] = turned

    lane = lax.broadcasted_iota(jnp.int32, (LANES, LANES), 1)

    def lower_right(k, carry):
        here = aligned(k * LANES, LANES)
        right_only = jnp.logical_and(lane >= hidden, lane < 2 * hidden)
        tr_ref[here, :] = jnp.where(right_only, tr_ref[here, :].T * live_column(k), 0.0)
        return carry

    lax.fori_loop(0, chunks, lower_right, 0, unroll=min(2 * UNROLL, chunks))
    giver = r * factor + lax.rem(c, factor)
    giver_row = c // factor
    giver_col = 2 * lax.rem(giver, chips) + giver // chips
    kept_here = jnp.logical_and(giver_row == r, giver_col == c)

    @pl.when(kept_here)
    def _():
        gl_home.wait()

    @pl.when(jnp.logical_not(kept_here))
    def _():
        remote(glmid_ref, glfin_ref, one_sems.at[2], one_sems.at[3], giver_row, giver_col).wait_recv()

    for im in range(majors):
        piece = glfin_ref[:, im * LANES : (im + 1) * LANES].astype(F32)
        for k in range(fold):
            rolled = pltpu.roll(piece, LANES - k * hidden, 1) if k else piece
            prj_ref[pl.ds(im * fold + k, seq_local, stride=res_local), :] = rolled

    def lower(k, bias_sum):
        here = aligned(k * LANES, LANES)
        projected = jnp.where(lane < hidden, prj_ref[here, :] * live_column(k), tr_ref[here, :])
        low_ref[here, :] = projected.astype(BF16)
        return bias_sum + jnp.sum(projected, axis=0, keepdims=True)

    bias_sum = lax.fori_loop(0, chunks, lower, jnp.zeros((1, LANES), F32), unroll=min(2 * UNROLL, chunks))
    joined = tn(low_ref[...], both_ref[...])
    grad_w_in = joined[:, :channels]
    low_sum = jnp.sum(low_ref[...].astype(F32), axis=0, keepdims=True)
    turned = w_turned.astype(F32)
    gain_sum = jnp.sum(joined[:, channels:] * turned, axis=0, keepdims=True)
    shift_sum = jnp.sum(low_sum.T * turned, axis=0, keepdims=True)
    parts = channels // LANES
    sv_ref[...] = jnp.zeros(sv_ref.shape, F32)
    for k in range(parts):
        sv_ref[k : k + 1, :] = gain_sum[:, k * LANES : (k + 1) * LANES]
        sv_ref[parts + k : parts + k + 1, :] = shift_sum[:, k * LANES : (k + 1) * LANES]
    sv_ref[2 * parts : 2 * parts + 1, :] = bias_sum
    quarter = 2 * hidden // cols
    for k in range(cols):
        sw_ref[k] = grad_w_in[k * quarter : (k + 1) * quarter, :].astype(BF16)
    hand(HAND_SV, sv_ref, svp_ref.at[0])

    def hand_sw(k, carry):
        hand(HAND_SW, sw_ref.at[2 * k + 1 - core], swp_ref.at[k])
        return carry

    lax.fori_loop(0, chips, hand_sw, 0)

    def backward(k, carry):
        here = aligned(k * LANES, LANES)
        scaled = scaled_ref[here, :]
        grad_scaled = nn(low_ref[here, :], w_turned) * gain
        first = jnp.mean(grad_scaled, axis=-1, keepdims=True)
        second = jnp.mean(grad_scaled * scaled, axis=-1, keepdims=True)
        ag_ref[here, :] = (inv_ref[here, :] * (grad_scaled - first - scaled * second)).astype(BF16)
        return carry

    split = chunks // 2
    lax.fori_loop(0, split, backward, 0, unroll=min(UNROLL, split))
    handed(HAND_SW, swp_ref).wait_recv()

    def add_sw(k, carry):
        swx_ref[k] = (sw_ref[2 * k + core].astype(F32) + swp_ref[k].astype(F32)).astype(BF16)
        return carry

    lax.fori_loop(0, chips, add_sw, 0)
    sw_args = ("core", 6, lambda k: swx_ref.at[lax.rem(k, chips)], lambda k: swr_ref.at[k], swr_ref)
    start(*sw_args)
    handed(HAND_SV, svp_ref).wait_recv()
    svc_ref[...] = sv_ref[...] + svp_ref[0]
    sv_args = ("core", 8, lambda k: svc_ref, lambda k: svr_ref.at[k], svr_ref)
    start(*sv_args)
    receive(*gw_col_args)

    def add_w_col(t, carry):
        return carry + gwcr_ref[lax.rem(r + t, rows)].astype(F32)

    gw_ref[c, r] = lax.fori_loop(1, rows, add_w_col, gwc_ref[r].astype(F32)).astype(BF16)
    gw_all_args = (
        "core",
        9,
        lambda k: gw_ref.at[c, r],
        lambda k: gw_ref.at[2 * lax.rem(k, chips) + core, k // chips],
        gw_bulk,
    )
    start(*gw_all_args)

    lax.fori_loop(split, chunks, backward, 0, unroll=min(UNROLL, chunks - split))

    def ordered(received, count):
        def add(t, carry):
            return carry + received[t].astype(F32)

        return lax.fori_loop(1, count, add, received[0].astype(F32))

    swr_ref[r * chips + chip] = swx_ref[chip]
    receive(*sw_args)
    swf_ref[...] = ordered(swr_ref, rows * chips)
    gpw_ref[c] = swf_ref[...]
    sw_out_args = ("col", 11, lambda k: swf_ref, lambda k: gpw_ref.at[k], gpw_ref)
    start(*sw_out_args)
    receive(*gw_all_args)

    def hand_out(k, carry):
        slot = gw_ref.at[2 * k + core]
        hand(HAND_OUT, slot, slot)
        return carry

    lax.fori_loop(0, chips, hand_out, 0)
    svr_ref[r * chips + chip] = svc_ref[...]
    receive(*sv_args)
    vec_ref[...] = ordered(svr_ref, rows * chips)
    def widen(of_core):
        def body(t, carry):
            for k in range(rows):
                at = (2 * t + of_core) * rows * w_small + k * w_small
                owf_ref[aligned(at, w_small), :] = gw_ref[2 * t + of_core, k].astype(F32)
            return carry

        lax.fori_loop(0, chips, body, 0)

    widen(core)
    handed(HAND_OUT, gw_ref.at[pl.ds(0, chips)]).wait_recv()
    widen(1 - core)
    for k in range(hidden):
        gwf_ref[k * hidden : (k + 1) * hidden, :] = owf_ref[pl.ds(k, hidden, stride=hidden), :]
    receive(*sw_out_args)

    @pl.when(jnp.logical_not(at_home))
    def _():
        gl_out.wait_send()

    @pl.when(jnp.logical_not(left_stays))
    def _():
        left_out.wait_send()

    for i in range(rows // 2):
        for q in range(factor):
            k, near, _ = passed(i, q)

            @pl.when(near)
            def _():
                rest = glr_ref.at[pl.ds(0, chips - 1)]
                remote(rest, rest, left_send.at[k], left_recv.at[k], r, partner).wait_send()

    handed(HAND_LEFT, glp_ref).wait_send()
    handed(HAND_SW, swp_ref).wait_send()
    handed(HAND_SV, svp_ref).wait_send()
    handed(HAND_GL, glp_ref).wait_send()
    handed(HAND_OUT, gw_ref.at[pl.ds(0, chips)]).wait_send()
    for plane in (HAND_A, HAND_B):
        handed(plane, gwp_ref.at[pl.ds(0, chips // 2)]).wait_send()
    for args in (
        right_args,
        gl_args,
        gr_args,
        gw_row_args,
        gw_col_args,
        sw_args,
        sv_args,
        gw_all_args,
        sw_out_args,
    ):
        drain(*args)


def finish_kernel(*refs):
    pair_ref, ag_ref, gw_ref, gpw_ref, vec_ref = refs[:5]
    pair_hbm, ag_hbm, gain_hbm, shift_hbm, gpw_hbm, bias_hbm, gw_hbm = refs[5:12]
    gain_ref, shift_ref, bias_ref, sems = refs[12:]
    copies = []

    def send(source, target):
        copy = pltpu.make_async_copy(source, target, sems.at[len(copies)])
        copy.start()
        copies.append(copy)

    send(gw_ref, gw_hbm)
    send(ag_ref, ag_hbm)
    send(pair_ref, pair_hbm)
    send(gpw_ref, gpw_hbm)
    parts = gain_ref.shape[1] // LANES
    for k in range(parts):
        gain_ref[:, k * LANES : (k + 1) * LANES] = vec_ref[k : k + 1, :]
        shift_ref[:, k * LANES : (k + 1) * LANES] = vec_ref[parts + k : parts + k + 1, :]
    bias_ref[...] = vec_ref[2 * parts : 2 * parts + 1, : bias_ref.shape[1]]
    send(gain_ref, gain_hbm)
    send(shift_ref, shift_hbm)
    send(bias_ref, bias_hbm)
    for copy in copies:
        copy.wait()


def shards(
    alignment,
    sequence_mask,
    residue_mask,
    layer_norm_gain,
    norm_shift,
    proj_weight,
    proj_bias,
    out_weight,
    out_bias,
    cotangent,
):
    rows = lax.axis_size("row")
    cols = lax.axis_size("col")
    factor = cols // rows
    seq_local, res_local, channels = alignment.shape
    seqs = seq_local * rows
    hidden = proj_weight.shape[1] // 2
    width = out_weight.shape[1]
    tile_rows = res_local * factor
    n = seq_local * res_local
    pairs = tile_rows * res_local
    block = res_local * hidden
    majors = block // LANES
    inner = tile_rows * hidden
    w_block = hidden * hidden // cols
    w_small = w_block // rows
    quarter = 2 * hidden // cols
    dims = (rows, cols, seq_local, res_local, hidden, channels, width)
    vmem = pl.BlockSpec(memory_space=pltpu.VMEM)
    hbm = pl.BlockSpec(memory_space=pltpu.HBM)
    operands = [
        alignment.reshape(n, channels),
        sequence_mask.reshape(1, -1),
        residue_mask.reshape(1, -1),
        layer_norm_gain.reshape(1, -1),
        norm_shift.reshape(1, -1),
        proj_weight.T,
        proj_bias.reshape(1, -1),
        out_weight,
        out_bias.reshape(1, -1),
        cotangent.reshape(pairs, width),
    ]
    operands = [pltpu.with_memory_space_constraint(array, pltpu.HBM) for array in operands]
    pair, grad_alignment, grad_w, grad_pw, vectors = pl.pallas_call(
        functools.partial(fused_kernel, dims),
        out_shape=[
            jax.ShapeDtypeStruct((pairs, width), BF16),
            jax.ShapeDtypeStruct((n, channels), BF16),
            jax.ShapeDtypeStruct((hidden * hidden, width), F32),
            jax.ShapeDtypeStruct((cols, quarter, channels), F32),
            jax.ShapeDtypeStruct((8, LANES), F32),
        ],
        in_specs=[hbm] * 10,
        out_specs=[vmem] * 5,
        scratch_shapes=[
            *[pltpu.VMEM(array.shape, array.dtype) for array in operands],
            pltpu.VMEM((n, channels), F32),
            pltpu.VMEM((n, 1), F32),
            pltpu.VMEM((n, 2 * channels), BF16),
            pltpu.VMEM((n, LANES), F32),
            pltpu.VMEM((n, LANES), F32),
            pltpu.VMEM((majors * seq_local, LANES), F32),
            pltpu.VMEM((seq_local, LANES), F32),
            pltpu.VMEM((seq_local, block), BF16),
            pltpu.VMEM((seqs, inner), BF16),
            pltpu.VMEM((inner, seqs), BF16),
            pltpu.VMEM((seqs, block), BF16),
            pltpu.VMEM((hidden * hidden, width), F32),
            pltpu.VMEM((hidden * hidden, width), BF16),
            pltpu.VMEM((width, hidden * hidden), BF16),
            pltpu.VMEM((pairs, width), BF16),
            pltpu.VMEM((inner, block), BF16),
            pltpu.VMEM((hidden * hidden, pairs), BF16),
            pltpu.VMEM((seqs, inner), BF16),
            pltpu.VMEM((cols, seq_local, block), BF16),
            pltpu.VMEM((cols // 2, seq_local, block), BF16),
            pltpu.VMEM((cols // 2, seq_local, block), BF16),
            pltpu.VMEM((seq_local, block), BF16),
            pltpu.VMEM((seq_local, block), BF16),
            pltpu.VMEM((seqs, block), BF16),
            pltpu.VMEM((rows, seq_local, block), BF16),
            pltpu.VMEM((hidden * hidden, width), BF16),
            pltpu.VMEM((cols // 2, w_block, width), BF16),
            pltpu.VMEM((cols // 2, w_block, width), BF16),
            pltpu.VMEM((cols // 2, w_block, width), BF16),
            pltpu.VMEM((rows, w_small, width), BF16),
            pltpu.VMEM((rows, w_small, width), BF16),
            pltpu.VMEM((cols, rows, w_small, width), BF16),
            pltpu.VMEM((n, LANES), BF16),
            pltpu.VMEM((cols, quarter, channels), BF16),
            pltpu.VMEM((cols // 2, quarter, channels), BF16),
            pltpu.VMEM((cols // 2, quarter, channels), BF16),
            pltpu.VMEM((rows * cols // 2, quarter, channels), BF16),
            pltpu.VMEM((quarter, channels), F32),
            pltpu.VMEM((8, LANES), F32),
            pltpu.VMEM((rows * cols // 2, 8, LANES), F32),
            pltpu.VMEM((1, 8, LANES), F32),
            pltpu.VMEM((8, LANES), F32),
            pltpu.SemaphoreType.DMA((12,)),
            pltpu.SemaphoreType.DMA((4,)),
            pltpu.SemaphoreType.DMA((16,)),
            pltpu.SemaphoreType.DMA((16,)),
            pltpu.SemaphoreType.DMA((cols,)),
            pltpu.SemaphoreType.DMA((cols,)),
        ],
        compiler_params=pltpu.CompilerParams(
            collective_id=0, has_side_effects=True, vmem_limit_bytes=48 * 1024 * 1024
        ),
    )(*operands)
    pair, grad_alignment, gain, shift, grad_pw, bias, grad_w = pl.pallas_call(
        finish_kernel,
        out_shape=[
            jax.ShapeDtypeStruct((pairs, width), BF16),
            jax.ShapeDtypeStruct((n, channels), BF16),
            jax.ShapeDtypeStruct((1, channels), F32),
            jax.ShapeDtypeStruct((1, channels), F32),
            jax.ShapeDtypeStruct((2 * hidden, channels), F32),
            jax.ShapeDtypeStruct((1, 2 * hidden), F32),
            jax.ShapeDtypeStruct((hidden * hidden, width), F32),
        ],
        in_specs=[vmem] * 5,
        out_specs=[hbm] * 7,
        scratch_shapes=[
            pltpu.VMEM((1, channels), F32),
            pltpu.VMEM((1, channels), F32),
            pltpu.VMEM((1, 2 * hidden), F32),
            pltpu.SemaphoreType.DMA((7,)),
        ],
        compiler_params=pltpu.CompilerParams(vmem_limit_bytes=16 * 1024 * 1024),
    )(pair, grad_alignment, grad_w, grad_pw.reshape(-1, channels), vectors)
    return (
        pair.reshape(tile_rows, res_local, width),
        grad_alignment.reshape(seq_local, res_local, channels),
        gain.reshape(-1),
        shift.reshape(-1),
        grad_pw.T,
        bias.reshape(-1),
        grad_w,
    )


def solution(mesh):
    return jax.shard_map(
        shards,
        mesh=mesh,
        in_specs=(
            P(("groups", "row"), "col", None),
            P("groups"),
            P("groups"),
            P(),
            P(),
            P(),
            P(),
            P(),
            P(),
            P(("groups", "row"), "col", None),
        ),
        out_specs=(
            P(("groups", "row"), "col", None),
            P(("groups", "row"), "col", None),
            P("groups"),
            P("groups"),
            P("groups", None),
            P("groups"),
            P("groups", None),
        ),
        check_vma=False,
    )
```

```python
import functools

import jax
import jax.numpy as jnp
from jax import lax
from jax.experimental import pallas as pl
from jax.experimental.pallas import tpu as pltpu
from jax.sharding import PartitionSpec as P

EPSILON = 1e-05
LANES = 128
WIDE = 256
UNROLL = 4
MESH = pl.DeviceIdType.MESH
F32 = jnp.float32
BF16 = jnp.bfloat16


def lane_group_swap(blocks, width):
    lane = lax.broadcasted_iota(jnp.int32, blocks[0].shape, 1)
    span = len(blocks) // 2
    while span:
        low = (lane // (width * span)) % 2 == 0
        out = list(blocks)
        for a in range(len(blocks)):
            if a & span:
                continue
            first, second = blocks[a], blocks[a + span]
            shift = width * span
            out[a] = jnp.where(low, first, pltpu.roll(second, shift, 1))
            out[a + span] = jnp.where(low, pltpu.roll(first, LANES - shift, 1), second)
        blocks = out
        span //= 2
    return blocks


def place_groups(pieces, shifts, width):
    group = lax.broadcasted_iota(jnp.int32, pieces[0].shape, 1) // width
    out = None
    for k, (piece, shift) in enumerate(zip(pieces, shifts)):
        rolled = pltpu.roll(piece, shift % LANES, 1) if shift % LANES else piece
        out = rolled if out is None else jnp.where(group == k, rolled, out)
    return out


def nt(a, b):
    return lax.dot_general(a, b, (((1,), (1,)), ((), ())), preferred_element_type=F32)


def tn(a, b):
    return lax.dot_general(a, b, (((0,), (0,)), ((), ())), preferred_element_type=F32)


def nn(a, b):
    return jnp.dot(a, b, preferred_element_type=F32)


def aligned(start, size, step=None):
    return pl.ds(pl.multiple_of(start, step or size), size)


def fused_kernel(dims, *refs):
    rows, cols, seq_local, res_local, hidden, channels, width = dims
    inputs = refs[:10]
    (pair_ref, ag_ref, gwf_ref, gpw_ref, vec_ref) = refs[10:15]
    (
        x_ref,
        seq_ref,
        res_ref,
        gain_ref,
        shift_ref,
        w_ref,
        pb_ref,
        ow_ref,
        ob_ref,
        cot_ref,
        scaled_ref,
        inv_ref,
        both_ref,
        prj_ref,
        tr_ref,
        u_ref,
        seqcol_ref,
        lsend_ref,
        lbuf_ref,
        lt_ref,
        rbuf_ref,
        owf_ref,
        wp_ref,
        wpt_ref,
        gpre_ref,
        gp_ref,
        prod_ref,
        gls_ref,
        glr_ref,
        glp_ref,
        glx_ref,
        glmid_ref,
        glfin_ref,
        grs_ref,
        grr_ref,
        gws_ref,
        gwr_ref,
        gwp_ref,
        gwx_ref,
        gwc_ref,
        gwcr_ref,
        gw_ref,
        low_ref,
        sw_ref,
        swp_ref,
        swx_ref,
        swr_ref,
        swf_ref,
        sv_ref,
        svr_ref,
        svp_ref,
        svc_ref,
        local_sems,
        one_sems,
        send_sems,
        recv_sems,
        left_send,
        left_recv,
    ) = refs[15:]
    r = lax.axis_index("row")
    c = lax.axis_index("col")
    factor = cols // rows
    seqs = seq_local * rows
    tile_rows = res_local * factor
    n = seq_local * res_local
    pairs = tile_rows * res_local
    block = res_local * hidden
    fold = LANES // res_local
    chunks = n // LANES
    majors = block // LANES
    total = rows * cols
    chips = cols // 2
    chip = c // 2
    core = lax.rem(c, 2)
    partner = chip * 2 + 1 - core
    barrier = pltpu.get_barrier_semaphore()

    def greet(t, carry):
        other = lax.rem(r * cols + c + t, total)
        pl.semaphore_signal(
            barrier,
            inc=1,
            device_id={"row": other // cols, "col": lax.rem(other, cols)},
            device_id_type=MESH,
        )
        return carry

    staged = (x_ref, seq_ref, res_ref, gain_ref, shift_ref, w_ref, pb_ref, ow_ref, ob_ref, cot_ref)
    loads = [
        pltpu.make_async_copy(source, target, local_sems.at[2 + k])
        for k, (source, target) in enumerate(zip(inputs, staged))
    ]
    late = (7, 8, 9)
    for load in loads[: late[0]]:
        load.start()
    lax.fori_loop(1, total, greet, 0)
    for k in late:
        loads[k].start()

    def remote(src, dst, send_sem, recv_sem, trow, tcol):
        return pltpu.make_async_remote_copy(
            src_ref=src,
            dst_ref=dst,
            send_sem=send_sem,
            recv_sem=recv_sem,
            device_id={"row": trow, "col": tcol},
            device_id_type=MESH,
        )

    gw_bulk = gws_ref.at[pl.ds(0, (rows * chips - 1) * (hidden * hidden // total)), :]

    def over(kind):
        if kind == "col":
            return cols, c, lambda k: (r, k)
        if kind == "row":
            return rows, r, lambda k: (k, c)
        if kind == "chip":
            return chips, chip, lambda k: (r, 2 * k + core)
        return rows * chips, r * chips + chip, lambda k: (k // chips, 2 * lax.rem(k, chips) + core)

    def send_to(args, k):
        kind, plane, src, dst, bulk = args
        _, me, where = over(kind)
        remote(src(k), dst(me), send_sems.at[plane], recv_sems.at[plane], *where(k)).start()

    def start(*args, first=1, last=None):
        kind = args[0]
        count, me, _ = over(kind)

        def body(t, carry):
            if kind != "row":
                send_to(args, lax.rem(me + t, count))
            else:
                @pl.when(me + t < count)
                def _():
                    send_to(args, lax.rem(me + t, count))

                @pl.when(me >= t)
                def _():
                    send_to(args, lax.rem(me - t + count, count))

            return carry

        lax.fori_loop(first, last or count, body, 0)

    def everything(kind, plane, bulk):
        count, me, where = over(kind)
        part = bulk if bulk is gw_bulk else bulk.at[pl.ds(0, count - 1)]
        return remote(part, part, send_sems.at[plane], recv_sems.at[plane], *where(lax.rem(me + 1, count)))

    def hand(plane, src, dst):
        remote(src, dst, send_sems.at[plane], recv_sems.at[plane], r, partner).start()

    def handed(plane, bulk):
        return remote(bulk, bulk, send_sems.at[plane], recv_sems.at[plane], r, partner)

    def receive(kind, plane, src, dst, bulk):
        everything(kind, plane, bulk).wait_recv()

    def drain(kind, plane, src, dst, bulk):
        everything(kind, plane, bulk).wait_send()

    for k in range(1, 7):
        loads[k].wait()

    def column(mask_ref, count, offset):
        size = mask_ref.shape[1]
        shape = (count, size)
        hit = lax.broadcasted_iota(jnp.int32, shape, 1) == lax.broadcasted_iota(jnp.int32, shape, 0) + offset
        values = jnp.broadcast_to(mask_ref[...].astype(F32), shape)
        return jnp.sum(jnp.where(hit, values, 0.0), axis=1, keepdims=True)

    seqcol_ref[...] = jnp.broadcast_to(column(seq_ref, seq_local, r * seq_local), seqcol_ref.shape)
    rescol = column(res_ref, res_local, c * res_local)
    tilecol = column(res_ref, tile_rows, r * tile_rows)
    kept = jnp.sum(seq_ref[...].astype(F32), axis=1, keepdims=True)

    def live_column(k):
        parts = []
        for q in range(fold):
            parts.append(rescol * seqcol_ref[pl.ds(k * fold + q, 1), 0:1])
        return jnp.concatenate(parts, axis=0)

    w = w_ref[...].astype(F32)
    w = jnp.concatenate([w, jnp.zeros((LANES - 2 * hidden, channels), F32)], axis=0)
    w_wide = w.T.astype(BF16)
    w_turned = w.astype(BF16)
    bias = pb_ref[...]
    bias = jnp.concatenate([bias, jnp.zeros((1, LANES - 2 * hidden), F32)], axis=1)
    gain = gain_ref[...]
    shift = shift_ref[...]

    loads[0].wait()

    def layer_norm(k, carry):
        here = aligned(k * LANES, LANES)
        widened = x_ref[here, :].astype(F32)
        centred = widened - jnp.mean(widened, axis=-1, keepdims=True)
        inverse = lax.rsqrt(jnp.mean(centred * centred, axis=-1, keepdims=True) + EPSILON)
        scaled = centred * inverse
        normed = (scaled * gain + shift).astype(BF16)
        scaled_ref[here, :] = scaled
        inv_ref[here, :] = inverse
        both_ref[here, :channels] = normed
        both_ref[here, channels:] = scaled.astype(BF16)
        prj = (nn(normed, w_wide) + bias) * live_column(k)
        prj_ref[here, :] = prj
        tr_ref[here, :] = prj.T
        return carry

    lax.fori_loop(0, chunks, layer_norm, 0, unroll=min(2 * UNROLL, chunks))

    for im in range(majors):
        pieces = [prj_ref[pl.ds(im * fold + k, seq_local, stride=res_local), :] for k in range(fold)]
        left = place_groups(pieces, [k * hidden for k in range(fold)], hidden)
        lsend_ref[:, im * LANES : (im + 1) * LANES] = left.astype(BF16)
    for sb in range(chunks):
        pieces = [
            tr_ref[pl.ds(sb * LANES + hidden + k, majors, stride=fold), :] for k in range(fold)
        ]
        for q in range(fold):
            turned = place_groups(pieces, [(k - q) * res_local for k in range(fold)], res_local)
            u_ref[pl.ds(sb * fold + q, majors, stride=seq_local), :] = turned
    my_seqs = aligned(r * seq_local, seq_local)
    for dm in range(majors):
        rbuf_ref[my_seqs, dm * LANES : (dm + 1) * LANES] = u_ref[
            dm * seq_local : (dm + 1) * seq_local, :
        ].astype(BF16)

    pl.semaphore_wait(barrier, total - 1)

    def left_slot(k):
        return lbuf_ref.at[aligned((k // factor) * seq_local, seq_local), aligned(lax.rem(k, factor) * block, block)]

    relay_row = c // factor
    relay_col = r * factor + lax.rem(c, factor)
    left_col = chip * 2 + lax.rem(r, 2)
    left_stays = jnp.logical_and(relay_row == r, left_col == c)
    left_out = remote(
        lsend_ref, left_slot(relay_col), one_sems.at[0], left_recv.at[relay_col], relay_row, left_col
    )
    left_home = pltpu.make_async_copy(lsend_ref, left_slot(relay_col), local_sems.at[0])

    @pl.when(left_stays)
    def _():
        left_home.start()

    @pl.when(jnp.logical_not(left_stays))
    def _():
        left_out.start()

    HAND_GL, HAND_A, HAND_B, HAND_LEFT, HAND_OUT, HAND_SW, HAND_SV, HAND_SWR = 12, 13, 14, 15, 1, 10, 7, 16

    def passed(i, q):
        begin = jnp.minimum((r + 1 - core) // 2, rows // 2 - 1)
        row = 2 * lax.rem(begin + i, rows // 2) + core
        near = (r * factor + q) // 2 == chip
        return row * factor + q, near, jnp.logical_and(row == r, r * factor + q == c)

    def pass_left(i):
        for q in range(factor):
            k, near, own = passed(i, q)
            slot = left_slot(k)

            @pl.when(own)
            def _():
                left_home.wait()

            @pl.when(jnp.logical_not(own))
            def _():
                remote(slot, slot, one_sems.at[0], left_recv.at[k], r, partner).wait_recv()

            @pl.when(near)
            def _():
                def body(t, carry):
                    other = lax.rem(chip + t, chips)
                    remote(slot, slot, left_send.at[k], left_recv.at[k], r, 2 * other + core).start()
                    return carry

                lax.fori_loop(1, chips, body, 0)

            hand(HAND_LEFT, slot, slot)

    def right_block(k):
        return rbuf_ref.at[aligned(k * seq_local, seq_local), :]

    right_args = ("row", 0, lambda k: right_block(r), right_block, grr_ref)

    start(*right_args, last=2)
    for k in late:
        loads[k].wait()
    owf_ref[...] = ow_ref[...].astype(F32)
    for d in range(hidden):
        wp_ref[d * hidden : (d + 1) * hidden, :] = owf_ref[pl.ds(d, hidden, stride=hidden), :].astype(BF16)

    def inverse_divisor(i):
        return 1.0 / jnp.maximum(kept * tilecol[i : i + 1, :] * rescol, 1.0)

    for i in range(tile_rows):
        here = slice(i * res_local, (i + 1) * res_local)
        gpre_ref[here, :] = (cot_ref[here, :].astype(F32) * inverse_divisor(i)).astype(BF16)

    half = WIDE // LANES

    def grad_products(ip, carry):
        upstream = gpre_ref[aligned(ip * WIDE, WIDE), :]
        for dm in range(majors):
            tile = nt(wp_ref[dm * LANES : (dm + 1) * LANES, :], upstream)
            for h in range(half):
                blocks = [
                    tile[a * hidden : (a + 1) * hidden, h * LANES : (h + 1) * LANES] for a in range(fold)
                ]
                for a, swapped in enumerate(lane_group_swap(blocks, res_local)):
                    gp_ref[
                        aligned(((ip * half + h) * fold + a) * hidden, hidden), dm * LANES : (dm + 1) * LANES
                    ] = swapped.astype(BF16)
        return carry

    steps = pairs // WIDE
    lax.fori_loop(0, steps // 2, grad_products, 0)
    start(*right_args, first=2)
    pass_left(0)
    lax.fori_loop(steps // 2, steps, grad_products, 0)

    for i in range(1, rows // 2):
        pass_left(i)
    handed(HAND_LEFT, glp_ref).wait_recv()
    for k in range(block // WIDE):
        grs_ref[:, k * WIDE : (k + 1) * WIDE] = nn(lbuf_ref[...], gp_ref[:, k * WIDE : (k + 1) * WIDE]).astype(BF16)
    gr_args = (
        "row",
        3,
        lambda k: grs_ref.at[aligned(k * seq_local, seq_local), :],
        lambda k: grr_ref.at[k],
        grr_ref,
    )
    for im in range(tile_rows * hidden // LANES):
        lt_ref[im * LANES : (im + 1) * LANES, :] = lbuf_ref[:, im * LANES : (im + 1) * LANES].T
    for k in range(hidden * hidden // LANES):
        wpt_ref[:, k * LANES : (k + 1) * LANES] = wp_ref[k * LANES : (k + 1) * LANES, :].T
    receive(*right_args)
    start(*gr_args)

    def gl_part(k):
        return gls_ref.at[aligned((k // factor) * seq_local, seq_local), aligned(lax.rem(k, factor) * block, block)]

    for k in range(tile_rows * hidden // WIDE):
        gls_ref[:, k * WIDE : (k + 1) * WIDE] = nt(rbuf_ref[...], gp_ref[k * WIDE : (k + 1) * WIDE, :]).astype(BF16)

    def left_block(k, of_core):
        return of_core * chips + k

    def hand_left(k, carry):
        hand(HAND_GL, gl_part(left_block(k, 1 - core)), glp_ref.at[k])
        return carry

    lax.fori_loop(0, chips, hand_left, 0)
    gl_args = ("chip", 2, lambda k: glx_ref.at[k], lambda k: glr_ref.at[k], glr_ref)

    def sum_left():
        handed(HAND_GL, glp_ref).wait_recv()

        def add(k, carry):
            t = left_block(k, core)
            mine = gls_ref[aligned((t // factor) * seq_local, seq_local), aligned(lax.rem(t, factor) * block, block)]
            glx_ref[k] = (mine.astype(F32) + glp_ref[k].astype(F32)).astype(BF16)
            return carry

        lax.fori_loop(0, chips, add, 0)
        start(*gl_args)


    w_block = hidden * hidden // cols
    gw_row_args = ("chip", 4, lambda k: gwx_ref.at[k], lambda k: gwr_ref.at[k], gwr_ref)
    strips = hidden * hidden // WIDE
    per = WIDE // w_block
    first = lax.rem((chip + 1) * 2 * w_block // WIDE, strips)

    def sum_weight(later):
        plane = HAND_B if later else HAND_A
        some = chips // 2
        offset = some if later else 0
        handed(plane, gwp_ref.at[pl.ds(0, some)]).wait_recv()

        def add(k, carry):
            k = lax.rem(first * per // 2 + offset + k, chips)
            t = 2 * k + core
            mine = gws_ref[aligned(t * w_block, w_block), :]
            gwx_ref[k] = (mine.astype(F32) + gwp_ref[k].astype(F32)).astype(BF16)

            @pl.when(k != chip)
            def _():
                send_to(gw_row_args, k)

            return carry

        lax.fori_loop(0, some, add, 0)

    for k in range(strips):
        strip = lax.rem(first + k, strips)
        right = rbuf_ref[:, aligned(strip * WIDE, WIDE)]

        def products(im, carry, strip=strip, right=right):
            tile = nn(lt_ref[aligned(im * LANES, LANES), :], right)
            for h in range(half):
                blocks = [
                    tile[a * hidden : (a + 1) * hidden, h * LANES : (h + 1) * LANES] for a in range(fold)
                ]
                for a, swapped in enumerate(lane_group_swap(blocks, res_local)):
                    at = strip * WIDE + (h * fold + a) * hidden
                    prod_ref[aligned(at, hidden), aligned(im * LANES, LANES)] = swapped.astype(BF16)
            return carry

        lax.fori_loop(0, tile_rows // fold, products, 0, unroll=8)
        here = aligned(strip * WIDE, WIDE)
        gws_ref[here, :] = nn(prod_ref[here, :], gpre_ref[...]).astype(BF16)
        for j in range(per):
            target = strip * per + j

            @pl.when(lax.rem(target, 2) != core)
            def _(target=target, k=k):
                hand(
                    HAND_A if k < strips // 2 else HAND_B,
                    gws_ref.at[aligned(target * w_block, w_block), :],
                    gwp_ref.at[target // 2],
                )

        if k == 0:
            sum_left()
        if k == strips // 2:
            sum_weight(False)

    receive(*gl_args)

    def add_left(t, carry):
        return carry + glr_ref[lax.rem(chip + t, chips)].astype(F32)

    glmid_ref[...] = lax.fori_loop(1, chips, add_left, glx_ref[chip].astype(F32)).astype(BF16)
    gathered = left_block(chip, core)
    owner_row = gathered // factor
    owner_col = r * factor + lax.rem(gathered, factor)
    at_home = jnp.logical_and(owner_row == r, owner_col == c)
    gl_out = remote(glmid_ref, glfin_ref, one_sems.at[2], one_sems.at[3], owner_row, owner_col)
    gl_home = pltpu.make_async_copy(glmid_ref, glfin_ref, local_sems.at[1])

    @pl.when(at_home)
    def _():
        gl_home.start()

    @pl.when(jnp.logical_not(at_home))
    def _():
        gl_out.start()

    out_bias = ob_ref[...]
    for k in range(pairs // WIDE):
        pre = nn(wpt_ref[...], prod_ref[:, k * WIDE : (k + 1) * WIDE]).T + out_bias
        for q in range(WIDE // res_local):
            i = k * (WIDE // res_local) + q
            pair_ref[i * res_local : (i + 1) * res_local, :] = (
                pre[q * res_local : (q + 1) * res_local, :] * inverse_divisor(i)
            ).astype(BF16)

    sum_weight(True)
    w_small = w_block // rows
    receive(*gw_row_args)

    def add_w(t, carry):
        return carry + gwr_ref[lax.rem(chip + t, chips)].astype(F32)

    summed = lax.fori_loop(1, chips, add_w, gwx_ref[chip].astype(F32)).astype(BF16)
    for k in range(rows):
        gwc_ref[k] = summed[k * w_small : (k + 1) * w_small, :]
    gw_col_args = ("row", 5, lambda k: gwc_ref.at[k], lambda k: gwcr_ref.at[k], gwcr_ref)
    start(*gw_col_args)

    receive(*gr_args)
    for dm in range(majors):
        part = slice(dm * LANES, (dm + 1) * LANES)
        total_right = grs_ref[my_seqs, part].astype(F32)

        def add_right(t, carry, part=part):
            return carry + grr_ref[lax.rem(r + t, rows), :, part].astype(F32)

        u_ref[dm * seq_local : (dm + 1) * seq_local, :] = lax.fori_loop(1, rows, add_right, total_right)
    for sb in range(chunks):
        pieces = [u_ref[pl.ds(sb * fold + q, majors, stride=seq_local), :] for q in range(fold)]
        for k in range(fold):
            turned = place_groups(pieces, [(q - k) * res_local for q in range(fold)], res_local)
            tr_ref[pl.ds(sb * LANES + hidden + k, majors, stride=fold), :] = turned

    lane = lax.broadcasted_iota(jnp.int32, (LANES, LANES), 1)

    def lower_right(k, carry):
        here = aligned(k * LANES, LANES)
        right_only = jnp.logical_and(lane >= hidden, lane < 2 * hidden)
        right_part = jnp.where(right_only, tr_ref[here, :].T * live_column(k), 0.0)
        tr_ref[here, :] = right_part
        low_ref[here, :] = right_part.astype(BF16)
        return carry

    lax.fori_loop(0, chunks, lower_right, 0, unroll=min(2 * UNROLL, chunks))
    quarter = 2 * hidden // cols
    sw_args = ("core", 6, lambda k: swx_ref.at[lax.rem(k, chips)], lambda k: swr_ref.at[k], swr_ref)
    few = chips // 2

    def hand_quarters(plane, low_chip, summed_over):
        for k in range(2 * low_chip, 2 * (low_chip + few)):
            sw_ref[k] = summed_over[k * quarter : (k + 1) * quarter, :].astype(BF16)

        def body(k, carry):
            hand(plane, sw_ref.at[2 * k + 1 - core], swp_ref.at[k])
            return carry

        lax.fori_loop(low_chip, low_chip + few, body, 0)

    def send_quarters(plane, low_chip):
        handed(plane, swp_ref.at[pl.ds(low_chip, few)]).wait_recv()

        def add(k, carry):
            swx_ref[k] = (sw_ref[2 * k + core].astype(F32) + swp_ref[k].astype(F32)).astype(BF16)
            return carry

        lax.fori_loop(low_chip, low_chip + few, add, 0)

        def body(t, carry):
            k = lax.rem(r * chips + chip + t, rows * chips)
            target = lax.rem(k, chips)

            @pl.when(jnp.logical_and(target >= low_chip, target < low_chip + few))
            def _():
                send_to(sw_args, k)

            return carry

        lax.fori_loop(1, rows * chips, body, 0)

    hand_quarters(HAND_SWR, few, tn(low_ref[...], both_ref[:, :channels]))
    send_quarters(HAND_SWR, few)
    giver = r * factor + lax.rem(c, factor)
    giver_row = c // factor
    giver_col = 2 * lax.rem(giver, chips) + giver // chips
    kept_here = jnp.logical_and(giver_row == r, giver_col == c)

    @pl.when(kept_here)
    def _():
        gl_home.wait()

    @pl.when(jnp.logical_not(kept_here))
    def _():
        remote(glmid_ref, glfin_ref, one_sems.at[2], one_sems.at[3], giver_row, giver_col).wait_recv()

    for im in range(majors):
        piece = glfin_ref[:, im * LANES : (im + 1) * LANES].astype(F32)
        for k in range(fold):
            rolled = pltpu.roll(piece, LANES - k * hidden, 1) if k else piece
            prj_ref[pl.ds(im * fold + k, seq_local, stride=res_local), :] = rolled

    def lower(k, bias_sum):
        here = aligned(k * LANES, LANES)
        projected = jnp.where(lane < hidden, prj_ref[here, :] * live_column(k), tr_ref[here, :])
        low_ref[here, :] = projected.astype(BF16)
        return bias_sum + jnp.sum(projected, axis=0, keepdims=True)

    bias_sum = lax.fori_loop(0, chunks, lower, jnp.zeros((1, LANES), F32), unroll=min(2 * UNROLL, chunks))
    joined = tn(low_ref[...], both_ref[...])
    grad_w_in = joined[:, :channels]
    low_sum = jnp.sum(low_ref[...].astype(F32), axis=0, keepdims=True)
    turned = w_turned.astype(F32)
    gain_sum = jnp.sum(joined[:, channels:] * turned, axis=0, keepdims=True)
    shift_sum = jnp.sum(low_sum.T * turned, axis=0, keepdims=True)
    parts = channels // LANES
    sv_ref[...] = jnp.zeros(sv_ref.shape, F32)
    for k in range(parts):
        sv_ref[k : k + 1, :] = gain_sum[:, k * LANES : (k + 1) * LANES]
        sv_ref[parts + k : parts + k + 1, :] = shift_sum[:, k * LANES : (k + 1) * LANES]
    sv_ref[2 * parts : 2 * parts + 1, :] = bias_sum
    hand(HAND_SV, sv_ref, svp_ref.at[0])

    hand_quarters(HAND_SW, 0, grad_w_in)
    def backward(k, carry):
        here = aligned(k * LANES, LANES)
        scaled = scaled_ref[here, :]
        grad_scaled = nn(low_ref[here, :], w_turned) * gain
        first = jnp.mean(grad_scaled, axis=-1, keepdims=True)
        second = jnp.mean(grad_scaled * scaled, axis=-1, keepdims=True)
        ag_ref[here, :] = (inv_ref[here, :] * (grad_scaled - first - scaled * second)).astype(BF16)
        return carry

    split = chunks // 2
    lax.fori_loop(0, split, backward, 0, unroll=min(UNROLL, split))
    send_quarters(HAND_SW, 0)
    handed(HAND_SV, svp_ref).wait_recv()
    svc_ref[...] = sv_ref[...] + svp_ref[0]
    sv_args = ("core", 8, lambda k: svc_ref, lambda k: svr_ref.at[k], svr_ref)
    start(*sv_args)
    receive(*gw_col_args)

    def add_w_col(t, carry):
        return carry + gwcr_ref[lax.rem(r + t, rows)].astype(F32)

    gw_ref[c, r] = lax.fori_loop(1, rows, add_w_col, gwc_ref[r].astype(F32)).astype(BF16)
    gw_all_args = (
        "core",
        9,
        lambda k: gw_ref.at[c, r],
        lambda k: gw_ref.at[2 * lax.rem(k, chips) + core, k // chips],
        gw_bulk,
    )
    start(*gw_all_args)

    lax.fori_loop(split, chunks, backward, 0, unroll=min(UNROLL, chunks - split))

    def ordered(received, count):
        def add(t, carry):
            return carry + received[t].astype(F32)

        return lax.fori_loop(1, count, add, received[0].astype(F32))

    swr_ref[r * chips + chip] = swx_ref[chip]
    receive(*sw_args)
    swf_ref[...] = ordered(swr_ref, rows * chips)
    gpw_ref[c] = swf_ref[...]
    sw_out_args = ("col", 11, lambda k: swf_ref, lambda k: gpw_ref.at[k], gpw_ref)
    start(*sw_out_args)
    receive(*gw_all_args)

    def hand_out(k, carry):
        slot = gw_ref.at[2 * k + core]
        hand(HAND_OUT, slot, slot)
        return carry

    lax.fori_loop(0, chips, hand_out, 0)
    svr_ref[r * chips + chip] = svc_ref[...]
    receive(*sv_args)
    vec_ref[...] = ordered(svr_ref, rows * chips)
    def widen(of_core):
        def body(t, carry):
            for k in range(rows):
                at = (2 * t + of_core) * rows * w_small + k * w_small
                owf_ref[aligned(at, w_small), :] = gw_ref[2 * t + of_core, k].astype(F32)
            return carry

        lax.fori_loop(0, chips, body, 0)

    widen(core)
    handed(HAND_OUT, gw_ref.at[pl.ds(0, chips)]).wait_recv()
    widen(1 - core)
    for k in range(hidden):
        gwf_ref[k * hidden : (k + 1) * hidden, :] = owf_ref[pl.ds(k, hidden, stride=hidden), :]
    receive(*sw_out_args)

    @pl.when(jnp.logical_not(at_home))
    def _():
        gl_out.wait_send()

    @pl.when(jnp.logical_not(left_stays))
    def _():
        left_out.wait_send()

    for i in range(rows // 2):
        for q in range(factor):
            k, near, _ = passed(i, q)

            @pl.when(near)
            def _():
                rest = glr_ref.at[pl.ds(0, chips - 1)]
                remote(rest, rest, left_send.at[k], left_recv.at[k], r, partner).wait_send()

    handed(HAND_LEFT, glp_ref).wait_send()
    for plane in (HAND_SW, HAND_SWR):
        handed(plane, swp_ref.at[pl.ds(0, few)]).wait_send()
    handed(HAND_SV, svp_ref).wait_send()
    handed(HAND_GL, glp_ref).wait_send()
    handed(HAND_OUT, gw_ref.at[pl.ds(0, chips)]).wait_send()
    for plane in (HAND_A, HAND_B):
        handed(plane, gwp_ref.at[pl.ds(0, chips // 2)]).wait_send()
    for args in (
        right_args,
        gl_args,
        gr_args,
        gw_row_args,
        gw_col_args,
        sw_args,
        sv_args,
        gw_all_args,
        sw_out_args,
    ):
        drain(*args)


def finish_kernel(*refs):
    pair_ref, ag_ref, gw_ref, gpw_ref, vec_ref = refs[:5]
    pair_hbm, ag_hbm, gain_hbm, shift_hbm, gpw_hbm, bias_hbm, gw_hbm = refs[5:12]
    gain_ref, shift_ref, bias_ref, sems = refs[12:]
    copies = []

    def send(source, target):
        copy = pltpu.make_async_copy(source, target, sems.at[len(copies)])
        copy.start()
        copies.append(copy)

    send(gw_ref, gw_hbm)
    send(ag_ref, ag_hbm)
    send(pair_ref, pair_hbm)
    send(gpw_ref, gpw_hbm)
    parts = gain_ref.shape[1] // LANES
    for k in range(parts):
        gain_ref[:, k * LANES : (k + 1) * LANES] = vec_ref[k : k + 1, :]
        shift_ref[:, k * LANES : (k + 1) * LANES] = vec_ref[parts + k : parts + k + 1, :]
    bias_ref[...] = vec_ref[2 * parts : 2 * parts + 1, : bias_ref.shape[1]]
    send(gain_ref, gain_hbm)
    send(shift_ref, shift_hbm)
    send(bias_ref, bias_hbm)
    for copy in copies:
        copy.wait()


def shards(
    alignment,
    sequence_mask,
    residue_mask,
    layer_norm_gain,
    norm_shift,
    proj_weight,
    proj_bias,
    out_weight,
    out_bias,
    cotangent,
):
    rows = lax.axis_size("row")
    cols = lax.axis_size("col")
    factor = cols // rows
    seq_local, res_local, channels = alignment.shape
    seqs = seq_local * rows
    hidden = proj_weight.shape[1] // 2
    width = out_weight.shape[1]
    tile_rows = res_local * factor
    n = seq_local * res_local
    pairs = tile_rows * res_local
    block = res_local * hidden
    majors = block // LANES
    inner = tile_rows * hidden
    w_block = hidden * hidden // cols
    w_small = w_block // rows
    quarter = 2 * hidden // cols
    dims = (rows, cols, seq_local, res_local, hidden, channels, width)
    vmem = pl.BlockSpec(memory_space=pltpu.VMEM)
    hbm = pl.BlockSpec(memory_space=pltpu.HBM)
    operands = [
        alignment.reshape(n, channels),
        sequence_mask.reshape(1, -1),
        residue_mask.reshape(1, -1),
        layer_norm_gain.reshape(1, -1),
        norm_shift.reshape(1, -1),
        proj_weight.T,
        proj_bias.reshape(1, -1),
        out_weight,
        out_bias.reshape(1, -1),
        cotangent.reshape(pairs, width),
    ]
    operands = [pltpu.with_memory_space_constraint(array, pltpu.HBM) for array in operands]
    pair, grad_alignment, grad_w, grad_pw, vectors = pl.pallas_call(
        functools.partial(fused_kernel, dims),
        out_shape=[
            jax.ShapeDtypeStruct((pairs, width), BF16),
            jax.ShapeDtypeStruct((n, channels), BF16),
            jax.ShapeDtypeStruct((hidden * hidden, width), F32),
            jax.ShapeDtypeStruct((cols, quarter, channels), F32),
            jax.ShapeDtypeStruct((8, LANES), F32),
        ],
        in_specs=[hbm] * 10,
        out_specs=[vmem] * 5,
        scratch_shapes=[
            *[pltpu.VMEM(array.shape, array.dtype) for array in operands],
            pltpu.VMEM((n, channels), F32),
            pltpu.VMEM((n, 1), F32),
            pltpu.VMEM((n, 2 * channels), BF16),
            pltpu.VMEM((n, LANES), F32),
            pltpu.VMEM((n, LANES), F32),
            pltpu.VMEM((majors * seq_local, LANES), F32),
            pltpu.VMEM((seq_local, LANES), F32),
            pltpu.VMEM((seq_local, block), BF16),
            pltpu.VMEM((seqs, inner), BF16),
            pltpu.VMEM((inner, seqs), BF16),
            pltpu.VMEM((seqs, block), BF16),
            pltpu.VMEM((hidden * hidden, width), F32),
            pltpu.VMEM((hidden * hidden, width), BF16),
            pltpu.VMEM((width, hidden * hidden), BF16),
            pltpu.VMEM((pairs, width), BF16),
            pltpu.VMEM((inner, block), BF16),
            pltpu.VMEM((hidden * hidden, pairs), BF16),
            pltpu.VMEM((seqs, inner), BF16),
            pltpu.VMEM((cols, seq_local, block), BF16),
            pltpu.VMEM((cols // 2, seq_local, block), BF16),
            pltpu.VMEM((cols // 2, seq_local, block), BF16),
            pltpu.VMEM((seq_local, block), BF16),
            pltpu.VMEM((seq_local, block), BF16),
            pltpu.VMEM((seqs, block), BF16),
            pltpu.VMEM((rows, seq_local, block), BF16),
            pltpu.VMEM((hidden * hidden, width), BF16),
            pltpu.VMEM((cols // 2, w_block, width), BF16),
            pltpu.VMEM((cols // 2, w_block, width), BF16),
            pltpu.VMEM((cols // 2, w_block, width), BF16),
            pltpu.VMEM((rows, w_small, width), BF16),
            pltpu.VMEM((rows, w_small, width), BF16),
            pltpu.VMEM((cols, rows, w_small, width), BF16),
            pltpu.VMEM((n, LANES), BF16),
            pltpu.VMEM((cols, quarter, channels), BF16),
            pltpu.VMEM((cols // 2, quarter, channels), BF16),
            pltpu.VMEM((cols // 2, quarter, channels), BF16),
            pltpu.VMEM((rows * cols // 2, quarter, channels), BF16),
            pltpu.VMEM((quarter, channels), F32),
            pltpu.VMEM((8, LANES), F32),
            pltpu.VMEM((rows * cols // 2, 8, LANES), F32),
            pltpu.VMEM((1, 8, LANES), F32),
            pltpu.VMEM((8, LANES), F32),
            pltpu.SemaphoreType.DMA((12,)),
            pltpu.SemaphoreType.DMA((4,)),
            pltpu.SemaphoreType.DMA((17,)),
            pltpu.SemaphoreType.DMA((17,)),
            pltpu.SemaphoreType.DMA((cols,)),
            pltpu.SemaphoreType.DMA((cols,)),
        ],
        compiler_params=pltpu.CompilerParams(
            collective_id=0, has_side_effects=True, vmem_limit_bytes=48 * 1024 * 1024
        ),
    )(*operands)
    pair, grad_alignment, gain, shift, grad_pw, bias, grad_w = pl.pallas_call(
        finish_kernel,
        out_shape=[
            jax.ShapeDtypeStruct((pairs, width), BF16),
            jax.ShapeDtypeStruct((n, channels), BF16),
            jax.ShapeDtypeStruct((1, channels), F32),
            jax.ShapeDtypeStruct((1, channels), F32),
            jax.ShapeDtypeStruct((2 * hidden, channels), F32),
            jax.ShapeDtypeStruct((1, 2 * hidden), F32),
            jax.ShapeDtypeStruct((hidden * hidden, width), F32),
        ],
        in_specs=[vmem] * 5,
        out_specs=[hbm] * 7,
        scratch_shapes=[
            pltpu.VMEM((1, channels), F32),
            pltpu.VMEM((1, channels), F32),
            pltpu.VMEM((1, 2 * hidden), F32),
            pltpu.SemaphoreType.DMA((7,)),
        ],
        compiler_params=pltpu.CompilerParams(vmem_limit_bytes=16 * 1024 * 1024),
    )(pair, grad_alignment, grad_w, grad_pw.reshape(-1, channels), vectors)
    return (
        pair.reshape(tile_rows, res_local, width),
        grad_alignment.reshape(seq_local, res_local, channels),
        gain.reshape(-1),
        shift.reshape(-1),
        grad_pw.T,
        bias.reshape(-1),
        grad_w,
    )


def solution(mesh):
    return jax.shard_map(
        shards,
        mesh=mesh,
        in_specs=(
            P(("groups", "row"), "col", None),
            P("groups"),
            P("groups"),
            P(),
            P(),
            P(),
            P(),
            P(),
            P(),
            P(("groups", "row"), "col", None),
        ),
        out_specs=(
            P(("groups", "row"), "col", None),
            P(("groups", "row"), "col", None),
            P("groups"),
            P("groups"),
            P("groups", None),
            P("groups"),
            P("groups", None),
        ),
        check_vma=False,
    )
```

```python
import functools

import jax
import jax.numpy as jnp
from jax import lax
from jax.experimental import pallas as pl
from jax.experimental.pallas import tpu as pltpu
from jax.sharding import PartitionSpec as P

EPSILON = 1e-05
LANES = 128
WIDE = 256
UNROLL = 4
MESH = pl.DeviceIdType.MESH
F32 = jnp.float32
BF16 = jnp.bfloat16


def lane_group_swap(blocks, width):
    lane = lax.broadcasted_iota(jnp.int32, blocks[0].shape, 1)
    span = len(blocks) // 2
    while span:
        low = (lane // (width * span)) % 2 == 0
        out = list(blocks)
        for a in range(len(blocks)):
            if a & span:
                continue
            first, second = blocks[a], blocks[a + span]
            shift = width * span
            out[a] = jnp.where(low, first, pltpu.roll(second, shift, 1))
            out[a + span] = jnp.where(low, pltpu.roll(first, LANES - shift, 1), second)
        blocks = out
        span //= 2
    return blocks


def place_groups(pieces, shifts, width):
    group = lax.broadcasted_iota(jnp.int32, pieces[0].shape, 1) // width
    out = None
    for k, (piece, shift) in enumerate(zip(pieces, shifts)):
        rolled = pltpu.roll(piece, shift % LANES, 1) if shift % LANES else piece
        out = rolled if out is None else jnp.where(group == k, rolled, out)
    return out


def nt(a, b):
    return lax.dot_general(a, b, (((1,), (1,)), ((), ())), preferred_element_type=F32)


def tn(a, b):
    return lax.dot_general(a, b, (((0,), (0,)), ((), ())), preferred_element_type=F32)


def nn(a, b):
    return jnp.dot(a, b, preferred_element_type=F32)


def aligned(start, size, step=None):
    return pl.ds(pl.multiple_of(start, step or size), size)


def fused_kernel(dims, *refs):
    rows, cols, seq_local, res_local, hidden, channels, width = dims
    inputs = refs[:10]
    (pair_ref, ag_ref, gwf_ref, gpw_ref, vec_ref) = refs[10:15]
    (
        x_ref,
        seq_ref,
        res_ref,
        gain_ref,
        shift_ref,
        w_ref,
        pb_ref,
        ow_ref,
        ob_ref,
        cot_ref,
        scaled_ref,
        inv_ref,
        both_ref,
        prj_ref,
        tr_ref,
        u_ref,
        seqcol_ref,
        lsend_ref,
        lbuf_ref,
        lt_ref,
        rbuf_ref,
        owf_ref,
        wp_ref,
        wpt_ref,
        gpre_ref,
        gp_ref,
        prod_ref,
        gls_ref,
        glr_ref,
        glp_ref,
        glx_ref,
        glmid_ref,
        glfin_ref,
        grs_ref,
        grr_ref,
        gws_ref,
        gwr_ref,
        gwp_ref,
        gwx_ref,
        gwc_ref,
        gwcr_ref,
        gw_ref,
        low_ref,
        sw_ref,
        swp_ref,
        swx_ref,
        swr_ref,
        swf_ref,
        sv_ref,
        svr_ref,
        svp_ref,
        svc_ref,
        local_sems,
        one_sems,
        send_sems,
        recv_sems,
        left_send,
        left_recv,
    ) = refs[15:]
    r = lax.axis_index("row")
    c = lax.axis_index("col")
    factor = cols // rows
    seqs = seq_local * rows
    tile_rows = res_local * factor
    n = seq_local * res_local
    pairs = tile_rows * res_local
    block = res_local * hidden
    fold = LANES // res_local
    chunks = n // LANES
    majors = block // LANES
    total = rows * cols
    chips = cols // 2
    chip = c // 2
    core = lax.rem(c, 2)
    partner = chip * 2 + 1 - core
    barrier = pltpu.get_barrier_semaphore()

    def greet(t, carry):
        other = lax.rem(r * cols + c + t, total)
        pl.semaphore_signal(
            barrier,
            inc=1,
            device_id={"row": other // cols, "col": lax.rem(other, cols)},
            device_id_type=MESH,
        )
        return carry

    staged = (x_ref, seq_ref, res_ref, gain_ref, shift_ref, w_ref, pb_ref, ow_ref, ob_ref, cot_ref)
    loads = [
        pltpu.make_async_copy(source, target, local_sems.at[2 + k])
        for k, (source, target) in enumerate(zip(inputs, staged))
    ]
    late = (7, 8, 9)
    for load in loads[: late[0]]:
        load.start()
    lax.fori_loop(1, total, greet, 0)
    for k in late:
        loads[k].start()

    def remote(src, dst, send_sem, recv_sem, trow, tcol):
        return pltpu.make_async_remote_copy(
            src_ref=src,
            dst_ref=dst,
            send_sem=send_sem,
            recv_sem=recv_sem,
            device_id={"row": trow, "col": tcol},
            device_id_type=MESH,
        )

    gw_bulk = gws_ref.at[pl.ds(0, (rows * chips - 1) * (hidden * hidden // total)), :]

    def over(kind):
        if kind == "col":
            return cols, c, lambda k: (r, k)
        if kind == "row":
            return rows, r, lambda k: (k, c)
        if kind == "chip":
            return chips, chip, lambda k: (r, 2 * k + core)
        return rows * chips, r * chips + chip, lambda k: (k // chips, 2 * lax.rem(k, chips) + core)

    def send_to(args, k):
        kind, plane, src, dst, bulk = args
        _, me, where = over(kind)
        remote(src(k), dst(me), send_sems.at[plane], recv_sems.at[plane], *where(k)).start()

    def start(*args, first=1, last=None):
        kind = args[0]
        count, me, _ = over(kind)

        def body(t, carry):
            if kind != "row":
                send_to(args, lax.rem(me + t, count))
            else:
                @pl.when(me + t < count)
                def _():
                    send_to(args, lax.rem(me + t, count))

                @pl.when(me >= t)
                def _():
                    send_to(args, lax.rem(me - t + count, count))

            return carry

        lax.fori_loop(first, last or count, body, 0)

    def everything(kind, plane, bulk):
        count, me, where = over(kind)
        part = bulk if bulk is gw_bulk else bulk.at[pl.ds(0, count - 1)]
        return remote(part, part, send_sems.at[plane], recv_sems.at[plane], *where(lax.rem(me + 1, count)))

    def hand(plane, src, dst):
        remote(src, dst, send_sems.at[plane], recv_sems.at[plane], r, partner).start()

    def handed(plane, bulk):
        return remote(bulk, bulk, send_sems.at[plane], recv_sems.at[plane], r, partner)

    def receive(kind, plane, src, dst, bulk):
        everything(kind, plane, bulk).wait_recv()

    def drain(kind, plane, src, dst, bulk):
        everything(kind, plane, bulk).wait_send()

    for k in range(1, 7):
        loads[k].wait()

    def column(mask_ref, count, offset):
        size = mask_ref.shape[1]
        shape = (count, size)
        hit = lax.broadcasted_iota(jnp.int32, shape, 1) == lax.broadcasted_iota(jnp.int32, shape, 0) + offset
        values = jnp.broadcast_to(mask_ref[...].astype(F32), shape)
        return jnp.sum(jnp.where(hit, values, 0.0), axis=1, keepdims=True)

    seqcol_ref[...] = jnp.broadcast_to(column(seq_ref, seq_local, r * seq_local), seqcol_ref.shape)
    rescol = column(res_ref, res_local, c * res_local)
    tilecol = column(res_ref, tile_rows, r * tile_rows)
    kept = jnp.sum(seq_ref[...].astype(F32), axis=1, keepdims=True)

    def live_column(k):
        parts = []
        for q in range(fold):
            parts.append(rescol * seqcol_ref[pl.ds(k * fold + q, 1), 0:1])
        return jnp.concatenate(parts, axis=0)

    w = w_ref[...].astype(F32)
    w = jnp.concatenate([w, jnp.zeros((LANES - 2 * hidden, channels), F32)], axis=0)
    w_wide = w.T.astype(BF16)
    w_turned = w.astype(BF16)
    bias = pb_ref[...]
    bias = jnp.concatenate([bias, jnp.zeros((1, LANES - 2 * hidden), F32)], axis=1)
    gain = gain_ref[...]
    shift = shift_ref[...]

    loads[0].wait()

    def layer_norm(k, carry):
        here = aligned(k * LANES, LANES)
        widened = x_ref[here, :].astype(F32)
        centred = widened - jnp.mean(widened, axis=-1, keepdims=True)
        inverse = lax.rsqrt(jnp.mean(centred * centred, axis=-1, keepdims=True) + EPSILON)
        scaled = centred * inverse
        normed = (scaled * gain + shift).astype(BF16)
        scaled_ref[here, :] = scaled
        inv_ref[here, :] = inverse
        both_ref[here, :channels] = normed
        both_ref[here, channels:] = scaled.astype(BF16)
        prj = (nn(normed, w_wide) + bias) * live_column(k)
        prj_ref[here, :] = prj
        tr_ref[here, :] = prj.T
        return carry

    lax.fori_loop(0, chunks, layer_norm, 0, unroll=min(2 * UNROLL, chunks))

    for im in range(majors):
        pieces = [prj_ref[pl.ds(im * fold + k, seq_local, stride=res_local), :] for k in range(fold)]
        left = place_groups(pieces, [k * hidden for k in range(fold)], hidden)
        lsend_ref[:, im * LANES : (im + 1) * LANES] = left.astype(BF16)
    for sb in range(chunks):
        pieces = [
            tr_ref[pl.ds(sb * LANES + hidden + k, majors, stride=fold), :] for k in range(fold)
        ]
        for q in range(fold):
            turned = place_groups(pieces, [(k - q) * res_local for k in range(fold)], res_local)
            u_ref[pl.ds(sb * fold + q, majors, stride=seq_local), :] = turned
    my_seqs = aligned(r * seq_local, seq_local)
    for dm in range(majors):
        rbuf_ref[my_seqs, dm * LANES : (dm + 1) * LANES] = u_ref[
            dm * seq_local : (dm + 1) * seq_local, :
        ].astype(BF16)

    pl.semaphore_wait(barrier, total - 1)

    def left_slot(k):
        return lbuf_ref.at[aligned((k // factor) * seq_local, seq_local), aligned(lax.rem(k, factor) * block, block)]

    relay_row = c // factor
    relay_col = r * factor + lax.rem(c, factor)
    left_col = chip * 2 + lax.rem(r, 2)
    left_stays = jnp.logical_and(relay_row == r, left_col == c)
    left_out = remote(
        lsend_ref, left_slot(relay_col), one_sems.at[0], left_recv.at[relay_col], relay_row, left_col
    )
    left_home = pltpu.make_async_copy(lsend_ref, left_slot(relay_col), local_sems.at[0])

    @pl.when(left_stays)
    def _():
        left_home.start()

    @pl.when(jnp.logical_not(left_stays))
    def _():
        left_out.start()

    HAND_GL, HAND_A, HAND_B, HAND_LEFT, HAND_OUT, HAND_SW, HAND_SV, HAND_SWR = 12, 13, 14, 15, 1, 10, 7, 16

    def passed(i, q):
        begin = jnp.minimum((r + 1 - core) // 2, rows // 2 - 1)
        row = 2 * lax.rem(begin + i, rows // 2) + core
        near = (r * factor + q) // 2 == chip
        return row * factor + q, near, jnp.logical_and(row == r, r * factor + q == c)

    def pass_left(i):
        for q in range(factor):
            k, near, own = passed(i, q)
            slot = left_slot(k)

            @pl.when(own)
            def _():
                left_home.wait()

            @pl.when(jnp.logical_not(own))
            def _():
                remote(slot, slot, one_sems.at[0], left_recv.at[k], r, partner).wait_recv()

            @pl.when(near)
            def _():
                def body(t, carry):
                    other = lax.rem(chip + t, chips)
                    remote(slot, slot, left_send.at[k], left_recv.at[k], r, 2 * other + core).start()
                    return carry

                lax.fori_loop(1, chips, body, 0)

            hand(HAND_LEFT, slot, slot)

    def right_block(k):
        return rbuf_ref.at[aligned(k * seq_local, seq_local), :]

    right_args = ("row", 0, lambda k: right_block(r), right_block, grr_ref)

    start(*right_args, last=2)
    for k in late:
        loads[k].wait()
    owf_ref[...] = ow_ref[...].astype(F32)
    for d in range(hidden):
        wp_ref[d * hidden : (d + 1) * hidden, :] = owf_ref[pl.ds(d, hidden, stride=hidden), :].astype(BF16)

    def inverse_divisor(i):
        return 1.0 / jnp.maximum(kept * tilecol[i : i + 1, :] * rescol, 1.0)

    for i in range(tile_rows):
        here = slice(i * res_local, (i + 1) * res_local)
        gpre_ref[here, :] = (cot_ref[here, :].astype(F32) * inverse_divisor(i)).astype(BF16)

    half = WIDE // LANES

    def grad_products(ip, carry):
        upstream = gpre_ref[aligned(ip * WIDE, WIDE), :]
        for dm in range(majors):
            tile = nt(wp_ref[dm * LANES : (dm + 1) * LANES, :], upstream)
            for h in range(half):
                blocks = [
                    tile[a * hidden : (a + 1) * hidden, h * LANES : (h + 1) * LANES] for a in range(fold)
                ]
                for a, swapped in enumerate(lane_group_swap(blocks, res_local)):
                    gp_ref[
                        aligned(((ip * half + h) * fold + a) * hidden, hidden), dm * LANES : (dm + 1) * LANES
                    ] = swapped.astype(BF16)
        return carry

    steps = pairs // WIDE
    lax.fori_loop(0, steps // 2, grad_products, 0)
    start(*right_args, first=2)
    pass_left(0)
    lax.fori_loop(steps // 2, steps, grad_products, 0)

    for i in range(1, rows // 2):
        pass_left(i)
    handed(HAND_LEFT, glp_ref).wait_recv()
    for k in range(block // WIDE):
        grs_ref[:, k * WIDE : (k + 1) * WIDE] = nn(lbuf_ref[...], gp_ref[:, k * WIDE : (k + 1) * WIDE]).astype(BF16)
    gr_args = (
        "row",
        3,
        lambda k: grs_ref.at[aligned(k * seq_local, seq_local), :],
        lambda k: grr_ref.at[k],
        grr_ref,
    )
    for im in range(tile_rows * hidden // LANES):
        lt_ref[im * LANES : (im + 1) * LANES, :] = lbuf_ref[:, im * LANES : (im + 1) * LANES].T
    for k in range(hidden * hidden // LANES):
        wpt_ref[:, k * LANES : (k + 1) * LANES] = wp_ref[k * LANES : (k + 1) * LANES, :].T
    receive(*right_args)
    start(*gr_args)

    def gl_part(k):
        return gls_ref.at[aligned((k // factor) * seq_local, seq_local), aligned(lax.rem(k, factor) * block, block)]

    for k in range(tile_rows * hidden // WIDE):
        gls_ref[:, k * WIDE : (k + 1) * WIDE] = nt(rbuf_ref[...], gp_ref[k * WIDE : (k + 1) * WIDE, :]).astype(BF16)

    def left_block(k, of_core):
        return of_core * chips + k

    def hand_left(k, carry):
        hand(HAND_GL, gl_part(left_block(k, 1 - core)), glp_ref.at[k])
        return carry

    lax.fori_loop(0, chips, hand_left, 0)
    gl_args = ("chip", 2, lambda k: glx_ref.at[k], lambda k: glr_ref.at[k], glr_ref)

    def sum_left():
        handed(HAND_GL, glp_ref).wait_recv()

        def add(k, carry):
            t = left_block(k, core)
            mine = gls_ref[aligned((t // factor) * seq_local, seq_local), aligned(lax.rem(t, factor) * block, block)]
            glx_ref[k] = (mine.astype(F32) + glp_ref[k].astype(F32)).astype(BF16)
            return carry

        lax.fori_loop(0, chips, add, 0)
        start(*gl_args)


    w_block = hidden * hidden // cols
    gw_row_args = ("chip", 4, lambda k: gwx_ref.at[k], lambda k: gwr_ref.at[k], gwr_ref)
    strips = hidden * hidden // WIDE
    per = WIDE // w_block
    first = lax.rem((chip + 1) * 2 * w_block // WIDE, strips)

    def sum_weight(later):
        plane = HAND_B if later else HAND_A
        some = chips // 2
        offset = some if later else 0
        handed(plane, gwp_ref.at[pl.ds(0, some)]).wait_recv()

        def add(k, carry):
            k = lax.rem(first * per // 2 + offset + k, chips)
            t = 2 * k + core
            mine = gws_ref[aligned(t * w_block, w_block), :]
            gwx_ref[k] = (mine.astype(F32) + gwp_ref[k].astype(F32)).astype(BF16)

            @pl.when(k != chip)
            def _():
                send_to(gw_row_args, k)

            return carry

        lax.fori_loop(0, some, add, 0)

    for k in range(strips):
        strip = lax.rem(first + k, strips)
        right = rbuf_ref[:, aligned(strip * WIDE, WIDE)]

        def products(im, carry, strip=strip, right=right):
            tile = nn(lt_ref[aligned(im * LANES, LANES), :], right)
            for h in range(half):
                blocks = [
                    tile[a * hidden : (a + 1) * hidden, h * LANES : (h + 1) * LANES] for a in range(fold)
                ]
                for a, swapped in enumerate(lane_group_swap(blocks, res_local)):
                    at = strip * WIDE + (h * fold + a) * hidden
                    prod_ref[aligned(at, hidden), aligned(im * LANES, LANES)] = swapped.astype(BF16)
            return carry

        lax.fori_loop(0, tile_rows // fold, products, 0, unroll=8)
        here = aligned(strip * WIDE, WIDE)
        gws_ref[here, :] = nn(prod_ref[here, :], gpre_ref[...]).astype(BF16)
        for j in range(per):
            target = strip * per + j

            @pl.when(lax.rem(target, 2) != core)
            def _(target=target, k=k):
                hand(
                    HAND_A if k < strips // 2 else HAND_B,
                    gws_ref.at[aligned(target * w_block, w_block), :],
                    gwp_ref.at[target // 2],
                )

        if k == 0:
            sum_left()
        if k == strips // 2:
            sum_weight(False)

    receive(*gl_args)

    def add_left(t, carry):
        return carry + glr_ref[lax.rem(chip + t, chips)].astype(F32)

    glmid_ref[...] = lax.fori_loop(1, chips, add_left, glx_ref[chip].astype(F32)).astype(BF16)
    gathered = left_block(chip, core)
    owner_row = gathered // factor
    owner_col = r * factor + lax.rem(gathered, factor)
    at_home = jnp.logical_and(owner_row == r, owner_col == c)
    gl_out = remote(glmid_ref, glfin_ref, one_sems.at[2], one_sems.at[3], owner_row, owner_col)
    gl_home = pltpu.make_async_copy(glmid_ref, glfin_ref, local_sems.at[1])

    @pl.when(at_home)
    def _():
        gl_home.start()

    @pl.when(jnp.logical_not(at_home))
    def _():
        gl_out.start()

    out_bias = ob_ref[...]
    for k in range(pairs // WIDE):
        pre = nn(wpt_ref[...], prod_ref[:, k * WIDE : (k + 1) * WIDE]).T + out_bias
        for q in range(WIDE // res_local):
            i = k * (WIDE // res_local) + q
            pair_ref[i * res_local : (i + 1) * res_local, :] = (
                pre[q * res_local : (q + 1) * res_local, :] * inverse_divisor(i)
            ).astype(BF16)

    sum_weight(True)
    w_small = w_block // rows
    receive(*gw_row_args)

    def add_w(t, carry):
        return carry + gwr_ref[lax.rem(chip + t, chips)].astype(F32)

    summed = lax.fori_loop(1, chips, add_w, gwx_ref[chip].astype(F32)).astype(BF16)
    for k in range(rows):
        gwc_ref[k] = summed[k * w_small : (k + 1) * w_small, :]
    gw_col_args = ("row", 5, lambda k: gwc_ref.at[k], lambda k: gwcr_ref.at[k], gwcr_ref)
    start(*gw_col_args)

    receive(*gr_args)
    for dm in range(majors):
        part = slice(dm * LANES, (dm + 1) * LANES)
        total_right = grs_ref[my_seqs, part].astype(F32)

        def add_right(t, carry, part=part):
            return carry + grr_ref[lax.rem(r + t, rows), :, part].astype(F32)

        u_ref[dm * seq_local : (dm + 1) * seq_local, :] = lax.fori_loop(1, rows, add_right, total_right)
    for sb in range(chunks):
        pieces = [u_ref[pl.ds(sb * fold + q, majors, stride=seq_local), :] for q in range(fold)]
        for k in range(fold):
            turned = place_groups(pieces, [(q - k) * res_local for q in range(fold)], res_local)
            tr_ref[pl.ds(sb * LANES + hidden + k, majors, stride=fold), :] = turned

    lane = lax.broadcasted_iota(jnp.int32, (LANES, LANES), 1)

    def lower_right(k, carry):
        here = aligned(k * LANES, LANES)
        right_only = jnp.logical_and(lane >= hidden, lane < 2 * hidden)
        right_part = jnp.where(right_only, tr_ref[here, :].T * live_column(k), 0.0)
        tr_ref[here, :] = right_part
        low_ref[here, :] = right_part.astype(BF16)
        return carry

    lax.fori_loop(0, chunks, lower_right, 0, unroll=min(2 * UNROLL, chunks))
    quarter = 2 * hidden // cols
    sw_args = ("core", 6, lambda k: swx_ref.at[lax.rem(k, chips)], lambda k: swr_ref.at[k], swr_ref)
    few = chips // 2

    def hand_quarters(plane, low_chip, summed_over):
        for k in range(2 * low_chip, 2 * (low_chip + few)):
            sw_ref[k] = summed_over[k * quarter : (k + 1) * quarter, :].astype(BF16)

        def body(k, carry):
            hand(plane, sw_ref.at[2 * k + 1 - core], swp_ref.at[k])
            return carry

        lax.fori_loop(low_chip, low_chip + few, body, 0)

    def send_quarters(plane, low_chip):
        handed(plane, swp_ref.at[pl.ds(low_chip, few)]).wait_recv()

        def add(k, carry):
            swx_ref[k] = (sw_ref[2 * k + core].astype(F32) + swp_ref[k].astype(F32)).astype(BF16)
            return carry

        lax.fori_loop(low_chip, low_chip + few, add, 0)

        def body(t, carry):
            k = lax.rem(r * chips + chip + t, rows * chips)
            target = lax.rem(k, chips)

            @pl.when(jnp.logical_and(target >= low_chip, target < low_chip + few))
            def _():
                send_to(sw_args, k)

            return carry

        lax.fori_loop(1, rows * chips, body, 0)

    hand_quarters(HAND_SWR, few, tn(low_ref[...], both_ref[:, :channels]))
    giver = r * factor + lax.rem(c, factor)
    giver_row = c // factor
    giver_col = 2 * lax.rem(giver, chips) + giver // chips
    kept_here = jnp.logical_and(giver_row == r, giver_col == c)

    @pl.when(kept_here)
    def _():
        gl_home.wait()

    @pl.when(jnp.logical_not(kept_here))
    def _():
        remote(glmid_ref, glfin_ref, one_sems.at[2], one_sems.at[3], giver_row, giver_col).wait_recv()

    for im in range(majors):
        piece = glfin_ref[:, im * LANES : (im + 1) * LANES].astype(F32)
        for k in range(fold):
            rolled = pltpu.roll(piece, LANES - k * hidden, 1) if k else piece
            prj_ref[pl.ds(im * fold + k, seq_local, stride=res_local), :] = rolled

    send_quarters(HAND_SWR, few)
    def lower(k, bias_sum):
        here = aligned(k * LANES, LANES)
        projected = jnp.where(lane < hidden, prj_ref[here, :] * live_column(k), tr_ref[here, :])
        low_ref[here, :] = projected.astype(BF16)
        return bias_sum + jnp.sum(projected, axis=0, keepdims=True)

    bias_sum = lax.fori_loop(0, chunks, lower, jnp.zeros((1, LANES), F32), unroll=min(2 * UNROLL, chunks))
    joined = tn(low_ref[...], both_ref[...])
    grad_w_in = joined[:, :channels]
    low_sum = jnp.sum(low_ref[...].astype(F32), axis=0, keepdims=True)
    turned = w_turned.astype(F32)
    gain_sum = jnp.sum(joined[:, channels:] * turned, axis=0, keepdims=True)
    shift_sum = jnp.sum(low_sum.T * turned, axis=0, keepdims=True)
    parts = channels // LANES
    sv_ref[...] = jnp.zeros(sv_ref.shape, F32)
    for k in range(parts):
        sv_ref[k : k + 1, :] = gain_sum[:, k * LANES : (k + 1) * LANES]
        sv_ref[parts + k : parts + k + 1, :] = shift_sum[:, k * LANES : (k + 1) * LANES]
    sv_ref[2 * parts : 2 * parts + 1, :] = bias_sum
    hand(HAND_SV, sv_ref, svp_ref.at[0])

    hand_quarters(HAND_SW, 0, grad_w_in)
    def backward(k, carry):
        here = aligned(k * LANES, LANES)
        scaled = scaled_ref[here, :]
        grad_scaled = nn(low_ref[here, :], w_turned) * gain
        first = jnp.mean(grad_scaled, axis=-1, keepdims=True)
        second = jnp.mean(grad_scaled * scaled, axis=-1, keepdims=True)
        ag_ref[here, :] = (inv_ref[here, :] * (grad_scaled - first - scaled * second)).astype(BF16)
        return carry

    split = chunks // 2
    lax.fori_loop(0, split, backward, 0, unroll=min(UNROLL, split))
    send_quarters(HAND_SW, 0)
    handed(HAND_SV, svp_ref).wait_recv()
    svc_ref[...] = sv_ref[...] + svp_ref[0]
    sv_args = ("core", 8, lambda k: svc_ref, lambda k: svr_ref.at[k], svr_ref)
    start(*sv_args)
    receive(*gw_col_args)

    def add_w_col(t, carry):
        return carry + gwcr_ref[lax.rem(r + t, rows)].astype(F32)

    gw_ref[c, r] = lax.fori_loop(1, rows, add_w_col, gwc_ref[r].astype(F32)).astype(BF16)
    gw_all_args = (
        "core",
        9,
        lambda k: gw_ref.at[c, r],
        lambda k: gw_ref.at[2 * lax.rem(k, chips) + core, k // chips],
        gw_bulk,
    )
    start(*gw_all_args)

    lax.fori_loop(split, chunks, backward, 0, unroll=min(UNROLL, chunks - split))

    def ordered(received, count):
        def add(t, carry):
            return carry + received[t].astype(F32)

        return lax.fori_loop(1, count, add, received[0].astype(F32))

    swr_ref[r * chips + chip] = swx_ref[chip]
    receive(*sw_args)
    swf_ref[...] = ordered(swr_ref, rows * chips)
    gpw_ref[c] = swf_ref[...]
    sw_out_args = ("col", 11, lambda k: swf_ref, lambda k: gpw_ref.at[k], gpw_ref)
    start(*sw_out_args)
    receive(*gw_all_args)

    def hand_out(k, carry):
        slot = gw_ref.at[2 * k + core]
        hand(HAND_OUT, slot, slot)
        return carry

    lax.fori_loop(0, chips, hand_out, 0)
    svr_ref[r * chips + chip] = svc_ref[...]
    receive(*sv_args)
    vec_ref[...] = ordered(svr_ref, rows * chips)
    def widen(of_core):
        def body(t, carry):
            for k in range(rows):
                at = (2 * t + of_core) * rows * w_small + k * w_small
                owf_ref[aligned(at, w_small), :] = gw_ref[2 * t + of_core, k].astype(F32)
            return carry

        lax.fori_loop(0, chips, body, 0)

    widen(core)
    handed(HAND_OUT, gw_ref.at[pl.ds(0, chips)]).wait_recv()
    widen(1 - core)
    for k in range(hidden):
        gwf_ref[k * hidden : (k + 1) * hidden, :] = owf_ref[pl.ds(k, hidden, stride=hidden), :]
    receive(*sw_out_args)

    @pl.when(jnp.logical_not(at_home))
    def _():
        gl_out.wait_send()

    @pl.when(jnp.logical_not(left_stays))
    def _():
        left_out.wait_send()

    for i in range(rows // 2):
        for q in range(factor):
            k, near, _ = passed(i, q)

            @pl.when(near)
            def _():
                rest = glr_ref.at[pl.ds(0, chips - 1)]
                remote(rest, rest, left_send.at[k], left_recv.at[k], r, partner).wait_send()

    handed(HAND_LEFT, glp_ref).wait_send()
    for plane in (HAND_SW, HAND_SWR):
        handed(plane, swp_ref.at[pl.ds(0, few)]).wait_send()
    handed(HAND_SV, svp_ref).wait_send()
    handed(HAND_GL, glp_ref).wait_send()
    handed(HAND_OUT, gw_ref.at[pl.ds(0, chips)]).wait_send()
    for plane in (HAND_A, HAND_B):
        handed(plane, gwp_ref.at[pl.ds(0, chips // 2)]).wait_send()
    for args in (
        right_args,
        gl_args,
        gr_args,
        gw_row_args,
        gw_col_args,
        sw_args,
        sv_args,
        gw_all_args,
        sw_out_args,
    ):
        drain(*args)


def finish_kernel(*refs):
    pair_ref, ag_ref, gw_ref, gpw_ref, vec_ref = refs[:5]
    pair_hbm, ag_hbm, gain_hbm, shift_hbm, gpw_hbm, bias_hbm, gw_hbm = refs[5:12]
    gain_ref, shift_ref, bias_ref, sems = refs[12:]
    copies = []

    def send(source, target):
        copy = pltpu.make_async_copy(source, target, sems.at[len(copies)])
        copy.start()
        copies.append(copy)

    send(gw_ref, gw_hbm)
    send(ag_ref, ag_hbm)
    send(pair_ref, pair_hbm)
    send(gpw_ref, gpw_hbm)
    parts = gain_ref.shape[1] // LANES
    for k in range(parts):
        gain_ref[:, k * LANES : (k + 1) * LANES] = vec_ref[k : k + 1, :]
        shift_ref[:, k * LANES : (k + 1) * LANES] = vec_ref[parts + k : parts + k + 1, :]
    bias_ref[...] = vec_ref[2 * parts : 2 * parts + 1, : bias_ref.shape[1]]
    send(gain_ref, gain_hbm)
    send(shift_ref, shift_hbm)
    send(bias_ref, bias_hbm)
    for copy in copies:
        copy.wait()


def shards(
    alignment,
    sequence_mask,
    residue_mask,
    layer_norm_gain,
    norm_shift,
    proj_weight,
    proj_bias,
    out_weight,
    out_bias,
    cotangent,
):
    rows = lax.axis_size("row")
    cols = lax.axis_size("col")
    factor = cols // rows
    seq_local, res_local, channels = alignment.shape
    seqs = seq_local * rows
    hidden = proj_weight.shape[1] // 2
    width = out_weight.shape[1]
    tile_rows = res_local * factor
    n = seq_local * res_local
    pairs = tile_rows * res_local
    block = res_local * hidden
    majors = block // LANES
    inner = tile_rows * hidden
    w_block = hidden * hidden // cols
    w_small = w_block // rows
    quarter = 2 * hidden // cols
    dims = (rows, cols, seq_local, res_local, hidden, channels, width)
    vmem = pl.BlockSpec(memory_space=pltpu.VMEM)
    hbm = pl.BlockSpec(memory_space=pltpu.HBM)
    operands = [
        alignment.reshape(n, channels),
        sequence_mask.reshape(1, -1),
        residue_mask.reshape(1, -1),
        layer_norm_gain.reshape(1, -1),
        norm_shift.reshape(1, -1),
        proj_weight.T,
        proj_bias.reshape(1, -1),
        out_weight,
        out_bias.reshape(1, -1),
        cotangent.reshape(pairs, width),
    ]
    operands = [pltpu.with_memory_space_constraint(array, pltpu.HBM) for array in operands]
    pair, grad_alignment, grad_w, grad_pw, vectors = pl.pallas_call(
        functools.partial(fused_kernel, dims),
        out_shape=[
            jax.ShapeDtypeStruct((pairs, width), BF16),
            jax.ShapeDtypeStruct((n, channels), BF16),
            jax.ShapeDtypeStruct((hidden * hidden, width), F32),
            jax.ShapeDtypeStruct((cols, quarter, channels), F32),
            jax.ShapeDtypeStruct((8, LANES), F32),
        ],
        in_specs=[hbm] * 10,
        out_specs=[vmem] * 5,
        scratch_shapes=[
            *[pltpu.VMEM(array.shape, array.dtype) for array in operands],
            pltpu.VMEM((n, channels), F32),
            pltpu.VMEM((n, 1), F32),
            pltpu.VMEM((n, 2 * channels), BF16),
            pltpu.VMEM((n, LANES), F32),
            pltpu.VMEM((n, LANES), F32),
            pltpu.VMEM((majors * seq_local, LANES), F32),
            pltpu.VMEM((seq_local, LANES), F32),
            pltpu.VMEM((seq_local, block), BF16),
            pltpu.VMEM((seqs, inner), BF16),
            pltpu.VMEM((inner, seqs), BF16),
            pltpu.VMEM((seqs, block), BF16),
            pltpu.VMEM((hidden * hidden, width), F32),
            pltpu.VMEM((hidden * hidden, width), BF16),
            pltpu.VMEM((width, hidden * hidden), BF16),
            pltpu.VMEM((pairs, width), BF16),
            pltpu.VMEM((inner, block), BF16),
            pltpu.VMEM((hidden * hidden, pairs), BF16),
            pltpu.VMEM((seqs, inner), BF16),
            pltpu.VMEM((cols, seq_local, block), BF16),
            pltpu.VMEM((cols // 2, seq_local, block), BF16),
            pltpu.VMEM((cols // 2, seq_local, block), BF16),
            pltpu.VMEM((seq_local, block), BF16),
            pltpu.VMEM((seq_local, block), BF16),
            pltpu.VMEM((seqs, block), BF16),
            pltpu.VMEM((rows, seq_local, block), BF16),
            pltpu.VMEM((hidden * hidden, width), BF16),
            pltpu.VMEM((cols // 2, w_block, width), BF16),
            pltpu.VMEM((cols // 2, w_block, width), BF16),
            pltpu.VMEM((cols // 2, w_block, width), BF16),
            pltpu.VMEM((rows, w_small, width), BF16),
            pltpu.VMEM((rows, w_small, width), BF16),
            pltpu.VMEM((cols, rows, w_small, width), BF16),
            pltpu.VMEM((n, LANES), BF16),
            pltpu.VMEM((cols, quarter, channels), BF16),
            pltpu.VMEM((cols // 2, quarter, channels), BF16),
            pltpu.VMEM((cols // 2, quarter, channels), BF16),
            pltpu.VMEM((rows * cols // 2, quarter, channels), BF16),
            pltpu.VMEM((quarter, channels), F32),
            pltpu.VMEM((8, LANES), F32),
            pltpu.VMEM((rows * cols // 2, 8, LANES), F32),
            pltpu.VMEM((1, 8, LANES), F32),
            pltpu.VMEM((8, LANES), F32),
            pltpu.SemaphoreType.DMA((12,)),
            pltpu.SemaphoreType.DMA((4,)),
            pltpu.SemaphoreType.DMA((17,)),
            pltpu.SemaphoreType.DMA((17,)),
            pltpu.SemaphoreType.DMA((cols,)),
            pltpu.SemaphoreType.DMA((cols,)),
        ],
        compiler_params=pltpu.CompilerParams(
            collective_id=0, has_side_effects=True, vmem_limit_bytes=48 * 1024 * 1024
        ),
    )(*operands)
    pair, grad_alignment, gain, shift, grad_pw, bias, grad_w = pl.pallas_call(
        finish_kernel,
        out_shape=[
            jax.ShapeDtypeStruct((pairs, width), BF16),
            jax.ShapeDtypeStruct((n, channels), BF16),
            jax.ShapeDtypeStruct((1, channels), F32),
            jax.ShapeDtypeStruct((1, channels), F32),
            jax.ShapeDtypeStruct((2 * hidden, channels), F32),
            jax.ShapeDtypeStruct((1, 2 * hidden), F32),
            jax.ShapeDtypeStruct((hidden * hidden, width), F32),
        ],
        in_specs=[vmem] * 5,
        out_specs=[hbm] * 7,
        scratch_shapes=[
            pltpu.VMEM((1, channels), F32),
            pltpu.VMEM((1, channels), F32),
            pltpu.VMEM((1, 2 * hidden), F32),
            pltpu.SemaphoreType.DMA((7,)),
        ],
        compiler_params=pltpu.CompilerParams(vmem_limit_bytes=16 * 1024 * 1024),
    )(pair, grad_alignment, grad_w, grad_pw.reshape(-1, channels), vectors)
    return (
        pair.reshape(tile_rows, res_local, width),
        grad_alignment.reshape(seq_local, res_local, channels),
        gain.reshape(-1),
        shift.reshape(-1),
        grad_pw.T,
        bias.reshape(-1),
        grad_w,
    )


def solution(mesh):
    return jax.shard_map(
        shards,
        mesh=mesh,
        in_specs=(
            P(("groups", "row"), "col", None),
            P("groups"),
            P("groups"),
            P(),
            P(),
            P(),
            P(),
            P(),
            P(),
            P(("groups", "row"), "col", None),
        ),
        out_specs=(
            P(("groups", "row"), "col", None),
            P(("groups", "row"), "col", None),
            P("groups"),
            P("groups"),
            P("groups", None),
            P("groups"),
            P("groups", None),
        ),
        check_vma=False,
    )
```
